128 devices in a mesh: blk: 32 (over z, y, core), rhs: 4 (over x).
Axes of the slice: x: 4, y: 4, z: 4, core: 2. Of those that a mesh axis runs over, the one named last changes fastest.
Arguments:
- charges: bfloat16 [64, 65536], P('rhs', 'blk'), may hold values from -6 to 6
- counts: int32 [512], P('blk'), may hold values from 32 to 128
- self_tiles: bfloat16 [512, 128, 128], P('blk'), may hold values from -0.5 to 0.5
- basis: bfloat16 [512, 128, 64], P('blk'), may hold values from -0.5 to 0.5
- near_first: int32 [16384], P('blk'), may hold values from 0 to 511, as said below
- near_second: int32 [16384], P('blk'), may hold values from 0 to 511, as said below
- near_tiles: bfloat16 [16384, 128, 128], P(('blk', 'rhs')), may hold values from -0.125 to 0.125
- far_source: int32 [16384], P('blk'), may hold values from 0 to 511, as said below
- far_target: int32 [16384], P('blk'), may hold values from 0 to 511, as said below
- far_tiles: bfloat16 [16384, 64, 64], P('blk'), may hold values from -0.09375 to 0.09375
Outputs:
- potentials: float32 [64, 65536], P('rhs', 'blk')
The draws below stay inside these ranges and needn't reach their ends.
Inputs may be any that keep to these rules, and one draw needn't show every extreme that they name: Block c holds counts[c] real panels in its first slots; the others are padding. `near_first`: the first block of a pair is one of the 16 blocks of the blk index that holds the pair. `near_second`: the second block lies within 48 blocks of the first, counted cyclically. `far_source`: any cell. `far_target`: the target cell is one of the 16 cells of the blk index that holds the interaction.
All inputs are finite; a program needn't handle non-finite values.
Results may differ from the reference program's by a relative error of at most 0.0012.
Values may be sent and summed in bfloat16 or wider, within the bound.
A program may use at most 128 MiB of HBM per device.

```python
import jax
import jax.numpy as jnp
from jax import lax

BS = 128
P_SIZE = 64
NRHS = 64
BLK_DEV = 16
PAIR_DEV = 128
FAR_DEV = 512
BLOCKS = 512
PANELS = 65536
NEAR = 16384
FAR = 16384


def near_pairs(key):
    owners = BLOCKS // BLK_DEV
    per_owner = NEAR // owners
    owner = jnp.arange(NEAR, dtype=jnp.int32) // per_owner
    first = owner * BLK_DEV + jax.random.randint(jax.random.fold_in(key, 11), (NEAR,), 0, BLK_DEV, dtype=jnp.int32)
    offset = jax.random.randint(jax.random.fold_in(key, 12), (NEAR,), -3 * BLK_DEV, 3 * BLK_DEV + 1, dtype=jnp.int32)
    second = jnp.mod(first + offset, BLOCKS).astype(jnp.int32)
    return (first.astype(jnp.int32), second)


def draw_near_first(key, part):
    return near_pairs(key)[0]


def draw_near_second(key, part):
    return near_pairs(key)[1]


def draw_far_source(key, part):
    return jax.random.randint(jax.random.fold_in(key, 21), (FAR,), 0, BLOCKS, dtype=jnp.int32)


def draw_far_target(key, part):
    owner = jnp.arange(FAR, dtype=jnp.int32) // FAR_DEV
    local = jax.random.randint(jax.random.fold_in(key, 22), (FAR,), 0, BLK_DEV, dtype=jnp.int32)
    return (owner * BLK_DEV + local).astype(jnp.int32)


def set_ends(drawn, own_key, low, top_value):
    shape = drawn.shape
    spot = [jax.random.randint(jax.random.fold_in(own_key, axis), (), 0, shape[axis]) for axis in range(len(shape))]
    drawn = drawn.at[tuple(spot)].set(low)
    longest = shape.index(max(shape))
    spot[longest] = (spot[longest] + 1) % shape[longest]
    return drawn.at[tuple(spot)].set(top_value)


def block_scale(rng, dims, pieces, low, top_value):
    def one(position, blocks):
        draws = jax.random.uniform(jax.random.fold_in(jax.random.fold_in(rng, 6), position), (blocks,), jnp.float32, low / len(pieces), top_value / len(pieces))
        return jnp.repeat(jnp.exp(draws), dims[position] // blocks).reshape((-1,) + (1,) * (len(dims) - position - 1))

    level = one(*pieces[0])
    for cut in pieces[1:]:
        level = level * one(*cut)
    return level


def bell_draw(stream_key, shape, deviation, bound, pieces=(), kind=jnp.bfloat16):
    factor_of = block_scale(stream_key, shape, pieces, -0.22, 0.18) if pieces else 1.0
    drawn = jax.random.normal(stream_key, shape, jnp.float32) * deviation * factor_of
    return jnp.minimum(jnp.maximum(drawn, -bound), bound).astype(kind)


def setup_inputs(seed: int = 0) -> dict:
    key_list = jax.random.split(jax.random.key(seed), 11)
    charges = bell_draw(key_list[0], (NRHS, PANELS), 1.0, 6.0, ((0, 4), (1, 32)))
    counts = set_ends(jax.random.randint(key_list[1], (BLOCKS,), BS // 4, BS + 1), jax.random.fold_in(key_list[1], 1), BS // 4, BS).astype(jnp.int32)
    self_tiles = bell_draw(key_list[2], (BLOCKS, BS, BS), BS ** -0.5, 0.5, ((0, 32),))
    basis = bell_draw(key_list[3], (BLOCKS, BS, P_SIZE), BS ** -0.5, 0.5, ((0, 32),))
    near_first = draw_near_first(jax.random.fold_in(key_list[10], 71), 0)
    near_second = draw_near_second(jax.random.fold_in(key_list[10], 71), 0)
    near_tiles = bell_draw(key_list[6], (NEAR, BS, BS), (BS * 16) ** -0.5, 0.125, ((0, 128),))
    far_source = draw_far_source(jax.random.fold_in(key_list[10], 71), 0)
    far_target = draw_far_target(jax.random.fold_in(key_list[10], 71), 0)
    far_tiles = bell_draw(key_list[9], (FAR, P_SIZE, P_SIZE), (P_SIZE * 64) ** -0.5, 0.09375, ((0, 32),))
    return dict(charges=charges, counts=counts, self_tiles=self_tiles, basis=basis, near_first=near_first, near_second=near_second, near_tiles=near_tiles, far_source=far_source, far_target=far_target, far_tiles=far_tiles)


def pair_terms(blocks, first, second, tiles):
    hi = lax.Precision.HIGHEST
    tiles32 = tiles.astype(jnp.float32)
    from_second = blocks[:, second].astype(jnp.float32)
    from_first = blocks[:, first].astype(jnp.float32)
    to_first = jnp.einsum('rnj,nij->rni', from_second, tiles32, precision=hi)
    to_second = jnp.einsum('rni,nij->rnj', from_first, tiles32, precision=hi)
    return to_first, to_second


def reference(charges, counts, self_tiles, basis, near_first, near_second, near_tiles, far_source, far_target, far_tiles):
    hi = lax.Precision.HIGHEST
    rows = charges.shape[0]
    valid = (jnp.arange(BS)[None, :] < counts[:, None]).reshape(-1)
    masked = jnp.where(valid[None, :], charges, jnp.zeros_like(charges))
    blocks = masked.reshape(rows, BLOCKS, BS)
    moments = jnp.einsum('rcb,cbp->rcp', blocks.astype(jnp.float32), basis.astype(jnp.float32), precision=hi).astype(jnp.bfloat16)

    def near_step(total, group):
        first, second, tiles = group
        to_first, to_second = pair_terms(blocks, first, second, tiles)
        return total.at[:, first].add(to_first).at[:, second].add(to_second), None

    near_groups = (near_first.reshape(-1, PAIR_DEV), near_second.reshape(-1, PAIR_DEV), near_tiles.reshape(-1, PAIR_DEV, BS, BS))
    near, _ = lax.scan(near_step, jnp.zeros((rows, BLOCKS, BS), jnp.float32), near_groups)

    def far_step(total, group):
        source, target, tiles = group
        to_target, to_source = pair_terms(moments, target, source, tiles)
        return total.at[:, target].add(to_target).at[:, source].add(to_source), None

    far_groups = (far_source.reshape(-1, FAR_DEV), far_target.reshape(-1, FAR_DEV), far_tiles.reshape(-1, FAR_DEV, P_SIZE, P_SIZE))
    fields, _ = lax.scan(far_step, jnp.zeros((rows, BLOCKS, P_SIZE), jnp.float32), far_groups)
    fields = fields.astype(jnp.bfloat16)
    far_part = jnp.einsum('rcp,cbp->rcb', fields.astype(jnp.float32), basis.astype(jnp.float32), precision=hi)
    self_part = jnp.einsum('rcj,cij->rci', blocks.astype(jnp.float32), self_tiles.astype(jnp.float32), precision=hi)
    total = (near + far_part + self_part).reshape(rows, PANELS)
    return jnp.where(valid[None, :], total, jnp.zeros_like(total))
```

```python
import functools

import jax
import jax.numpy as jnp
from jax import lax
from jax.experimental import pallas as pl
from jax.experimental.pallas import tpu as pltpu
from jax.sharding import PartitionSpec as P

MESH = pl.DeviceIdType.MESH
F32 = jnp.float32
BF16 = jnp.bfloat16
NT = (((1,), (1,)), ((), ()))
TN = (((0,), (0,)), ((), ()))


class Place:
    def __init__(self):
        self.o = lax.axis_index("blk")
        self.x = lax.axis_index("rhs")
        self.k = self.o % 2
        self.c = self.o // 2
        self.y = self.c % 4
        self.z = self.c // 4
        self.xp = (self.x + 1) % 4
        self.xm = (self.x + 3) % 4
        self.xo = (self.x + 2) % 4
        self.yp = (self.y + 1) % 4
        self.ym = (self.y + 3) % 4
        self.yo = (self.y + 2) % 4
        self.zp = (self.z + 1) % 4
        self.zm = (self.z + 3) % 4
        self.zo = (self.z + 2) % 4
        self.sib = self.dev(self.c, 1 - self.k)
        self.east = {"blk": self.o, "rhs": self.xp}
        self.west = {"blk": self.o, "rhs": self.xm}
        self.cp = (self.c + 1) % 16
        self.cm = (self.c + 15) % 16
        self.up = self.dev(self.cp, self.k)
        self.down = self.dev(self.cm, self.k)
        self.up_other = self.dev(self.cp, 1 - self.k)
        self.down_other = self.dev(self.cm, 1 - self.k)
        self.y_plus = self.dev(self.z * 4 + self.yp, self.k)
        self.y_minus = self.dev(self.z * 4 + self.ym, self.k)
        self.z_plus = self.dev(self.zp * 4 + self.y, self.k)
        self.z_minus = self.dev(self.zm * 4 + self.y, self.k)
        self.far_chip = self.dev((self.c + 15 + 2 * self.k) % 16, 1 - self.k)

    def dev(self, chip, core):
        return {"blk": chip * 2 + core, "rhs": self.x}

    def greet(self):
        barrier = pltpu.get_barrier_semaphore()
        peers = [
            self.sib,
            self.east,
            self.west,
            self.up,
            self.down,
            self.up_other,
            self.down_other,
            self.y_plus,
            self.y_minus,
            self.z_plus,
            self.z_minus,
        ]
        for peer in peers:
            pl.semaphore_signal(barrier, inc=1, device_id=peer, device_id_type=MESH)
        pl.semaphore_wait(barrier, len(peers))


class Sender:
    def __init__(self, send_sems, recv_sems):
        self.send_sems, self.recv_sems, self.n, self.out = send_sems, recv_sems, 0, []

    def copy(self, src, dst, peer):
        at = self.n
        self.n += 1
        made = pltpu.make_async_remote_copy(
            src_ref=src,
            dst_ref=dst,
            send_sem=self.send_sems.at[at],
            recv_sem=self.recv_sems.at[at],
            device_id=peer,
            device_id_type=MESH,
        )
        made.start()
        self.out.append(made)
        return made

    def drain(self):
        for made in self.out:
            made.wait_send()


def gather_kernel(
    charges, counts, basis_t, far, X, Mt, mown, tout, own, tin, tf, tb, tin_sem, tout_sem, ss, rs
):
    p = Place()
    x, k = p.x, p.k
    loads = [
        pltpu.make_async_copy(far.at[:, :, pl.ds(q * 128, 128)], tin.at[q], tin_sem.at[q])
        for q in range(4)
    ]
    for load in loads:
        load.start()
    lane = lax.broadcasted_iota(jnp.int32, (16, 128), 1)
    moments = []
    for b in range(16):
        block = charges[:, b * 128 : (b + 1) * 128]
        block = jnp.where(lane < counts[b], block.astype(F32), 0.0).astype(BF16)
        own[b] = block
        m = lax.dot_general(block, basis_t[b], NT, preferred_element_type=F32).astype(BF16)
        mown[b * 16 : (b + 1) * 16, :] = m
        moments.append(m.astype(F32))
    rows = jnp.swapaxes(jnp.stack(moments, axis=0), 0, 1)
    Mt[p.z, p.y, k] = jnp.concatenate([rows[r] for r in range(16)], axis=-1).astype(BF16)
    for b in range(16):
        X[3 + k, x, b] = own[b]

    p.greet()
    s = Sender(ss, rs)
    me = X.at[3 + k, x]
    to_up = s.copy(me, X.at[1 + k, x], p.up)
    to_down = s.copy(me, X.at[5 + k, x], p.down)
    far_yp = s.copy(Mt.at[p.z, p.y, k], Mt.at[p.z, p.y, k], p.y_plus)
    far_ym = s.copy(Mt.at[p.z, p.y, k], Mt.at[p.z, p.y, k], p.y_minus)

    def ring_start(u):
        src = X.at[u, x]
        return s.copy(src, X.at[u, x], p.east), s.copy(src, X.at[u, x], p.west)

    def ring_relay(u, pair):
        pair[0].wait_recv()
        pair[1].wait_recv()
        return (
            s.copy(X.at[u, p.xm, pl.ds(0, 8)], X.at[u, p.xm, pl.ds(0, 8)], p.east),
            s.copy(X.at[u, p.xp, pl.ds(8, 8)], X.at[u, p.xp, pl.ds(8, 8)], p.west),
        )

    def to_sib(u, at):
        return s.copy(X.at[u, at], X.at[u, at], p.sib)

    def relayout(q):
        loads[q].wait()

        @pl.loop(0, 64, unroll=2)
        def _(i):
            tf[pl.ds(pl.multiple_of(i * 64, 64), 64), :] = tin[q, i].astype(F32)

        @pl.loop(0, 64, unroll=2)
        def _(j):
            tb[q, j] = tf[pl.ds(j, 64, stride=64), :].astype(BF16)

        store = pltpu.make_async_copy(tb.at[q], tout.at[q], tout_sem.at[q])
        store.start()
        return store

    sib = []
    ring2 = ring_start(3 + k)
    sib.append(to_sib(3 + k, x))
    stores = [relayout(0)]
    to_up.wait_recv()
    to_down.wait_recv()
    two = s.copy(X.at[5 - 3 * k, x], X.at[7 - 7 * k, x], p.far_chip)
    ring1 = ring_start(1 + k)
    ring3 = ring_start(5 + k)
    sib.append(to_sib(1 + k, x))
    sib.append(to_sib(5 + k, x))
    far_yp.wait_recv()
    far_ym.wait_recv()
    far_y2 = (
        s.copy(Mt.at[p.z, p.ym, k, :, pl.ds(0, 512)], Mt.at[p.z, p.ym, k, :, pl.ds(0, 512)], p.y_plus),
        s.copy(Mt.at[p.z, p.yp, k, :, pl.ds(512, 512)], Mt.at[p.z, p.yp, k, :, pl.ds(512, 512)], p.y_minus),
    )
    relay2 = ring_relay(3 + k, ring2)
    sib.append(to_sib(3 + k, p.xm))
    sib.append(to_sib(3 + k, p.xp))
    stores.append(relayout(1))
    far_y2[0].wait_recv()
    far_y2[1].wait_recv()
    plane = Mt.at[p.z, :, k]
    far_zp = s.copy(plane, Mt.at[p.z, :, k], p.z_plus)
    far_zm = s.copy(plane, Mt.at[p.z, :, k], p.z_minus)
    sib.append(s.copy(plane, Mt.at[p.z, :, k], p.sib))
    two.wait_recv()
    ring0 = ring_start(7 * k)
    relay1 = ring_relay(1 + k, ring1)
    sib.append(to_sib(1 + k, p.xm))
    sib.append(to_sib(1 + k, p.xp))
    relay3 = ring_relay(5 + k, ring3)
    sib.append(to_sib(5 + k, p.xm))
    sib.append(to_sib(5 + k, p.xp))
    stores.append(relayout(2))
    far_zp.wait_recv()
    far_zm.wait_recv()
    far_z2 = (
        s.copy(Mt.at[p.zm, pl.ds(0, 2), k], Mt.at[p.zm, pl.ds(0, 2), k], p.z_plus),
        s.copy(Mt.at[p.zp, pl.ds(2, 2), k], Mt.at[p.zp, pl.ds(2, 2), k], p.z_minus),
    )
    sib.append(s.copy(Mt.at[p.zm, :, k], Mt.at[p.zm, :, k], p.sib))
    sib.append(s.copy(Mt.at[p.zp, :, k], Mt.at[p.zp, :, k], p.sib))
    relay0 = ring_relay(7 * k, ring0)
    stores.append(relayout(3))
    for u, relay in ((3 + k, relay2), (1 + k, relay1), (5 + k, relay3)):
        relay[0].wait_recv()
        relay[1].wait_recv()
        sib.append(to_sib(u, p.xo))
    far_z2[0].wait_recv()
    far_z2[1].wait_recv()
    sib.append(s.copy(Mt.at[p.zo, :, k], Mt.at[p.zo, :, k], p.sib))
    relay0[0].wait_recv()
    relay0[1].wait_recv()
    for made in sib:
        made.wait_recv()
    s.drain()
    for store in stores:
        store.wait()


PAIRS = 16
TERMS = 8
STEPS = 8


def local_kernel(
    nf, ns, tiles, X, tt, Mt, mown, fs, ft, nacc, S, out1, gsc, ysc, ohs, ohb
):
    step = pl.program_id(0)
    o = lax.axis_index("blk")
    k = o % 2
    base = lax.axis_index("rhs") * 128 + step * PAIRS
    tl = ft[...] - o * 16

    @pl.when(step == 0)
    def _():
        nacc[...] = jnp.zeros_like(nacc)
        out1[...] = jnp.zeros_like(out1)
        ohs[...] = jnp.where(
            lax.broadcasted_iota(jnp.int32, (512, 512), 0) == fs[...], 1.0, 0.0
        ).astype(BF16)
        for t in range(16):
            ohb[t * 16 : (t + 1) * 16, :] = jnp.broadcast_to(
                jnp.where(tl == t, 1.0, 0.0).astype(BF16), (16, 512)
            )
        for h in range(4):
            g = lax.dot_general(
                Mt[:, h * 256 : (h + 1) * 256], ohs[...], TN, preferred_element_type=F32
            )
            for q in range(4):
                gsc[q, h * 256 : (h + 1) * 256, :] = g[:, q * 128 : (q + 1) * 128]

    @pl.loop(0, PAIRS, unroll=4)
    def _(n):
        a = nf[base + n] - o * 16
        d = lax.rem(ns[base + n] - o * 16 + 560, 512)
        ub, bb = d // 16 + k, lax.rem(d, 16)
        ua = 3 + k
        tile = tiles[n]
        xb = X[ub, :, bb].reshape(64, 128)
        xa = X[ua, :, a].reshape(64, 128)
        to_first = lax.dot_general(xb, tile, NT, preferred_element_type=F32)
        to_second = jnp.dot(xa, tile, preferred_element_type=F32)
        nacc[ua, :, a] += to_first.reshape(4, 16, 128)
        nacc[ub, :, bb] += to_second.reshape(4, 16, 128)

    @pl.loop(0, TERMS, unroll=2)
    def _(jl):
        j = step * TERMS + jl
        ms = jnp.concatenate(
            [gsc[q, pl.ds(j, 16, stride=64), :] for q in range(4)], axis=-1
        ).astype(BF16)
        tj = jnp.concatenate([tt[q, jl] for q in range(4)], axis=-1)
        zj = (ohb[...].reshape(16, 16, 512) * ms[None]).reshape(256, 512)
        out1[...] += lax.dot_general(zj, tj, NT, preferred_element_type=F32)
        yj = jnp.dot(mown[...], tj, preferred_element_type=F32)
        y = jnp.where(tl == 0, yj[0:16], 0.0)
        for t in range(1, 16):
            y = y + jnp.where(tl == t, yj[t * 16 : (t + 1) * 16], 0.0)
        for q in range(4):
            ysc[q, pl.ds(j, 16, stride=64), :] = y[:, q * 128 : (q + 1) * 128]

    @pl.when(step == STEPS - 1)
    def _():
        for h in range(4):
            y = jnp.concatenate([ysc[q, h * 256 : (h + 1) * 256, :] for q in range(4)], axis=-1)
            hi = y.astype(BF16)
            lo = (y - hi.astype(F32)).astype(BF16)
            S[:, h * 256 : (h + 1) * 256] = lax.dot_general(
                ohs[...], hi, NT, preferred_element_type=F32
            ) + lax.dot_general(ohs[...], lo, NT, preferred_element_type=F32)


def reduce_kernel(
    nacc, S, out1, charges, counts, self_tiles, basis_t, out,
    R, C, A, B, D, E, V, Fr, H1, H3, RF, CF, AF, BF, DF, EF, W, AY, BY, DY, EY, ss, rs,
):
    p = Place()
    x, k = p.x, p.k
    p.greet()
    s = Sender(ss, rs)
    near_sib = [s.copy(nacc.at[2 - k + 2 * i], R.at[i], p.sib) for i in range(3)]
    far_sib = s.copy(S.at[:, :, 1 - k], RF, p.sib)
    own = 1 + k

    C[0] = nacc[7 * k]
    two = []
    ring = []

    def first(i):
        two.append(
            (
                s.copy(C.at[i, p.xo, pl.ds(0, 8)], A.at[i], p.east),
                s.copy(C.at[i, p.xo, pl.ds(8, 8)], B.at[i], p.west),
            )
        )

    first(0)
    for i in range(3):
        near_sib[i].wait_recv()
        C[i + 1] = nacc[own + 2 * i] + R[i]
        first(i + 1)
    far_sib.wait_recv()
    CF[...] = S[:, :, k] + RF[...]
    fz2 = (
        s.copy(CF.at[p.zo, pl.ds(0, 2)], AF, p.z_plus),
        s.copy(CF.at[p.zo, pl.ds(2, 2)], BF, p.z_minus),
    )
    for i in range(4):
        two[i][0].wait_recv()
        two[i][1].wait_recv()
        C[i, p.xp, pl.ds(0, 8)] += A[i]
        C[i, p.xm, pl.ds(8, 8)] += B[i]
        ring.append(
            (s.copy(C.at[i, p.xp], D.at[i], p.east), s.copy(C.at[i, p.xm], E.at[i], p.west))
        )
    fz2[0].wait_recv()
    fz2[1].wait_recv()
    CF[p.zp, pl.ds(0, 2)] += AF[...]
    CF[p.zm, pl.ds(2, 2)] += BF[...]
    fz = s.copy(CF.at[p.zp], DF, p.z_plus), s.copy(CF.at[p.zm], EF, p.z_minus)

    valid = []
    lane = lax.broadcasted_iota(jnp.int32, (16, 128), 1)
    for b in range(16):
        part = charges[:, b * 128 : (b + 1) * 128]
        part = jnp.where(lane < counts[b], part.astype(F32), 0.0).astype(BF16)
        out[:, b * 128 : (b + 1) * 128] = lax.dot_general(
            part, self_tiles[b], NT, preferred_element_type=F32
        )

    def summed(i):
        ring[i][0].wait_recv()
        ring[i][1].wait_recv()
        V[i] = C[i, x] + D[i] + E[i]

    summed(0)
    relay = s.copy(V.at[0], Fr, p.far_chip)
    summed(1)
    summed(2)
    summed(3)
    fz[0].wait_recv()
    fz[1].wait_recv()
    W[...] = CF[p.z] + DF[...] + EF[...]
    fy2 = (
        s.copy(W.at[p.yo, :, pl.ds(0, 512)], AY, p.y_plus),
        s.copy(W.at[p.yo, :, pl.ds(512, 512)], BY, p.y_minus),
    )
    relay.wait_recv()
    V[3 - 2 * k] += Fr[...]
    near_last = s.copy(V.at[1], H1, p.down), s.copy(V.at[3], H3, p.up)
    fy2[0].wait_recv()
    fy2[1].wait_recv()
    W[p.yp, :, pl.ds(0, 512)] += AY[...]
    W[p.ym, :, pl.ds(512, 512)] += BY[...]
    fy = s.copy(W.at[p.yp], DY, p.y_plus), s.copy(W.at[p.ym], EY, p.y_minus)
    fy[0].wait_recv()
    fy[1].wait_recv()
    flat = W[p.y] + DY[...] + EY[...]
    rows = jnp.stack([flat[:, r * 64 : (r + 1) * 64] for r in range(16)], axis=0)
    rows = jnp.swapaxes(rows, 0, 1)
    near_last[0].wait_recv()
    near_last[1].wait_recv()
    for b in range(16):
        fields = (rows[b] + out1[b * 16 : (b + 1) * 16, :]).astype(BF16)
        far_part = jnp.dot(fields, basis_t[b], preferred_element_type=F32)
        near = V[2, b] + H1[b] + H3[b]
        cols = slice(b * 128, (b + 1) * 128)
        out[:, cols] = jnp.where(lane < counts[b], out[:, cols] + near + far_part, 0.0)
    s.drain()


def vmem():
    return pl.BlockSpec(memory_space=pltpu.VMEM)


def body(
    charges, counts, self_tiles, basis, near_first, near_second, near_tiles, far_source, far_target, far_tiles
):
    basis_t = jnp.transpose(basis, (0, 2, 1))
    far_t = jnp.transpose(far_tiles, (1, 2, 0))
    smem = pl.BlockSpec(memory_space=pltpu.SMEM)
    anyspace = pl.BlockSpec(memory_space=pl.ANY)
    dma = pltpu.SemaphoreType.DMA
    X, Mt, mown, tt = pl.pallas_call(
        gather_kernel,
        name="gather",
        out_shape=(
            jax.ShapeDtypeStruct((8, 4, 16, 16, 128), BF16),
            jax.ShapeDtypeStruct((4, 4, 2, 16, 1024), BF16),
            jax.ShapeDtypeStruct((256, 64), BF16),
            jax.ShapeDtypeStruct((4, 64, 64, 128), BF16),
        ),
        in_specs=[vmem(), smem, vmem(), anyspace],
        out_specs=(vmem(), vmem(), vmem(), anyspace),
        scratch_shapes=[
            pltpu.VMEM((16, 16, 128), BF16),
            pltpu.VMEM((4, 64, 64, 128), BF16),
            pltpu.VMEM((4096, 128), F32),
            pltpu.VMEM((4, 64, 64, 128), BF16),
            dma((4,)),
            dma((4,)),
            dma((48,)),
            dma((48,)),
        ],
        compiler_params=pltpu.CompilerParams(
            collective_id=0, has_side_effects=True, vmem_limit_bytes=48 << 20
        ),
    )(charges, counts, basis_t, far_t)

    def whole(shape):
        return pl.BlockSpec(shape, lambda i, *_: (0,) * len(shape))

    nacc, S, out1 = pl.pallas_call(
        local_kernel,
        name="local",
        out_shape=(
            jax.ShapeDtypeStruct((8, 4, 16, 16, 128), F32),
            jax.ShapeDtypeStruct((512, 1024), F32),
            jax.ShapeDtypeStruct((256, 64), F32),
        ),
        grid_spec=pltpu.PrefetchScalarGridSpec(
            num_scalar_prefetch=2,
            grid=(STEPS,),
            in_specs=[
                pl.BlockSpec((PAIRS, 128, 128), lambda i, *_: (i, 0, 0)),
                whole((8, 4, 16, 16, 128)),
                pl.BlockSpec((4, TERMS, 64, 128), lambda i, *_: (0, i, 0, 0)),
                whole((512, 1024)),
                whole((256, 64)),
                whole((1, 512)),
                whole((1, 512)),
            ],
            out_specs=(
                whole((8, 4, 16, 16, 128)),
                whole((512, 1024)),
                whole((256, 64)),
            ),
            scratch_shapes=[
                pltpu.VMEM((4, 1024, 128), F32),
                pltpu.VMEM((4, 1024, 128), F32),
                pltpu.VMEM((512, 512), BF16),
                pltpu.VMEM((256, 512), BF16),
            ],
        ),
        compiler_params=pltpu.CompilerParams(vmem_limit_bytes=56 << 20),
    )(
        near_first,
        near_second,
        near_tiles,
        X,
        tt,
        Mt.reshape(512, 1024),
        mown,
        far_source.reshape(1, 512),
        far_target.reshape(1, 512),
    )
    chunk = (16, 16, 128)
    half = (8, 16, 128)
    return pl.pallas_call(
        reduce_kernel,
        name="reduce",
        out_shape=jax.ShapeDtypeStruct((16, 2048), F32),
        in_specs=[vmem(), vmem(), vmem(), vmem(), smem, vmem(), vmem()],
        out_specs=vmem(),
        scratch_shapes=[
            pltpu.VMEM((3, 4) + chunk, F32),
            pltpu.VMEM((4, 4) + chunk, F32),
            pltpu.VMEM((4,) + half, F32),
            pltpu.VMEM((4,) + half, F32),
            pltpu.VMEM((4,) + chunk, F32),
            pltpu.VMEM((4,) + chunk, F32),
            pltpu.VMEM((4,) + chunk, F32),
            pltpu.VMEM(chunk, F32),
            pltpu.VMEM(chunk, F32),
            pltpu.VMEM(chunk, F32),
            pltpu.VMEM((4, 4, 16, 1024), F32),
            pltpu.VMEM((4, 4, 16, 1024), F32),
            pltpu.VMEM((2, 16, 1024), F32),
            pltpu.VMEM((2, 16, 1024), F32),
            pltpu.VMEM((4, 16, 1024), F32),
            pltpu.VMEM((4, 16, 1024), F32),
            pltpu.VMEM((4, 16, 1024), F32),
            pltpu.VMEM((16, 512), F32),
            pltpu.VMEM((16, 512), F32),
            pltpu.VMEM((16, 1024), F32),
            pltpu.VMEM((16, 1024), F32),
            dma((32,)),
            dma((32,)),
        ],
        compiler_params=pltpu.CompilerParams(
            collective_id=1, has_side_effects=True, vmem_limit_bytes=56 << 20
        ),
    )(nacc, S.reshape(4, 4, 2, 16, 1024), out1, charges, counts, self_tiles, basis_t)


def solution(mesh):
    in_specs = (
        P("rhs", "blk"),
        P("blk"),
        P("blk", None, None),
        P("blk", None, None),
        P("blk"),
        P("blk"),
        P(("blk", "rhs"), None, None),
        P("blk"),
        P("blk"),
        P("blk", None, None),
    )
    return jax.shard_map(
        body, mesh=mesh, in_specs=in_specs, out_specs=P("rhs", "blk"), check_vma=False
    )
```

```python
import functools

import jax
import jax.numpy as jnp
from jax import lax
from jax.experimental import pallas as pl
from jax.experimental.pallas import tpu as pltpu
from jax.sharding import PartitionSpec as P

MESH = pl.DeviceIdType.MESH
F32 = jnp.float32
BF16 = jnp.bfloat16
NT = (((1,), (1,)), ((), ()))
TN = (((0,), (0,)), ((), ()))


class Place:
    def __init__(self):
        self.o = lax.axis_index("blk")
        self.x = lax.axis_index("rhs")
        self.k = self.o % 2
        self.c = self.o // 2
        self.y = self.c % 4
        self.z = self.c // 4
        self.xp = (self.x + 1) % 4
        self.xm = (self.x + 3) % 4
        self.xo = (self.x + 2) % 4
        self.yp = (self.y + 1) % 4
        self.ym = (self.y + 3) % 4
        self.yo = (self.y + 2) % 4
        self.zp = (self.z + 1) % 4
        self.zm = (self.z + 3) % 4
        self.zo = (self.z + 2) % 4
        self.sib = self.dev(self.c, 1 - self.k)
        self.east = {"blk": self.o, "rhs": self.xp}
        self.west = {"blk": self.o, "rhs": self.xm}
        self.cp = (self.c + 1) % 16
        self.cm = (self.c + 15) % 16
        self.up = self.dev(self.cp, self.k)
        self.down = self.dev(self.cm, self.k)
        self.up_other = self.dev(self.cp, 1 - self.k)
        self.down_other = self.dev(self.cm, 1 - self.k)
        self.y_plus = self.dev(self.z * 4 + self.yp, self.k)
        self.y_minus = self.dev(self.z * 4 + self.ym, self.k)
        self.z_plus = self.dev(self.zp * 4 + self.y, self.k)
        self.z_minus = self.dev(self.zm * 4 + self.y, self.k)
        self.far_chip = self.dev((self.c + 15 + 2 * self.k) % 16, 1 - self.k)

    def dev(self, chip, core):
        return {"blk": chip * 2 + core, "rhs": self.x}

    def greet(self):
        barrier = pltpu.get_barrier_semaphore()
        peers = [
            self.sib,
            self.east,
            self.west,
            self.up,
            self.down,
            self.up_other,
            self.down_other,
            self.y_plus,
            self.y_minus,
            self.z_plus,
            self.z_minus,
        ]
        for peer in peers:
            pl.semaphore_signal(barrier, inc=1, device_id=peer, device_id_type=MESH)
        pl.semaphore_wait(barrier, len(peers))


class Sender:
    def __init__(self, send_sems, recv_sems):
        self.send_sems, self.recv_sems, self.n, self.out = send_sems, recv_sems, 0, []

    def copy(self, src, dst, peer):
        at = self.n
        self.n += 1
        made = pltpu.make_async_remote_copy(
            src_ref=src,
            dst_ref=dst,
            send_sem=self.send_sems.at[at],
            recv_sem=self.recv_sems.at[at],
            device_id=peer,
            device_id_type=MESH,
        )
        made.start()
        self.out.append(made)
        return made

    def drain(self):
        for made in self.out:
            made.wait_send()


TG = 2
TQ = 16 // TG
NJ = 4


def gather_kernel(
    charges, counts, basis_t, far, fs, ft, X, S, out1,
    nbuf, qbuf, bbuf, ibuf, Mt, own, mq, tin, tt, tm, ohs, perm, mgb, mqb, gtmp, gj, yhi, ylo, zhi, zlo,
    in_sem, tin_sem, ss, rs,
):
    p = Place()
    x, k = p.x, p.k
    small = [
        pltpu.make_async_copy(charges, qbuf, in_sem.at[0]),
        pltpu.make_async_copy(basis_t, bbuf, in_sem.at[1]),
        pltpu.make_async_copy(fs, ibuf.at[0], in_sem.at[2]),
        pltpu.make_async_copy(ft, ibuf.at[1], in_sem.at[3]),
        pltpu.make_async_copy(counts, nbuf, in_sem.at[4]),
    ]
    loads = [
        pltpu.make_async_copy(far.at[pl.ds(i * 16, 16)], tin.at[pl.ds(i * 16, 16)], tin_sem.at[i])
        for i in range(4)
    ]
    for load in small + loads:
        load.start()
    row = lax.broadcasted_iota(jnp.int32, (256, 256), 0)
    col = lax.broadcasted_iota(jnp.int32, (256, 256), 1)
    swap = ((row >> 4) == (col & 15)) & ((row & 15) == (col >> 4))
    perm[...] = jnp.where(swap, 1.0, 0.0).astype(BF16)
    for load in small:
        load.wait()
    lane = lax.broadcasted_iota(jnp.int32, (16, 128), 1)
    moments = []
    for b in range(16):
        block = qbuf[:, b * 128 : (b + 1) * 128]
        block = jnp.where(lane < nbuf[b], block.astype(F32), 0.0).astype(BF16)
        own[b] = block
        m = lax.dot_general(block, bbuf[b], NT, preferred_element_type=F32).astype(BF16)
        moments.append(m.astype(F32))
    rows = jnp.swapaxes(jnp.stack(moments, axis=0), 0, 1)
    Mt[p.z, p.y, k] = jnp.concatenate([rows[r] for r in range(16)], axis=-1).astype(BF16)
    X[3 + k, x] = own[...]
    for a in range(TQ):
        mq[a * 16 : (a + 1) * 16, :] = jnp.concatenate(
            [moments[g * TQ + a] for g in range(TG)], axis=-1
        ).astype(BF16)

    p.greet()
    s = Sender(ss, rs)
    me = X.at[3 + k, x]
    to_up = s.copy(me, X.at[1 + k, x], p.up)
    to_down = s.copy(me, X.at[5 + k, x], p.down)
    far_yp = s.copy(Mt.at[p.z, p.y, k], Mt.at[p.z, p.y, k], p.y_plus)
    far_ym = s.copy(Mt.at[p.z, p.y, k], Mt.at[p.z, p.y, k], p.y_minus)

    def ring_start(u):
        src = X.at[u, x]
        return s.copy(src, X.at[u, x], p.east), s.copy(src, X.at[u, x], p.west)

    def ring_relay(u, pair):
        pair[0].wait_recv()
        pair[1].wait_recv()
        return (
            s.copy(X.at[u, p.xm, pl.ds(0, 8)], X.at[u, p.xm, pl.ds(0, 8)], p.east),
            s.copy(X.at[u, p.xp, pl.ds(8, 8)], X.at[u, p.xp, pl.ds(8, 8)], p.west),
        )

    def to_sib(u, at):
        return s.copy(X.at[u, at], X.at[u, at], p.sib)

    def relayout(i):
        loads[i].wait()

        @pl.loop(0, 4)
        def _(n):
            at = pl.ds(pl.multiple_of(n * 16, 16), 16)
            block = tin[i * 16 : (i + 1) * 16, at, :].reshape(256, 512)
            moved = jnp.dot(perm[...], block, preferred_element_type=F32).astype(BF16)
            tt[at, i * 16 : (i + 1) * 16, :] = moved.reshape(16, 16, 512)

    sib = []
    farsib = []
    ring2 = ring_start(3 + k)
    sib.append(to_sib(3 + k, x))
    tl = ibuf[1] - p.o * 16
    tg = tl // TQ
    tq = tl - tg * TQ
    ohs[...] = jnp.where(
        lax.broadcasted_iota(jnp.int32, (512, 512), 0) == ibuf[0], 1.0, 0.0
    ).astype(BF16)
    for g in range(TG):
        mgb[g] = jnp.broadcast_to(jnp.where(tg == g, 1.0, 0.0).astype(BF16), (16, 512))
    for g in range(TQ):
        mqb[g] = jnp.broadcast_to(jnp.where(tq == g, 1.0, 0.0).astype(BF16), (16, 512))
    out1[...] = jnp.zeros_like(out1)
    relayout(0)
    to_up.wait_recv()
    to_down.wait_recv()
    two = s.copy(X.at[5 - 3 * k, x], X.at[7 - 7 * k, x], p.far_chip)
    ring1 = ring_start(1 + k)
    ring3 = ring_start(5 + k)
    sib.append(to_sib(1 + k, x))
    sib.append(to_sib(5 + k, x))
    far_yp.wait_recv()
    far_ym.wait_recv()
    far_y2 = (
        s.copy(Mt.at[p.z, p.ym, k, :, pl.ds(0, 512)], Mt.at[p.z, p.ym, k, :, pl.ds(0, 512)], p.y_plus),
        s.copy(Mt.at[p.z, p.yp, k, :, pl.ds(512, 512)], Mt.at[p.z, p.yp, k, :, pl.ds(512, 512)], p.y_minus),
    )
    relay2 = ring_relay(3 + k, ring2)
    sib.append(to_sib(3 + k, p.xm))
    sib.append(to_sib(3 + k, p.xp))
    relayout(1)
    far_y2[0].wait_recv()
    far_y2[1].wait_recv()
    plane = Mt.at[p.z, :, k]
    far_zp = s.copy(plane, Mt.at[p.z, :, k], p.z_plus)
    far_zm = s.copy(plane, Mt.at[p.z, :, k], p.z_minus)
    farsib.append(s.copy(plane, Mt.at[p.z, :, k], p.sib))
    two.wait_recv()
    ring0 = ring_start(7 * k)
    relayout(2)
    relay1 = ring_relay(1 + k, ring1)
    sib.append(to_sib(1 + k, p.xm))
    sib.append(to_sib(1 + k, p.xp))
    relayout(3)
    far_zp.wait_recv()
    far_zm.wait_recv()
    far_z2 = (
        s.copy(Mt.at[p.zm, pl.ds(0, 2), k], Mt.at[p.zm, pl.ds(0, 2), k], p.z_plus),
        s.copy(Mt.at[p.zp, pl.ds(2, 2), k], Mt.at[p.zp, pl.ds(2, 2), k], p.z_minus),
    )
    farsib.append(s.copy(Mt.at[p.zm, :, k], Mt.at[p.zm, :, k], p.sib))
    farsib.append(s.copy(Mt.at[p.zp, :, k], Mt.at[p.zp, :, k], p.sib))
    relay3 = ring_relay(5 + k, ring3)
    sib.append(to_sib(5 + k, p.xm))
    sib.append(to_sib(5 + k, p.xp))
    far_z2[0].wait_recv()
    far_z2[1].wait_recv()
    farsib.append(s.copy(Mt.at[p.zo, :, k], Mt.at[p.zo, :, k], p.sib))
    relay0 = ring_relay(7 * k, ring0)
    for made in farsib:
        made.wait_recv()

    table = Mt[...].reshape(512, 1024)
    for h in range(4):
        gtmp[h * 256 : (h + 1) * 256, :] = lax.dot_general(
            table[:, h * 256 : (h + 1) * 256], ohs[...], TN, preferred_element_type=F32
        ).astype(BF16)
    for h in range(4):
        block = jnp.concatenate(
            [gtmp[r * 64 + h * 16 : r * 64 + (h + 1) * 16, :] for r in range(16)], axis=0
        )
        gj[h * 256 : (h + 1) * 256, :] = jnp.dot(
            perm[...], block, preferred_element_type=F32
        ).astype(BF16)

    def terms(lo, hi):
        @pl.loop(lo, hi)
        def _(n):
            zs = []
            for a in range(NJ):
                j = n * NJ + a
                ms = gj[pl.ds(pl.multiple_of(j * 16, 16), 16), :]
                tj = tt[j].reshape(4, 16, 512)
                for g in range(TG):
                    tm[a, g * 64 : (g + 1) * 64, :] = (tj * mgb[g][None]).reshape(64, 512)
                zs.append((ms[None] * mqb[...]).reshape(TQ * 16, 512))
            total = out1[...]
            for a in range(NJ):
                total = total + lax.dot_general(zs[a], tm[a], NT, preferred_element_type=F32)
            out1[...] = total
            for a in range(NJ):
                j = n * NJ + a
                yj = jnp.dot(mq[...], tm[a], preferred_element_type=F32)
                y = jnp.where(tq == 0, yj[0:16], 0.0)
                for g in range(1, TQ):
                    y = jnp.where(tq == g, yj[g * 16 : (g + 1) * 16], y)
                hi = y.astype(BF16)
                at = pl.ds(pl.multiple_of(j * 16, 16), 16)
                yhi[at, :] = hi
                ylo[at, :] = (y - hi.astype(F32)).astype(BF16)

    terms(0, 4)
    for u, relay in ((3 + k, relay2), (1 + k, relay1)):
        relay[0].wait_recv()
        relay[1].wait_recv()
        sib.append(to_sib(u, p.xo))
    terms(4, 8)
    relay3[0].wait_recv()
    relay3[1].wait_recv()
    sib.append(to_sib(5 + k, p.xo))
    terms(8, 16)
    for h in range(4):
        for src, dst in ((yhi, zhi), (ylo, zlo)):
            moved = jnp.dot(
                perm[...], src[h * 256 : (h + 1) * 256, :], preferred_element_type=F32
            ).astype(BF16)
            for r in range(16):
                dst[r * 64 + h * 16 : r * 64 + (h + 1) * 16, :] = moved[r * 16 : (r + 1) * 16]
    for h in range(4):
        at = slice(h * 256, (h + 1) * 256)
        S[:, at] = lax.dot_general(
            ohs[...], zhi[at, :], NT, preferred_element_type=F32
        ) + lax.dot_general(ohs[...], zlo[at, :], NT, preferred_element_type=F32)
    relay0[0].wait_recv()
    relay0[1].wait_recv()
    for made in sib:
        made.wait_recv()
    s.drain()


def local_kernel(nf, ns, tiles, X, nacc):
    o = lax.axis_index("blk")
    k = o % 2
    base = lax.axis_index("rhs") * 128
    nacc[...] = jnp.zeros_like(nacc)

    @pl.loop(0, 128, unroll=8)
    def _(n):
        a = nf[base + n] - o * 16
        d = lax.rem(ns[base + n] - o * 16 + 560, 512)
        ub, bb = d // 16 + k, lax.rem(d, 16)
        ua = 3 + k
        tile = tiles[n]
        xb = X[ub, :, bb].reshape(64, 128)
        xa = X[ua, :, a].reshape(64, 128)
        to_first = lax.dot_general(xb, tile, NT, preferred_element_type=F32)
        to_second = jnp.dot(xa, tile, preferred_element_type=F32)
        nacc[ua, :, a] += to_first.reshape(4, 16, 128)
        nacc[ub, :, bb] += to_second.reshape(4, 16, 128)


def reduce_kernel(
    nacc, S, out1, charges, counts, self_tiles, basis_t, out,
    R, C, A, B, D, E, V, Fr, H1, H3, RF, CF, AF, BF, DF, EF, W, AY, BY, DY, EY, ss, rs,
):
    p = Place()
    x, k = p.x, p.k
    p.greet()
    s = Sender(ss, rs)
    near_sib = [s.copy(nacc.at[2 - k + 2 * i], R.at[i], p.sib) for i in range(3)]
    far_sib = s.copy(S.at[:, :, 1 - k], RF, p.sib)
    own = 1 + k

    C[0] = nacc[7 * k]
    two = []
    ring = []

    def first(i):
        two.append(
            (
                s.copy(C.at[i, p.xo, pl.ds(0, 8)], A.at[i], p.east),
                s.copy(C.at[i, p.xo, pl.ds(8, 8)], B.at[i], p.west),
            )
        )

    first(0)
    for i in range(3):
        near_sib[i].wait_recv()
        C[i + 1] = nacc[own + 2 * i] + R[i]
        first(i + 1)
    far_sib.wait_recv()
    CF[...] = S[:, :, k] + RF[...]
    fz2 = (
        s.copy(CF.at[p.zo, pl.ds(0, 2)], AF, p.z_plus),
        s.copy(CF.at[p.zo, pl.ds(2, 2)], BF, p.z_minus),
    )
    for i in range(4):
        two[i][0].wait_recv()
        two[i][1].wait_recv()
        C[i, p.xp, pl.ds(0, 8)] += A[i]
        C[i, p.xm, pl.ds(8, 8)] += B[i]
        ring.append(
            (s.copy(C.at[i, p.xp], D.at[i], p.east), s.copy(C.at[i, p.xm], E.at[i], p.west))
        )
    fz2[0].wait_recv()
    fz2[1].wait_recv()
    CF[p.zp, pl.ds(0, 2)] += AF[...]
    CF[p.zm, pl.ds(2, 2)] += BF[...]
    fz = s.copy(CF.at[p.zp], DF, p.z_plus), s.copy(CF.at[p.zm], EF, p.z_minus)

    valid = []
    lane = lax.broadcasted_iota(jnp.int32, (16, 128), 1)
    for b in range(16):
        part = charges[:, b * 128 : (b + 1) * 128]
        part = jnp.where(lane < counts[b], part.astype(F32), 0.0).astype(BF16)
        out[:, b * 128 : (b + 1) * 128] = lax.dot_general(
            part, self_tiles[b], NT, preferred_element_type=F32
        )

    def summed(i):
        ring[i][0].wait_recv()
        ring[i][1].wait_recv()
        V[i] = C[i, x] + D[i] + E[i]

    summed(0)
    relay = s.copy(V.at[0], Fr, p.far_chip)
    summed(1)
    summed(2)
    summed(3)
    fz[0].wait_recv()
    fz[1].wait_recv()
    W[...] = CF[p.z] + DF[...] + EF[...]
    fy2 = (
        s.copy(W.at[p.yo, :, pl.ds(0, 512)], AY, p.y_plus),
        s.copy(W.at[p.yo, :, pl.ds(512, 512)], BY, p.y_minus),
    )
    relay.wait_recv()
    V[3 - 2 * k] += Fr[...]
    near_last = s.copy(V.at[1], H1, p.down), s.copy(V.at[3], H3, p.up)
    fy2[0].wait_recv()
    fy2[1].wait_recv()
    W[p.yp, :, pl.ds(0, 512)] += AY[...]
    W[p.ym, :, pl.ds(512, 512)] += BY[...]
    fy = s.copy(W.at[p.yp], DY, p.y_plus), s.copy(W.at[p.ym], EY, p.y_minus)
    fy[0].wait_recv()
    fy[1].wait_recv()
    flat = W[p.y] + DY[...] + EY[...]
    rows = jnp.stack([flat[:, r * 64 : (r + 1) * 64] for r in range(16)], axis=0)
    rows = jnp.swapaxes(rows, 0, 1)
    near_last[0].wait_recv()
    near_last[1].wait_recv()
    for b in range(16):
        own1 = out1[b % TQ * 16 : b % TQ * 16 + 16, b // TQ * 64 : b // TQ * 64 + 64]
        fields = (rows[b] + own1).astype(BF16)
        far_part = jnp.dot(fields, basis_t[b], preferred_element_type=F32)
        near = V[2, b] + H1[b] + H3[b]
        cols = slice(b * 128, (b + 1) * 128)
        out[:, cols] = jnp.where(lane < counts[b], out[:, cols] + near + far_part, 0.0)
    s.drain()


def vmem():
    return pl.BlockSpec(memory_space=pltpu.VMEM)


def body(
    charges, counts, self_tiles, basis, near_first, near_second, near_tiles, far_source, far_target, far_tiles
):
    basis_t = jnp.transpose(basis, (0, 2, 1))
    far_t = jnp.transpose(far_tiles, (1, 2, 0))
    smem = pl.BlockSpec(memory_space=pltpu.SMEM)
    hbm = pl.BlockSpec(memory_space=pltpu.HBM)
    dma = pltpu.SemaphoreType.DMA
    X, S, out1 = pl.pallas_call(
        gather_kernel,
        name="gather",
        out_shape=(
            jax.ShapeDtypeStruct((8, 4, 16, 16, 128), BF16),
            jax.ShapeDtypeStruct((512, 1024), F32),
            jax.ShapeDtypeStruct((TQ * 16, TG * 64), F32),
        ),
        in_specs=[hbm] * 6,
        out_specs=(vmem(), vmem(), vmem()),
        scratch_shapes=[
            pltpu.SMEM((16,), jnp.int32),
            pltpu.VMEM((16, 2048), BF16),
            pltpu.VMEM((16, 64, 128), BF16),
            pltpu.VMEM((2, 1, 512), jnp.int32),
            pltpu.VMEM((4, 4, 2, 16, 1024), BF16),
            pltpu.VMEM((16, 16, 128), BF16),
            pltpu.VMEM((TQ * 16, TG * 64), BF16),
            pltpu.VMEM((64, 64, 512), BF16),
            pltpu.VMEM((64, 64, 512), BF16),
            pltpu.VMEM((NJ, TG * 64, 512), BF16),
            pltpu.VMEM((512, 512), BF16),
            pltpu.VMEM((256, 256), BF16),
            pltpu.VMEM((TG, 16, 512), BF16),
            pltpu.VMEM((TQ, 16, 512), BF16),
            pltpu.VMEM((1024, 512), BF16),
            pltpu.VMEM((1024, 512), BF16),
            pltpu.VMEM((1024, 512), BF16),
            pltpu.VMEM((1024, 512), BF16),
            pltpu.VMEM((1024, 512), BF16),
            pltpu.VMEM((1024, 512), BF16),
            dma((5,)),
            dma((4,)),
            dma((48,)),
            dma((48,)),
        ],
        compiler_params=pltpu.CompilerParams(
            collective_id=0, has_side_effects=True, vmem_limit_bytes=32 << 20
        ),
    )(*[
        pltpu.with_memory_space_constraint(a, pltpu.HBM)
        for a in (
            charges,
            counts,
            basis_t,
            far_t,
            far_source.reshape(1, 512),
            far_target.reshape(1, 512),
        )
    ])
    nacc = pl.pallas_call(
        local_kernel,
        name="local",
        out_shape=jax.ShapeDtypeStruct((8, 4, 16, 16, 128), F32),
        in_specs=[smem, smem, vmem(), vmem()],
        out_specs=vmem(),
        compiler_params=pltpu.CompilerParams(vmem_limit_bytes=24 << 20),
    )(near_first, near_second, near_tiles, X)
    chunk = (16, 16, 128)
    half = (8, 16, 128)
    return pl.pallas_call(
        reduce_kernel,
        name="reduce",
        out_shape=jax.ShapeDtypeStruct((16, 2048), F32),
        in_specs=[vmem(), vmem(), vmem(), vmem(), smem, vmem(), vmem()],
        out_specs=vmem(),
        scratch_shapes=[
            pltpu.VMEM((3, 4) + chunk, F32),
            pltpu.VMEM((4, 4) + chunk, F32),
            pltpu.VMEM((4,) + half, F32),
            pltpu.VMEM((4,) + half, F32),
            pltpu.VMEM((4,) + chunk, F32),
            pltpu.VMEM((4,) + chunk, F32),
            pltpu.VMEM((4,) + chunk, F32),
            pltpu.VMEM(chunk, F32),
            pltpu.VMEM(chunk, F32),
            pltpu.VMEM(chunk, F32),
            pltpu.VMEM((4, 4, 16, 1024), F32),
            pltpu.VMEM((4, 4, 16, 1024), F32),
            pltpu.VMEM((2, 16, 1024), F32),
            pltpu.VMEM((2, 16, 1024), F32),
            pltpu.VMEM((4, 16, 1024), F32),
            pltpu.VMEM((4, 16, 1024), F32),
            pltpu.VMEM((4, 16, 1024), F32),
            pltpu.VMEM((16, 512), F32),
            pltpu.VMEM((16, 512), F32),
            pltpu.VMEM((16, 1024), F32),
            pltpu.VMEM((16, 1024), F32),
            dma((32,)),
            dma((32,)),
        ],
        compiler_params=pltpu.CompilerParams(
            collective_id=1, has_side_effects=True, vmem_limit_bytes=36 << 20
        ),
    )(nacc, S.reshape(4, 4, 2, 16, 1024), out1, charges, counts, self_tiles, basis_t)


def solution(mesh):
    in_specs = (
        P("rhs", "blk"),
        P("blk"),
        P("blk", None, None),
        P("blk", None, None),
        P("blk"),
        P("blk"),
        P(("blk", "rhs"), None, None),
        P("blk"),
        P("blk"),
        P("blk", None, None),
    )
    return jax.shard_map(
        body, mesh=mesh, in_specs=in_specs, out_specs=P("rhs", "blk"), check_vma=False
    )
```

```python
import functools

import jax
import jax.numpy as jnp
from jax import lax
from jax.experimental import pallas as pl
from jax.experimental.pallas import tpu as pltpu
from jax.sharding import PartitionSpec as P

MESH = pl.DeviceIdType.MESH
F32 = jnp.float32
BF16 = jnp.bfloat16
NT = (((1,), (1,)), ((), ()))
TN = (((0,), (0,)), ((), ()))


class Place:
    def __init__(self):
        self.o = lax.axis_index("blk")
        self.x = lax.axis_index("rhs")
        self.k = self.o % 2
        self.c = self.o // 2
        self.y = self.c % 4
        self.z = self.c // 4
        self.xp = (self.x + 1) % 4
        self.xm = (self.x + 3) % 4
        self.xo = (self.x + 2) % 4
        self.yp = (self.y + 1) % 4
        self.ym = (self.y + 3) % 4
        self.yo = (self.y + 2) % 4
        self.zp = (self.z + 1) % 4
        self.zm = (self.z + 3) % 4
        self.zo = (self.z + 2) % 4
        self.sib = self.dev(self.c, 1 - self.k)
        self.east = {"blk": self.o, "rhs": self.xp}
        self.west = {"blk": self.o, "rhs": self.xm}
        self.cp = (self.c + 1) % 16
        self.cm = (self.c + 15) % 16
        self.up = self.dev(self.cp, self.k)
        self.down = self.dev(self.cm, self.k)
        self.up_other = self.dev(self.cp, 1 - self.k)
        self.down_other = self.dev(self.cm, 1 - self.k)
        self.y_plus = self.dev(self.z * 4 + self.yp, self.k)
        self.y_minus = self.dev(self.z * 4 + self.ym, self.k)
        self.z_plus = self.dev(self.zp * 4 + self.y, self.k)
        self.z_minus = self.dev(self.zm * 4 + self.y, self.k)
        self.far_chip = self.dev((self.c + 15 + 2 * self.k) % 16, 1 - self.k)

    def dev(self, chip, core):
        return {"blk": chip * 2 + core, "rhs": self.x}

    def greet(self):
        self.barrier = pltpu.get_barrier_semaphore()
        self.peers = [
            self.sib,
            self.east,
            self.west,
            self.up,
            self.down,
            self.up_other,
            self.down_other,
            self.y_plus,
            self.y_minus,
            self.z_plus,
            self.z_minus,
        ]
        for peer in self.peers:
            pl.semaphore_signal(self.barrier, inc=1, device_id=peer, device_id_type=MESH)

    def met(self):
        pl.semaphore_wait(self.barrier, len(self.peers))


class Sender:
    def __init__(self, send_sems, recv_sems):
        self.send_sems, self.recv_sems, self.n, self.out = send_sems, recv_sems, 0, []

    def copy(self, src, dst, peer):
        at = self.n
        self.n += 1
        made = pltpu.make_async_remote_copy(
            src_ref=src,
            dst_ref=dst,
            send_sem=self.send_sems.at[at],
            recv_sem=self.recv_sems.at[at],
            device_id=peer,
            device_id_type=MESH,
        )
        made.start()
        self.out.append(made)
        return made

    def drain(self):
        for made in self.out:
            made.wait_send()


TG = 2
TQ = 16 // TG
NJ = 4


def gather_kernel(
    charges, counts, basis_t, far, fs, ft, X, S, out1,
    nbuf, qbuf, bbuf, ibuf, Mt, own, mq, tin, tm, ohs, perm, mgb, mqb, gtmp, gj, yhi, ylo, zhi, zlo,
    in_sem, tin_sem, ss, rs,
):
    p = Place()
    x, k = p.x, p.k
    p.greet()
    small = [
        pltpu.make_async_copy(charges, qbuf, in_sem.at[0]),
        pltpu.make_async_copy(basis_t, bbuf, in_sem.at[1]),
        pltpu.make_async_copy(counts, nbuf, in_sem.at[2]),
        pltpu.make_async_copy(fs, ibuf.at[0], in_sem.at[3]),
        pltpu.make_async_copy(ft, ibuf.at[1], in_sem.at[4]),
    ]
    loads = [
        pltpu.make_async_copy(far.at[pl.ds(i * 16, 16)], tin.at[pl.ds(i * 16, 16)], tin_sem.at[i])
        for i in range(4)
    ]
    for load in small + loads:
        load.start()
    for load in small[:3]:
        load.wait()
    lane = lax.broadcasted_iota(jnp.int32, (16, 128), 1)
    for b in range(16):
        block = qbuf[:, b * 128 : (b + 1) * 128]
        own[b] = jnp.where(lane < nbuf[b], block.astype(F32), 0.0).astype(BF16)
    X[3 + k, x] = own[...]
    p.met()
    s = Sender(ss, rs)
    sib = []
    farsib = []
    me = X.at[3 + k, x]

    def ring_start(u):
        src = X.at[u, x]
        return s.copy(src, X.at[u, x], p.east), s.copy(src, X.at[u, x], p.west)

    def arrived(pair):
        for made in pair:
            made.wait_recv()

    def ring_relay(u, pair):
        arrived(pair)
        made = (
            s.copy(X.at[u, p.xm, pl.ds(0, 8)], X.at[u, p.xm, pl.ds(0, 8)], p.east),
            s.copy(X.at[u, p.xp, pl.ds(8, 8)], X.at[u, p.xp, pl.ds(8, 8)], p.west),
        )
        if u is not edge:
            to_sib(u, p.xm)
            to_sib(u, p.xp)
        return made

    def to_sib(u, at):
        sib.append(s.copy(X.at[u, at], X.at[u, at], p.sib))

    u0, u1, u2, u3 = 7 * k, 1 + k, 3 + k, 5 + k
    edge = u0
    to_up = s.copy(me, X.at[u1, x], p.up)
    to_down = s.copy(me, X.at[u3, x], p.down)
    ring2 = ring_start(u2)

    moments = []
    for b in range(16):
        m = lax.dot_general(own[b], bbuf[b], NT, preferred_element_type=F32).astype(BF16)
        moments.append(m.astype(F32))
    rows = jnp.swapaxes(jnp.stack(moments, axis=0), 0, 1)
    Mt[p.z, p.y, k] = jnp.concatenate([rows[r] for r in range(16)], axis=-1).astype(BF16)
    mine = Mt.at[p.z, p.y, k]
    far_y = (s.copy(mine, mine, p.y_plus), s.copy(mine, mine, p.y_minus))
    to_sib(u2, x)

    for a in range(TQ):
        mq[a * 16 : (a + 1) * 16, :] = jnp.concatenate(
            [moments[g * TQ + a] for g in range(TG)], axis=-1
        ).astype(BF16)
    row = lax.broadcasted_iota(jnp.int32, (256, 256), 0)
    col = lax.broadcasted_iota(jnp.int32, (256, 256), 1)
    swap = ((row >> 4) == (col & 15)) & ((row & 15) == (col >> 4))
    perm[...] = jnp.where(swap, 1.0, 0.0).astype(BF16)
    small[3].wait()
    small[4].wait()
    tl = ibuf[1] - p.o * 16
    tg = tl // TQ
    tq = tl - tg * TQ
    ohs[...] = jnp.where(
        lax.broadcasted_iota(jnp.int32, (512, 512), 0) == ibuf[0], 1.0, 0.0
    ).astype(BF16)
    for g in range(TG):
        mgb[g] = jnp.broadcast_to(jnp.where(tg == g, 1.0, 0.0).astype(BF16), (16, 512))
    for g in range(TQ):
        mqb[g] = jnp.broadcast_to(jnp.where(tq == g, 1.0, 0.0).astype(BF16), (16, 512))
    out1[...] = jnp.zeros_like(out1)

    def relayout(i):
        loads[i].wait()

        @pl.loop(0, 4)
        def _(n):
            at = pl.ds(pl.multiple_of(n * 16, 16), 16)
            block = tin[i * 16 : (i + 1) * 16, at, :].reshape(256, 512)
            moved = jnp.dot(perm[...], block, preferred_element_type=F32).astype(BF16)
            moved = moved.reshape(16, 16, 512)
            for g in range(TG):
                tm[at, g * 64 + i * 16 : g * 64 + (i + 1) * 16, :] = moved * mgb[g][None]

    def to_sources(first, last):
        @pl.loop(first, last)
        def _(n):
            for a in range(NJ):
                j = n * NJ + a
                yj = jnp.dot(mq[...], tm[j], preferred_element_type=F32)
                y = jnp.where(tq == 0, yj[0:16], 0.0)
                for g in range(1, TQ):
                    y = jnp.where(tq == g, yj[g * 16 : (g + 1) * 16], y)
                hi = y.astype(BF16)
                at = pl.ds(pl.multiple_of(j * 16, 16), 16)
                yhi[at, :] = hi
                ylo[at, :] = (y - hi.astype(F32)).astype(BF16)

    def to_targets(first, last):
        @pl.loop(first, last)
        def _(n):
            total = out1[...]
            for a in range(NJ):
                j = n * NJ + a
                ms = gj[pl.ds(pl.multiple_of(j * 16, 16), 16), :]
                zj = (ms[None] * mqb[...]).reshape(TQ * 16, 512)
                total = total + lax.dot_general(zj, tm[j], NT, preferred_element_type=F32)
            out1[...] = total

    relayout(0)
    relayout(1)
    arrived((to_up, to_down))
    two = s.copy(X.at[5 - 3 * k, x], X.at[7 - 7 * k, x], p.far_chip)
    ring1 = ring_start(u1)
    ring3 = ring_start(u3)
    to_sib(u1, x)
    to_sib(u3, x)
    arrived(far_y)
    low, high = pl.ds(0, 512), pl.ds(512, 512)
    far_y2 = (
        s.copy(Mt.at[p.z, p.ym, k, :, low], Mt.at[p.z, p.ym, k, :, low], p.y_plus),
        s.copy(Mt.at[p.z, p.yp, k, :, high], Mt.at[p.z, p.yp, k, :, high], p.y_minus),
    )
    relayout(2)
    relay2 = ring_relay(u2, ring2)
    relayout(3)
    to_sources(0, 2)
    arrived(far_y2)
    plane = Mt.at[p.z, :, k]
    far_z = s.copy(plane, plane, p.z_plus), s.copy(plane, plane, p.z_minus)
    farsib.append(s.copy(plane, plane, p.sib))
    two.wait_recv()
    ring0 = ring_start(u0)
    to_sources(2, 5)
    relay1 = ring_relay(u1, ring1)
    to_sources(5, 7)
    relay3 = ring_relay(u3, ring3)
    to_sources(7, 10)
    arrived(far_z)
    after, before = Mt.at[p.zm, pl.ds(0, 2), k], Mt.at[p.zp, pl.ds(2, 2), k]
    far_z2 = s.copy(after, after, p.z_plus), s.copy(before, before, p.z_minus)
    for z in (p.zm, p.zp):
        farsib.append(s.copy(Mt.at[z, :, k], Mt.at[z, :, k], p.sib))
    to_sources(10, 13)
    arrived(relay2)
    to_sib(u2, p.xo)
    relay0 = ring_relay(u0, ring0)
    to_sources(13, 16)
    arrived(far_z2)
    farsib.append(s.copy(Mt.at[p.zo, :, k], Mt.at[p.zo, :, k], p.sib))
    for h in range(4):
        for src, dst in ((yhi, zhi), (ylo, zlo)):
            moved = jnp.dot(
                perm[...], src[h * 256 : (h + 1) * 256, :], preferred_element_type=F32
            ).astype(BF16)
            for r in range(16):
                dst[r * 64 + h * 16 : r * 64 + (h + 1) * 16, :] = moved[r * 16 : (r + 1) * 16]
    arrived(relay1)
    to_sib(u1, p.xo)
    for h in range(4):
        at = slice(h * 256, (h + 1) * 256)
        S[:, at] = lax.dot_general(
            ohs[...], zhi[at, :], NT, preferred_element_type=F32
        ) + lax.dot_general(ohs[...], zlo[at, :], NT, preferred_element_type=F32)
    arrived(relay3)
    to_sib(u3, p.xo)
    arrived(farsib)

    table = Mt[...].reshape(512, 1024)
    for h in range(4):
        gtmp[h * 256 : (h + 1) * 256, :] = lax.dot_general(
            table[:, h * 256 : (h + 1) * 256], ohs[...], TN, preferred_element_type=F32
        ).astype(BF16)
    for h in range(4):
        block = jnp.concatenate(
            [gtmp[r * 64 + h * 16 : r * 64 + (h + 1) * 16, :] for r in range(16)], axis=0
        )
        gj[h * 256 : (h + 1) * 256, :] = jnp.dot(
            perm[...], block, preferred_element_type=F32
        ).astype(BF16)
    to_targets(0, 16)
    arrived(relay0)
    arrived(sib)
    s.drain()


def local_kernel(nf, ns, tiles, X, nacc):
    o = lax.axis_index("blk")
    k = o % 2
    base = lax.axis_index("rhs") * 128
    nacc[...] = jnp.zeros_like(nacc)

    @pl.loop(0, 128, unroll=8)
    def _(n):
        a = nf[base + n] - o * 16
        d = lax.rem(ns[base + n] - o * 16 + 560, 512)
        ub, bb = d // 16 + k, lax.rem(d, 16)
        ua = 3 + k
        tile = tiles[n]
        xb = X[ub, :, bb].reshape(64, 128)
        xa = X[ua, :, a].reshape(64, 128)
        to_first = lax.dot_general(xb, tile, NT, preferred_element_type=F32)
        to_second = jnp.dot(xa, tile, preferred_element_type=F32)
        nacc[ua, :, a] += to_first.reshape(4, 16, 128)
        nacc[ub, :, bb] += to_second.reshape(4, 16, 128)


def reduce_kernel(
    nacc, S, out1, charges, counts, self_tiles, basis_t, out,
    R, C, A, B, D, E, V, Fr, H1, H3, RF, CF, AF, BF, DF, EF, W, AY, BY, DY, EY, ss, rs,
):
    p = Place()
    x, k = p.x, p.k
    p.greet()
    p.met()
    s = Sender(ss, rs)
    near_sib = [s.copy(nacc.at[2 - k + 2 * i], R.at[i], p.sib) for i in range(3)]
    far_sib = s.copy(S.at[:, :, 1 - k], RF, p.sib)
    own = 1 + k

    C[0] = nacc[7 * k]
    two = []
    ring = []

    def first(i):
        two.append(
            (
                s.copy(C.at[i, p.xo, pl.ds(0, 8)], A.at[i], p.east),
                s.copy(C.at[i, p.xo, pl.ds(8, 8)], B.at[i], p.west),
            )
        )

    first(0)
    for i in range(3):
        near_sib[i].wait_recv()
        C[i + 1] = nacc[own + 2 * i] + R[i]
        first(i + 1)
    far_sib.wait_recv()
    CF[...] = S[:, :, k] + RF[...]
    fz2 = (
        s.copy(CF.at[p.zo, pl.ds(0, 2)], AF, p.z_plus),
        s.copy(CF.at[p.zo, pl.ds(2, 2)], BF, p.z_minus),
    )
    for i in range(4):
        two[i][0].wait_recv()
        two[i][1].wait_recv()
        C[i, p.xp, pl.ds(0, 8)] += A[i]
        C[i, p.xm, pl.ds(8, 8)] += B[i]
        ring.append(
            (s.copy(C.at[i, p.xp], D.at[i], p.east), s.copy(C.at[i, p.xm], E.at[i], p.west))
        )
    fz2[0].wait_recv()
    fz2[1].wait_recv()
    CF[p.zp, pl.ds(0, 2)] += AF[...]
    CF[p.zm, pl.ds(2, 2)] += BF[...]
    fz = s.copy(CF.at[p.zp], DF, p.z_plus), s.copy(CF.at[p.zm], EF, p.z_minus)

    valid = []
    lane = lax.broadcasted_iota(jnp.int32, (16, 128), 1)
    for b in range(16):
        part = charges[:, b * 128 : (b + 1) * 128]
        part = jnp.where(lane < counts[b], part.astype(F32), 0.0).astype(BF16)
        out[:, b * 128 : (b + 1) * 128] = lax.dot_general(
            part, self_tiles[b], NT, preferred_element_type=F32
        )

    def summed(i):
        ring[i][0].wait_recv()
        ring[i][1].wait_recv()
        V[i] = C[i, x] + D[i] + E[i]

    summed(0)
    relay = s.copy(V.at[0], Fr, p.far_chip)
    summed(1)
    summed(2)
    summed(3)
    fz[0].wait_recv()
    fz[1].wait_recv()
    W[...] = CF[p.z] + DF[...] + EF[...]
    fy2 = (
        s.copy(W.at[p.yo, :, pl.ds(0, 512)], AY, p.y_plus),
        s.copy(W.at[p.yo, :, pl.ds(512, 512)], BY, p.y_minus),
    )
    relay.wait_recv()
    V[3 - 2 * k] += Fr[...]
    near_last = s.copy(V.at[1], H1, p.down), s.copy(V.at[3], H3, p.up)
    fy2[0].wait_recv()
    fy2[1].wait_recv()
    W[p.yp, :, pl.ds(0, 512)] += AY[...]
    W[p.ym, :, pl.ds(512, 512)] += BY[...]
    fy = s.copy(W.at[p.yp], DY, p.y_plus), s.copy(W.at[p.ym], EY, p.y_minus)
    fy[0].wait_recv()
    fy[1].wait_recv()
    flat = W[p.y] + DY[...] + EY[...]
    rows = jnp.stack([flat[:, r * 64 : (r + 1) * 64] for r in range(16)], axis=0)
    rows = jnp.swapaxes(rows, 0, 1)
    near_last[0].wait_recv()
    near_last[1].wait_recv()
    for b in range(16):
        own1 = out1[b % TQ * 16 : b % TQ * 16 + 16, b // TQ * 64 : b // TQ * 64 + 64]
        fields = (rows[b] + own1).astype(BF16)
        far_part = jnp.dot(fields, basis_t[b], preferred_element_type=F32)
        near = V[2, b] + H1[b] + H3[b]
        cols = slice(b * 128, (b + 1) * 128)
        out[:, cols] = jnp.where(lane < counts[b], out[:, cols] + near + far_part, 0.0)
    s.drain()


def vmem():
    return pl.BlockSpec(memory_space=pltpu.VMEM)


def body(
    charges, counts, self_tiles, basis, near_first, near_second, near_tiles, far_source, far_target, far_tiles
):
    basis_t = jnp.transpose(basis, (0, 2, 1))
    far_t = jnp.transpose(far_tiles, (1, 2, 0))
    smem = pl.BlockSpec(memory_space=pltpu.SMEM)
    hbm = pl.BlockSpec(memory_space=pltpu.HBM)
    dma = pltpu.SemaphoreType.DMA
    X, S, out1 = pl.pallas_call(
        gather_kernel,
        name="gather",
        out_shape=(
            jax.ShapeDtypeStruct((8, 4, 16, 16, 128), BF16),
            jax.ShapeDtypeStruct((512, 1024), F32),
            jax.ShapeDtypeStruct((TQ * 16, TG * 64), F32),
        ),
        in_specs=[hbm] * 6,
        out_specs=(vmem(), vmem(), vmem()),
        scratch_shapes=[
            pltpu.SMEM((16,), jnp.int32),
            pltpu.VMEM((16, 2048), BF16),
            pltpu.VMEM((16, 64, 128), BF16),
            pltpu.VMEM((2, 1, 512), jnp.int32),
            pltpu.VMEM((4, 4, 2, 16, 1024), BF16),
            pltpu.VMEM((16, 16, 128), BF16),
            pltpu.VMEM((TQ * 16, TG * 64), BF16),
            pltpu.VMEM((64, 64, 512), BF16),
            pltpu.VMEM((64, TG * 64, 512), BF16),
            pltpu.VMEM((512, 512), BF16),
            pltpu.VMEM((256, 256), BF16),
            pltpu.VMEM((TG, 16, 512), BF16),
            pltpu.VMEM((TQ, 16, 512), BF16),
            pltpu.VMEM((1024, 512), BF16),
            pltpu.VMEM((1024, 512), BF16),
            pltpu.VMEM((1024, 512), BF16),
            pltpu.VMEM((1024, 512), BF16),
            pltpu.VMEM((1024, 512), BF16),
            pltpu.VMEM((1024, 512), BF16),
            dma((5,)),
            dma((4,)),
            dma((48,)),
            dma((48,)),
        ],
        compiler_params=pltpu.CompilerParams(
            collective_id=0, has_side_effects=True, vmem_limit_bytes=32 << 20
        ),
    )(*[
        pltpu.with_memory_space_constraint(a, pltpu.HBM)
        for a in (
            charges,
            counts,
            basis_t,
            far_t,
            far_source.reshape(1, 512),
            far_target.reshape(1, 512),
        )
    ])
    nacc = pl.pallas_call(
        local_kernel,
        name="local",
        out_shape=jax.ShapeDtypeStruct((8, 4, 16, 16, 128), F32),
        in_specs=[smem, smem, vmem(), vmem()],
        out_specs=vmem(),
        compiler_params=pltpu.CompilerParams(vmem_limit_bytes=24 << 20),
    )(near_first, near_second, near_tiles, X)
    chunk = (16, 16, 128)
    half = (8, 16, 128)
    return pl.pallas_call(
        reduce_kernel,
        name="reduce",
        out_shape=jax.ShapeDtypeStruct((16, 2048), F32),
        in_specs=[vmem(), vmem(), vmem(), vmem(), smem, vmem(), vmem()],
        out_specs=vmem(),
        scratch_shapes=[
            pltpu.VMEM((3, 4) + chunk, F32),
            pltpu.VMEM((4, 4) + chunk, F32),
            pltpu.VMEM((4,) + half, F32),
            pltpu.VMEM((4,) + half, F32),
            pltpu.VMEM((4,) + chunk, F32),
            pltpu.VMEM((4,) + chunk, F32),
            pltpu.VMEM((4,) + chunk, F32),
            pltpu.VMEM(chunk, F32),
            pltpu.VMEM(chunk, F32),
            pltpu.VMEM(chunk, F32),
            pltpu.VMEM((4, 4, 16, 1024), F32),
            pltpu.VMEM((4, 4, 16, 1024), F32),
            pltpu.VMEM((2, 16, 1024), F32),
            pltpu.VMEM((2, 16, 1024), F32),
            pltpu.VMEM((4, 16, 1024), F32),
            pltpu.VMEM((4, 16, 1024), F32),
            pltpu.VMEM((4, 16, 1024), F32),
            pltpu.VMEM((16, 512), F32),
            pltpu.VMEM((16, 512), F32),
            pltpu.VMEM((16, 1024), F32),
            pltpu.VMEM((16, 1024), F32),
            dma((32,)),
            dma((32,)),
        ],
        compiler_params=pltpu.CompilerParams(
            collective_id=1, has_side_effects=True, vmem_limit_bytes=36 << 20
        ),
    )(nacc, S.reshape(4, 4, 2, 16, 1024), out1, charges, counts, self_tiles, basis_t)


def solution(mesh):
    in_specs = (
        P("rhs", "blk"),
        P("blk"),
        P("blk", None, None),
        P("blk", None, None),
        P("blk"),
        P("blk"),
        P(("blk", "rhs"), None, None),
        P("blk"),
        P("blk"),
        P("blk", None, None),
    )
    return jax.shard_map(
        body, mesh=mesh, in_specs=in_specs, out_specs=P("rhs", "blk"), check_vma=False
    )
```

```python
import functools

import jax
import jax.numpy as jnp
from jax import lax
from jax.experimental import pallas as pl
from jax.experimental.pallas import tpu as pltpu
from jax.sharding import PartitionSpec as P

MESH = pl.DeviceIdType.MESH
F32 = jnp.float32
BF16 = jnp.bfloat16
NT = (((1,), (1,)), ((), ()))
TN = (((0,), (0,)), ((), ()))


class Place:
    def __init__(self):
        self.o = lax.axis_index("blk")
        self.x = lax.axis_index("rhs")
        self.k = self.o % 2
        self.c = self.o // 2
        self.y = self.c % 4
        self.z = self.c // 4
        self.xp = (self.x + 1) % 4
        self.xm = (self.x + 3) % 4
        self.xo = (self.x + 2) % 4
        self.yp = (self.y + 1) % 4
        self.ym = (self.y + 3) % 4
        self.yo = (self.y + 2) % 4
        self.zp = (self.z + 1) % 4
        self.zm = (self.z + 3) % 4
        self.zo = (self.z + 2) % 4
        self.sib = self.dev(self.c, 1 - self.k)
        self.east = {"blk": self.o, "rhs": self.xp}
        self.west = {"blk": self.o, "rhs": self.xm}
        self.cp = (self.c + 1) % 16
        self.cm = (self.c + 15) % 16
        self.up = self.dev(self.cp, self.k)
        self.down = self.dev(self.cm, self.k)
        self.up_other = self.dev(self.cp, 1 - self.k)
        self.down_other = self.dev(self.cm, 1 - self.k)
        self.y_plus = self.dev(self.z * 4 + self.yp, self.k)
        self.y_minus = self.dev(self.z * 4 + self.ym, self.k)
        self.z_plus = self.dev(self.zp * 4 + self.y, self.k)
        self.z_minus = self.dev(self.zm * 4 + self.y, self.k)
        self.far_chip = self.dev((self.c + 15 + 2 * self.k) % 16, 1 - self.k)

    def dev(self, chip, core):
        return {"blk": chip * 2 + core, "rhs": self.x}

    def greet(self):
        self.barrier = pltpu.get_barrier_semaphore()
        self.peers = [
            self.sib,
            self.east,
            self.west,
            self.up,
            self.down,
            self.up_other,
            self.down_other,
            self.y_plus,
            self.y_minus,
            self.z_plus,
            self.z_minus,
        ]
        for peer in self.peers:
            pl.semaphore_signal(self.barrier, inc=1, device_id=peer, device_id_type=MESH)

    def met(self):
        pl.semaphore_wait(self.barrier, len(self.peers))


class Sender:
    def __init__(self, send_sems, recv_sems):
        self.send_sems, self.recv_sems, self.n, self.out = send_sems, recv_sems, 0, []

    def copy(self, src, dst, peer):
        at = self.n
        self.n += 1
        made = pltpu.make_async_remote_copy(
            src_ref=src,
            dst_ref=dst,
            send_sem=self.send_sems.at[at],
            recv_sem=self.recv_sems.at[at],
            device_id=peer,
            device_id_type=MESH,
        )
        made.start()
        self.out.append(made)
        return made

    def drain(self):
        for made in self.out:
            made.wait_send()


TG = 2
TQ = 16 // TG
NJ = 4


def gather_kernel(
    charges, counts, basis_t, far, fs, ft, X, S, Mt, tm, ohs, perm, mqb,
    nbuf, qbuf, bbuf, ibuf, own, mq, tin, mgb, yhi, ylo, zhi, zlo,
    in_sem, tin_sem, ss, rs,
):
    p = Place()
    x, k = p.x, p.k
    p.greet()
    small = [
        pltpu.make_async_copy(charges, qbuf, in_sem.at[0]),
        pltpu.make_async_copy(basis_t, bbuf, in_sem.at[1]),
        pltpu.make_async_copy(counts, nbuf, in_sem.at[2]),
        pltpu.make_async_copy(fs, ibuf.at[0], in_sem.at[3]),
        pltpu.make_async_copy(ft, ibuf.at[1], in_sem.at[4]),
    ]
    loads = [
        pltpu.make_async_copy(far.at[pl.ds(i * 16, 16)], tin.at[pl.ds(i * 16, 16)], tin_sem.at[i])
        for i in range(4)
    ]
    for load in small + loads:
        load.start()
    for load in small[:3]:
        load.wait()
    lane = lax.broadcasted_iota(jnp.int32, (16, 128), 1)
    for b in range(16):
        block = qbuf[:, b * 128 : (b + 1) * 128]
        own[b] = jnp.where(lane < nbuf[b], block.astype(F32), 0.0).astype(BF16)
    X[3 + k, x] = own[...]
    p.met()
    s = Sender(ss, rs)
    sib = []
    farsib = []
    me = X.at[3 + k, x]

    def ring_start(u):
        src = X.at[u, x]
        return s.copy(src, X.at[u, x], p.east), s.copy(src, X.at[u, x], p.west)

    def arrived(pair):
        for made in pair:
            made.wait_recv()

    def ring_relay(u, pair):
        arrived(pair)
        made = (
            s.copy(X.at[u, p.xm, pl.ds(0, 8)], X.at[u, p.xm, pl.ds(0, 8)], p.east),
            s.copy(X.at[u, p.xp, pl.ds(8, 8)], X.at[u, p.xp, pl.ds(8, 8)], p.west),
        )
        if u is not edge:
            to_sib(u, p.xm)
            to_sib(u, p.xp)
        return made

    def to_sib(u, at):
        sib.append(s.copy(X.at[u, at], X.at[u, at], p.sib))

    u0, u1, u2, u3 = 7 * k, 1 + k, 3 + k, 5 + k
    edge = u0
    to_up = s.copy(me, X.at[u1, x], p.up)
    to_down = s.copy(me, X.at[u3, x], p.down)
    ring2 = ring_start(u2)

    moments = []
    for b in range(16):
        m = lax.dot_general(own[b], bbuf[b], NT, preferred_element_type=F32).astype(BF16)
        moments.append(m.astype(F32))
    rows = jnp.swapaxes(jnp.stack(moments, axis=0), 0, 1)
    Mt[p.z, p.y, k] = jnp.concatenate([rows[r] for r in range(16)], axis=-1).astype(BF16)
    mine = Mt.at[p.z, p.y, k]
    far_y = (s.copy(mine, mine, p.y_plus), s.copy(mine, mine, p.y_minus))
    to_sib(u2, x)

    for a in range(TQ):
        mq[a * 16 : (a + 1) * 16, :] = jnp.concatenate(
            [moments[g * TQ + a] for g in range(TG)], axis=-1
        ).astype(BF16)
    row = lax.broadcasted_iota(jnp.int32, (256, 256), 0)
    col = lax.broadcasted_iota(jnp.int32, (256, 256), 1)
    swap = ((row >> 4) == (col & 15)) & ((row & 15) == (col >> 4))
    perm[...] = jnp.where(swap, 1.0, 0.0).astype(BF16)
    small[3].wait()
    small[4].wait()
    tl = ibuf[1] - p.o * 16
    tg = tl // TQ
    tq = tl - tg * TQ
    ohs[...] = jnp.where(
        lax.broadcasted_iota(jnp.int32, (512, 512), 0) == ibuf[0], 1.0, 0.0
    ).astype(BF16)
    for g in range(TG):
        mgb[g] = jnp.broadcast_to(jnp.where(tg == g, 1.0, 0.0).astype(BF16), (16, 512))
    for g in range(TQ):
        mqb[g] = jnp.broadcast_to(jnp.where(tq == g, 1.0, 0.0).astype(BF16), (16, 512))

    def relayout(i):
        loads[i].wait()

        @pl.loop(0, 4)
        def _(n):
            at = pl.ds(pl.multiple_of(n * 16, 16), 16)
            block = tin[i * 16 : (i + 1) * 16, at, :].reshape(256, 512)
            moved = jnp.dot(perm[...], block, preferred_element_type=F32).astype(BF16)
            moved = moved.reshape(16, 16, 512)
            for g in range(TG):
                tm[at, g * 64 + i * 16 : g * 64 + (i + 1) * 16, :] = moved * mgb[g][None]

    def to_sources(first, last):
        @pl.loop(first, last)
        def _(n):
            for a in range(NJ):
                j = n * NJ + a
                yj = jnp.dot(mq[...], tm[j], preferred_element_type=F32)
                y = jnp.where(tq == 0, yj[0:16], 0.0)
                for g in range(1, TQ):
                    y = jnp.where(tq == g, yj[g * 16 : (g + 1) * 16], y)
                hi = y.astype(BF16)
                at = pl.ds(pl.multiple_of(j * 16, 16), 16)
                yhi[at, :] = hi
                ylo[at, :] = (y - hi.astype(F32)).astype(BF16)

    relayout(0)
    relayout(1)
    arrived((to_up, to_down))
    two = s.copy(X.at[5 - 3 * k, x], X.at[7 - 7 * k, x], p.far_chip)
    ring1 = ring_start(u1)
    ring3 = ring_start(u3)
    to_sib(u1, x)
    to_sib(u3, x)
    arrived(far_y)
    low, high = pl.ds(0, 512), pl.ds(512, 512)
    far_y2 = (
        s.copy(Mt.at[p.z, p.ym, k, :, low], Mt.at[p.z, p.ym, k, :, low], p.y_plus),
        s.copy(Mt.at[p.z, p.yp, k, :, high], Mt.at[p.z, p.yp, k, :, high], p.y_minus),
    )
    relayout(2)
    relay2 = ring_relay(u2, ring2)
    relayout(3)
    to_sources(0, 2)
    arrived(far_y2)
    plane = Mt.at[p.z, :, k]
    far_z = s.copy(plane, plane, p.z_plus), s.copy(plane, plane, p.z_minus)
    farsib.append(s.copy(plane, plane, p.sib))
    two.wait_recv()
    ring0 = ring_start(u0)
    to_sources(2, 5)
    relay1 = ring_relay(u1, ring1)
    to_sources(5, 7)
    relay3 = ring_relay(u3, ring3)
    to_sources(7, 10)
    arrived(far_z)
    after, before = Mt.at[p.zm, pl.ds(0, 2), k], Mt.at[p.zp, pl.ds(2, 2), k]
    far_z2 = s.copy(after, after, p.z_plus), s.copy(before, before, p.z_minus)
    for z in (p.zm, p.zp):
        farsib.append(s.copy(Mt.at[z, :, k], Mt.at[z, :, k], p.sib))
    to_sources(10, 13)
    arrived(relay2)
    to_sib(u2, p.xo)
    relay0 = ring_relay(u0, ring0)
    to_sources(13, 16)
    arrived(far_z2)
    farsib.append(s.copy(Mt.at[p.zo, :, k], Mt.at[p.zo, :, k], p.sib))
    for h in range(4):
        for src, dst in ((yhi, zhi), (ylo, zlo)):
            moved = jnp.dot(
                perm[...], src[h * 256 : (h + 1) * 256, :], preferred_element_type=F32
            ).astype(BF16)
            for r in range(16):
                dst[r * 64 + h * 16 : r * 64 + (h + 1) * 16, :] = moved[r * 16 : (r + 1) * 16]
    arrived(relay1)
    to_sib(u1, p.xo)
    for h in range(4):
        at = slice(h * 256, (h + 1) * 256)
        S[:, at] = lax.dot_general(
            ohs[...], zhi[at, :], NT, preferred_element_type=F32
        ) + lax.dot_general(ohs[...], zlo[at, :], NT, preferred_element_type=F32)
    arrived(relay3)
    to_sib(u3, p.xo)
    arrived(farsib)

    arrived(relay0)
    arrived(sib)
    s.drain()


def local_kernel(nf, ns, tiles, X, nacc):
    o = lax.axis_index("blk")
    k = o % 2
    base = lax.axis_index("rhs") * 128
    nacc[...] = jnp.zeros_like(nacc)

    @pl.loop(0, 128, unroll=8)
    def _(n):
        a = nf[base + n] - o * 16
        d = lax.rem(ns[base + n] - o * 16 + 560, 512)
        ub, bb = d // 16 + k, lax.rem(d, 16)
        ua = 3 + k
        tile = tiles[n]
        xb = X[ub, :, bb].reshape(64, 128)
        xa = X[ua, :, a].reshape(64, 128)
        to_first = lax.dot_general(xb, tile, NT, preferred_element_type=F32)
        to_second = jnp.dot(xa, tile, preferred_element_type=F32)
        nacc[ua, :, a] += to_first.reshape(4, 16, 128)
        nacc[ub, :, bb] += to_second.reshape(4, 16, 128)


class Wire:
    def __init__(self, sender, scs, scr):
        self.sender, self.scs, self.scr, self.n = sender, scs, scr, 0

    def send(self, value, src, dst, peer):
        at = self.n
        self.n += 1
        lanes = value.shape[-1] // 128
        most = jnp.full((8, 128), 1e-30, F32)
        for w in range(lanes):
            top = jnp.max(jnp.abs(value[:, :, w * 128 : (w + 1) * 128]), axis=0)
            most = jnp.maximum(most, jnp.maximum(top[:8], top[8:]))
        self.scs[at] = most * (1.0 / 32000.0)
        src[...] = jnp.round(value * self.tile(32000.0 / most, lanes)).astype(jnp.int32).astype(jnp.int16)
        made = (
            self.sender.copy(self.scs.at[at], self.scr.at[at], peer),
            self.sender.copy(src, dst, peer),
        )
        return made, dst, at

    def tile(self, scale, lanes):
        both = jnp.concatenate([scale, scale], axis=0)
        return jnp.concatenate([both] * lanes, axis=1)[None]

    def take(self, sent):
        made, dst, at = sent
        made[0].wait_recv()
        made[1].wait_recv()
        value = dst[...].astype(jnp.int32).astype(F32)
        return value * self.tile(self.scr[at], value.shape[-1] // 128)


def reduce_kernel(
    nacc, S, Mt, tm, ohs, perm, mqb, charges, counts, self_tiles, basis_t, out,
    R, C, V, RF, CF, W, hs, hr, ws, wr, z2s, z2r, z1s, z1r, y2s, y2r, y1s, y1r, scs, scr,
    out1, gtmp, gj, ss, rs,
):
    p = Place()
    x, k = p.x, p.k
    p.greet()
    C[0] = nacc[7 * k]
    p.met()
    s = Sender(ss, rs)
    wire = Wire(s, scs, scr)
    near_sib = [s.copy(nacc.at[2 - k + 2 * i], R.at[i], p.sib) for i in range(3)]
    far_sib = s.copy(S.at[:, :, 1 - k], RF, p.sib)
    own = 1 + k
    two = []
    ring = []

    def first(i):
        two.append(
            (
                wire.send(C[i, p.xo, pl.ds(0, 8)], hs.at[2 * i], hr.at[2 * i], p.east),
                wire.send(C[i, p.xo, pl.ds(8, 8)], hs.at[2 * i + 1], hr.at[2 * i + 1], p.west),
            )
        )

    def second(i):
        C[i, p.xp, pl.ds(0, 8)] += wire.take(two[i][0])
        C[i, p.xm, pl.ds(8, 8)] += wire.take(two[i][1])
        ring.append(
            (
                wire.send(C[i, p.xp], ws.at[2 * i], wr.at[2 * i], p.east),
                wire.send(C[i, p.xm], ws.at[2 * i + 1], wr.at[2 * i + 1], p.west),
            )
        )

    def third(i):
        V[i] = C[i, x] + wire.take(ring[i][0]) + wire.take(ring[i][1])

    def source_moments(half):
        for h in (2 * half, 2 * half + 1):
            table = Mt[:, :, :, :, h * 256 : (h + 1) * 256].reshape(512, 256)
            gtmp[h * 256 : (h + 1) * 256, :] = lax.dot_general(
                table, ohs[...], TN, preferred_element_type=F32
            ).astype(BF16)

    def reorder():
        for h in range(4):
            block = jnp.concatenate(
                [gtmp[r * 64 + h * 16 : r * 64 + (h + 1) * 16, :] for r in range(16)], axis=0
            )
            gj[h * 256 : (h + 1) * 256, :] = jnp.dot(
                perm[...], block, preferred_element_type=F32
            ).astype(BF16)

    def to_targets(first, last):
        @pl.loop(first, last)
        def _(n):
            total = out1[...]
            for a in range(NJ):
                j = n * NJ + a
                ms = gj[pl.ds(pl.multiple_of(j * 16, 16), 16), :]
                zj = (ms[None] * mqb[...]).reshape(TQ * 16, 512)
                total = total + lax.dot_general(zj, tm[j], NT, preferred_element_type=F32)
            out1[...] = total

    first(0)
    for i in range(3):
        near_sib[i].wait_recv()
        C[i + 1] = nacc[own + 2 * i] + R[i]
        first(i + 1)
    far_sib.wait_recv()
    CF[...] = S[:, :, k] + RF[...]
    fz2 = (
        wire.send(CF[p.zo, pl.ds(0, 2)], z2s.at[0], z2r.at[0], p.z_plus),
        wire.send(CF[p.zo, pl.ds(2, 2)], z2s.at[1], z2r.at[1], p.z_minus),
    )
    out1[...] = jnp.zeros_like(out1)
    second(0)
    second(1)
    source_moments(0)
    second(2)
    second(3)
    CF[p.zp, pl.ds(0, 2)] += wire.take(fz2[0])
    CF[p.zm, pl.ds(2, 2)] += wire.take(fz2[1])
    fz = (
        wire.send(CF[p.zp], z1s.at[0], z1r.at[0], p.z_plus),
        wire.send(CF[p.zm], z1s.at[1], z1r.at[1], p.z_minus),
    )
    source_moments(1)
    third(0)
    relay = wire.send(V[0], ws.at[8], wr.at[8], p.far_chip)
    reorder()
    third(1)
    third(3)
    to_targets(0, 4)
    W[...] = CF[p.z] + wire.take(fz[0]) + wire.take(fz[1])
    fy2 = (
        wire.send(W[pl.ds(p.yo, 1), :, pl.ds(0, 512)], y2s.at[0], y2r.at[0], p.y_plus),
        wire.send(W[pl.ds(p.yo, 1), :, pl.ds(512, 512)], y2s.at[1], y2r.at[1], p.y_minus),
    )
    V[3 - 2 * k] += wire.take(relay)
    near_last = (
        wire.send(V[1], ws.at[9], wr.at[9], p.down),
        wire.send(V[3], ws.at[10], wr.at[10], p.up),
    )
    third(2)
    to_targets(4, 7)
    W[pl.ds(p.yp, 1), :, pl.ds(0, 512)] += wire.take(fy2[0])
    W[pl.ds(p.ym, 1), :, pl.ds(512, 512)] += wire.take(fy2[1])
    fy = (
        wire.send(W[pl.ds(p.yp, 1)], y1s.at[0], y1r.at[0], p.y_plus),
        wire.send(W[pl.ds(p.ym, 1)], y1s.at[1], y1r.at[1], p.y_minus),
    )
    to_targets(7, 16)
    lane = lax.broadcasted_iota(jnp.int32, (16, 128), 1)
    for b in range(16):
        part = charges[:, b * 128 : (b + 1) * 128]
        part = jnp.where(lane < counts[b], part.astype(F32), 0.0).astype(BF16)
        out[:, b * 128 : (b + 1) * 128] = lax.dot_general(
            part, self_tiles[b], NT, preferred_element_type=F32
        )
    V[2] += wire.take(near_last[0]) + wire.take(near_last[1])
    flat = (W[pl.ds(p.y, 1)] + wire.take(fy[0]) + wire.take(fy[1]))[0]
    rows = jnp.stack([flat[:, r * 64 : (r + 1) * 64] for r in range(16)], axis=0)
    rows = jnp.swapaxes(rows, 0, 1)
    for b in range(16):
        own1 = out1[b % TQ * 16 : b % TQ * 16 + 16, b // TQ * 64 : b // TQ * 64 + 64]
        fields = (rows[b] + own1).astype(BF16)
        far_part = jnp.dot(fields, basis_t[b], preferred_element_type=F32)
        cols = slice(b * 128, (b + 1) * 128)
        out[:, cols] = jnp.where(lane < counts[b], out[:, cols] + V[2, b] + far_part, 0.0)
    s.drain()


def vmem():
    return pl.BlockSpec(memory_space=pltpu.VMEM)


def body(
    charges, counts, self_tiles, basis, near_first, near_second, near_tiles, far_source, far_target, far_tiles
):
    basis_t = jnp.transpose(basis, (0, 2, 1))
    far_t = jnp.transpose(far_tiles, (1, 2, 0))
    smem = pl.BlockSpec(memory_space=pltpu.SMEM)
    hbm = pl.BlockSpec(memory_space=pltpu.HBM)
    dma = pltpu.SemaphoreType.DMA
    X, S, Mt, tm, ohs, perm, mqb = pl.pallas_call(
        gather_kernel,
        name="gather",
        out_shape=(
            jax.ShapeDtypeStruct((8, 4, 16, 16, 128), BF16),
            jax.ShapeDtypeStruct((512, 1024), F32),
            jax.ShapeDtypeStruct((4, 4, 2, 16, 1024), BF16),
            jax.ShapeDtypeStruct((64, TG * 64, 512), BF16),
            jax.ShapeDtypeStruct((512, 512), BF16),
            jax.ShapeDtypeStruct((256, 256), BF16),
            jax.ShapeDtypeStruct((TQ, 16, 512), BF16),
        ),
        in_specs=[hbm] * 6,
        out_specs=(vmem(),) * 7,
        scratch_shapes=[
            pltpu.SMEM((16,), jnp.int32),
            pltpu.VMEM((16, 2048), BF16),
            pltpu.VMEM((16, 64, 128), BF16),
            pltpu.VMEM((2, 1, 512), jnp.int32),
            pltpu.VMEM((16, 16, 128), BF16),
            pltpu.VMEM((TQ * 16, TG * 64), BF16),
            pltpu.VMEM((64, 64, 512), BF16),
            pltpu.VMEM((TG, 16, 512), BF16),
            pltpu.VMEM((1024, 512), BF16),
            pltpu.VMEM((1024, 512), BF16),
            pltpu.VMEM((1024, 512), BF16),
            pltpu.VMEM((1024, 512), BF16),
            dma((5,)),
            dma((4,)),
            dma((48,)),
            dma((48,)),
        ],
        compiler_params=pltpu.CompilerParams(
            collective_id=0, has_side_effects=True, vmem_limit_bytes=32 << 20
        ),
    )(*[
        pltpu.with_memory_space_constraint(a, pltpu.HBM)
        for a in (
            charges,
            counts,
            basis_t,
            far_t,
            far_source.reshape(1, 512),
            far_target.reshape(1, 512),
        )
    ])
    nacc = pl.pallas_call(
        local_kernel,
        name="local",
        out_shape=jax.ShapeDtypeStruct((8, 4, 16, 16, 128), F32),
        in_specs=[smem, smem, vmem(), vmem()],
        out_specs=vmem(),
        compiler_params=pltpu.CompilerParams(vmem_limit_bytes=24 << 20),
    )(near_first, near_second, near_tiles, X)
    chunk = (16, 16, 128)
    half = (8, 16, 128)
    i16 = jnp.int16
    return pl.pallas_call(
        reduce_kernel,
        name="reduce",
        out_shape=jax.ShapeDtypeStruct((16, 2048), F32),
        in_specs=[vmem()] * 8 + [smem, vmem(), vmem()],
        out_specs=vmem(),
        scratch_shapes=[
            pltpu.VMEM((3, 4) + chunk, F32),
            pltpu.VMEM((4, 4) + chunk, F32),
            pltpu.VMEM((4,) + chunk, F32),
            pltpu.VMEM((4, 4, 16, 1024), F32),
            pltpu.VMEM((4, 4, 16, 1024), F32),
            pltpu.VMEM((4, 16, 1024), F32),
            pltpu.VMEM((8,) + half, i16),
            pltpu.VMEM((8,) + half, i16),
            pltpu.VMEM((11,) + chunk, i16),
            pltpu.VMEM((11,) + chunk, i16),
            pltpu.VMEM((2, 2, 16, 1024), i16),
            pltpu.VMEM((2, 2, 16, 1024), i16),
            pltpu.VMEM((2, 4, 16, 1024), i16),
            pltpu.VMEM((2, 4, 16, 1024), i16),
            pltpu.VMEM((2, 1, 16, 512), i16),
            pltpu.VMEM((2, 1, 16, 512), i16),
            pltpu.VMEM((2, 1, 16, 1024), i16),
            pltpu.VMEM((2, 1, 16, 1024), i16),
            pltpu.VMEM((27, 8, 128), F32),
            pltpu.VMEM((27, 8, 128), F32),
            pltpu.VMEM((TQ * 16, TG * 64), F32),
            pltpu.VMEM((1024, 512), BF16),
            pltpu.VMEM((1024, 512), BF16),
            dma((58,)),
            dma((58,)),
        ],
        compiler_params=pltpu.CompilerParams(
            collective_id=1, has_side_effects=True, vmem_limit_bytes=28 << 20
        ),
    )(
        nacc, S.reshape(4, 4, 2, 16, 1024), Mt, tm, ohs, perm, mqb, charges, counts, self_tiles, basis_t
    )


def solution(mesh):
    in_specs = (
        P("rhs", "blk"),
        P("blk"),
        P("blk", None, None),
        P("blk", None, None),
        P("blk"),
        P("blk"),
        P(("blk", "rhs"), None, None),
        P("blk"),
        P("blk"),
        P("blk", None, None),
    )
    return jax.shard_map(
        body, mesh=mesh, in_specs=in_specs, out_specs=P("rhs", "blk"), check_vma=False
    )
```

```python
import functools

import jax
import jax.numpy as jnp
from jax import lax
from jax.experimental import pallas as pl
from jax.experimental.pallas import tpu as pltpu
from jax.sharding import PartitionSpec as P

MESH = pl.DeviceIdType.MESH
F32 = jnp.float32
BF16 = jnp.bfloat16
NT = (((1,), (1,)), ((), ()))
TN = (((0,), (0,)), ((), ()))


class Place:
    def __init__(self):
        self.o = lax.axis_index("blk")
        self.x = lax.axis_index("rhs")
        self.k = self.o % 2
        self.c = self.o // 2
        self.y = self.c % 4
        self.z = self.c // 4
        self.xp = (self.x + 1) % 4
        self.xm = (self.x + 3) % 4
        self.xo = (self.x + 2) % 4
        self.yp = (self.y + 1) % 4
        self.ym = (self.y + 3) % 4
        self.yo = (self.y + 2) % 4
        self.zp = (self.z + 1) % 4
        self.zm = (self.z + 3) % 4
        self.zo = (self.z + 2) % 4
        self.sib = self.dev(self.c, 1 - self.k)
        self.east = {"blk": self.o, "rhs": self.xp}
        self.west = {"blk": self.o, "rhs": self.xm}
        self.cp = (self.c + 1) % 16
        self.cm = (self.c + 15) % 16
        self.up = self.dev(self.cp, self.k)
        self.down = self.dev(self.cm, self.k)
        self.up_other = self.dev(self.cp, 1 - self.k)
        self.down_other = self.dev(self.cm, 1 - self.k)
        self.y_plus = self.dev(self.z * 4 + self.yp, self.k)
        self.y_minus = self.dev(self.z * 4 + self.ym, self.k)
        self.z_plus = self.dev(self.zp * 4 + self.y, self.k)
        self.z_minus = self.dev(self.zm * 4 + self.y, self.k)
        self.near_relay = self.dev((self.c + 15 + 2 * self.k) % 16, self.k)
        self.near_away = self.dev((self.c + 1 + 14 * self.k) % 16, self.k)
        self.far_chip = self.dev((self.c + 15 + 2 * self.k) % 16, 1 - self.k)

    def dev(self, chip, core):
        return {"blk": chip * 2 + core, "rhs": self.x}

    def plane(self):
        return [((self.z + dz) % 4, (self.y + dy) % 4) for dz, dy in STEPS]

    def greet(self, whole_plane):
        self.barrier = pltpu.get_barrier_semaphore()
        self.peers = [
            self.sib,
            self.east,
            self.west,
            self.up,
            self.down,
            self.up_other,
            self.down_other,
        ]
        if whole_plane:
            self.peers += [self.dev(z * 4 + y, self.k) for z, y in self.plane()]
        else:
            self.peers += [self.y_plus, self.y_minus, self.z_plus, self.z_minus]
        for peer in self.peers:
            pl.semaphore_signal(self.barrier, inc=1, device_id=peer, device_id_type=MESH)

    def met(self):
        pl.semaphore_wait(self.barrier, len(self.peers))


class Sender:
    def __init__(self, send_sems, recv_sems):
        self.send_sems, self.recv_sems, self.n, self.out = send_sems, recv_sems, 0, []

    def copy(self, src, dst, peer):
        at = self.n
        self.n += 1
        made = pltpu.make_async_remote_copy(
            src_ref=src,
            dst_ref=dst,
            send_sem=self.send_sems.at[at],
            recv_sem=self.recv_sems.at[at],
            device_id=peer,
            device_id_type=MESH,
        )
        made.start()
        self.out.append(made)
        return made

    def drain(self):
        for made in self.out:
            made.wait_send()


TG = 2
TQ = 16 // TG
NJ = 4


STEPS = sorted(
    [(dz, dy) for dz in range(4) for dy in range(4) if dz or dy],
    key=lambda d: -(min(d[0], 4 - d[0]) + min(d[1], 4 - d[1])),
)


def gather_kernel(
    charges, counts, basis_t, far, fs, ft, X, CF, Mt, tm, ohs, perm, mqb,
    nbuf, qbuf, bbuf, ibuf, own, mq, tin, mgb, yhi, ylo, zhi, zlo, S, RF,
    in_sem, tin_sem, ss, rs,
):
    p = Place()
    x, k = p.x, p.k
    p.greet(True)
    small = [
        pltpu.make_async_copy(charges, qbuf, in_sem.at[0]),
        pltpu.make_async_copy(basis_t, bbuf, in_sem.at[1]),
        pltpu.make_async_copy(counts, nbuf, in_sem.at[2]),
        pltpu.make_async_copy(fs, ibuf.at[0], in_sem.at[3]),
        pltpu.make_async_copy(ft, ibuf.at[1], in_sem.at[4]),
    ]
    loads = [
        pltpu.make_async_copy(far.at[pl.ds(i * 16, 16)], tin.at[pl.ds(i * 16, 16)], tin_sem.at[i])
        for i in range(4)
    ]
    for load in small + loads:
        load.start()
    for load in small[:3]:
        load.wait()
    lane = lax.broadcasted_iota(jnp.int32, (16, 128), 1)
    for b in range(16):
        block = qbuf[:, b * 128 : (b + 1) * 128]
        own[b] = jnp.where(lane < nbuf[b], block.astype(F32), 0.0).astype(BF16)
    X[3 + k, x] = own[...]
    p.met()
    s = Sender(ss, rs)
    sib = []
    farsib = []
    me = X.at[3 + k, x]

    def ring_start(u):
        src = X.at[u, x]
        return s.copy(src, X.at[u, x], p.east), s.copy(src, X.at[u, x], p.west)

    def arrived(pair):
        for made in pair:
            made.wait_recv()

    def ring_relay(u, pair):
        arrived(pair)
        made = (
            s.copy(X.at[u, p.xm, pl.ds(0, 8)], X.at[u, p.xm, pl.ds(0, 8)], p.east),
            s.copy(X.at[u, p.xp, pl.ds(8, 8)], X.at[u, p.xp, pl.ds(8, 8)], p.west),
        )
        if u is not edge:
            to_sib(u, p.xm)
            to_sib(u, p.xp)
        return made

    def far_on(first, last):
        for at in range(first, last):
            dz, dy = STEPS[at]
            far_all[at].wait_recv()
            block = Mt.at[(p.z + 4 - dz) % 4, (p.y + 4 - dy) % 4, k]
            farsib.append(s.copy(block, block, p.sib))

    def to_sib(u, at):
        sib.append(s.copy(X.at[u, at], X.at[u, at], p.sib))

    u0, u1, u2, u3 = 7 * k, 1 + k, 3 + k, 5 + k
    edge = u0
    to_up = s.copy(me, X.at[u1, x], p.up)
    to_down = s.copy(me, X.at[u3, x], p.down)
    ring2 = ring_start(u2)

    moments = []
    for b in range(16):
        m = lax.dot_general(own[b], bbuf[b], NT, preferred_element_type=F32).astype(BF16)
        moments.append(m.astype(F32))
    rows = jnp.swapaxes(jnp.stack(moments, axis=0), 0, 1)
    Mt[p.z, p.y, k] = jnp.concatenate([rows[r] for r in range(16)], axis=-1).astype(BF16)
    mine = Mt.at[p.z, p.y, k]
    plane = p.plane()
    far_all = [s.copy(mine, mine, p.dev(z * 4 + y, k)) for z, y in plane]
    farsib.append(s.copy(mine, mine, p.sib))
    to_sib(u2, x)

    for a in range(TQ):
        mq[a * 16 : (a + 1) * 16, :] = jnp.concatenate(
            [moments[g * TQ + a] for g in range(TG)], axis=-1
        ).astype(BF16)
    row = lax.broadcasted_iota(jnp.int32, (256, 256), 0)
    col = lax.broadcasted_iota(jnp.int32, (256, 256), 1)
    swap = ((row >> 4) == (col & 15)) & ((row & 15) == (col >> 4))
    perm[...] = jnp.where(swap, 1.0, 0.0).astype(BF16)
    small[3].wait()
    small[4].wait()
    tl = ibuf[1] - p.o * 16
    tg = tl // TQ
    tq = tl - tg * TQ
    ohs[...] = jnp.where(
        lax.broadcasted_iota(jnp.int32, (512, 512), 0) == ibuf[0], 1.0, 0.0
    ).astype(BF16)
    for g in range(TG):
        mgb[g] = jnp.broadcast_to(jnp.where(tg == g, 1.0, 0.0).astype(BF16), (16, 512))
    for g in range(TQ):
        mqb[g] = jnp.broadcast_to(jnp.where(tq == g, 1.0, 0.0).astype(BF16), (16, 512))

    def relayout(i):
        loads[i].wait()

        @pl.loop(0, 4)
        def _(n):
            at = pl.ds(pl.multiple_of(n * 16, 16), 16)
            block = tin[i * 16 : (i + 1) * 16, at, :].reshape(256, 512)
            moved = jnp.dot(perm[...], block, preferred_element_type=F32).astype(BF16)
            moved = moved.reshape(16, 16, 512)
            for g in range(TG):
                tm[at, g * 64 + i * 16 : g * 64 + (i + 1) * 16, :] = moved * mgb[g][None]

    def to_sources(first, last):
        @pl.loop(first, last)
        def _(n):
            for a in range(NJ):
                j = n * NJ + a
                yj = jnp.dot(mq[...], tm[j], preferred_element_type=F32)
                y = jnp.where(tq == 0, yj[0:16], 0.0)
                for g in range(1, TQ):
                    y = jnp.where(tq == g, yj[g * 16 : (g + 1) * 16], y)
                hi = y.astype(BF16)
                at = pl.ds(pl.multiple_of(j * 16, 16), 16)
                yhi[at, :] = hi
                ylo[at, :] = (y - hi.astype(F32)).astype(BF16)

    relayout(0)
    relayout(1)
    arrived((to_up, to_down))
    two = s.copy(X.at[5 - 3 * k, x], X.at[7 - 7 * k, x], p.far_chip)
    ring1 = ring_start(u1)
    ring3 = ring_start(u3)
    to_sib(u1, x)
    to_sib(u3, x)
    relayout(2)
    relay2 = ring_relay(u2, ring2)
    relayout(3)
    to_sources(0, 2)
    two.wait_recv()
    ring0 = ring_start(u0)
    to_sources(2, 5)
    relay1 = ring_relay(u1, ring1)
    to_sources(5, 7)
    relay3 = ring_relay(u3, ring3)
    to_sources(7, 10)
    far_on(9, 15)
    to_sources(10, 13)
    arrived(relay2)
    to_sib(u2, p.xo)
    relay0 = ring_relay(u0, ring0)
    to_sources(13, 16)
    far_on(0, 9)
    for h in range(4):
        for src, dst in ((yhi, zhi), (ylo, zlo)):
            moved = jnp.dot(
                perm[...], src[h * 256 : (h + 1) * 256, :], preferred_element_type=F32
            ).astype(BF16)
            for r in range(16):
                dst[r * 64 + h * 16 : r * 64 + (h + 1) * 16, :] = moved[r * 16 : (r + 1) * 16]
    arrived(relay1)
    to_sib(u1, p.xo)
    for h in range(4):
        at = slice(h * 256, (h + 1) * 256)
        part = lax.dot_general(
            ohs[...], zhi[at, :], NT, preferred_element_type=F32
        ) + lax.dot_general(ohs[...], zlo[at, :], NT, preferred_element_type=F32)
        S[:, :, :, :, at] = part.reshape(4, 4, 2, 16, 256)
    sums = s.copy(S.at[:, :, 1 - k], RF, p.sib)
    arrived(relay3)
    to_sib(u3, p.xo)
    arrived(farsib)

    sums.wait_recv()
    CF[...] = S[:, :, k] + RF[...]
    arrived(relay0)
    arrived(sib)
    s.drain()


def local_kernel(nf, ns, tiles, X, nacc):
    o = lax.axis_index("blk")
    k = o % 2
    base = lax.axis_index("rhs") * 128
    nacc[...] = jnp.zeros_like(nacc)

    @pl.loop(0, 128, unroll=8)
    def _(n):
        a = nf[base + n] - o * 16
        d = lax.rem(ns[base + n] - o * 16 + 560, 512)
        ub, bb = d // 16 + k, lax.rem(d, 16)
        ua = 3 + k
        tile = tiles[n]
        xb = X[ub, :, bb].reshape(64, 128)
        xa = X[ua, :, a].reshape(64, 128)
        to_first = lax.dot_general(xb, tile, NT, preferred_element_type=F32)
        to_second = jnp.dot(xa, tile, preferred_element_type=F32)
        nacc[ua, :, a] += to_first.reshape(4, 16, 128)
        nacc[ub, :, bb] += to_second.reshape(4, 16, 128)


class Wire:
    def __init__(self, sender, scs, scr):
        self.sender, self.scs, self.scr, self.n = sender, scs, scr, 0

    def send(self, value, src, dst, peer):
        at = self.n
        self.n += 1
        lanes = value.shape[-1] // 128
        most = jnp.full((8, 128), 1e-30, F32)
        for w in range(lanes):
            top = jnp.max(jnp.abs(value[:, :, w * 128 : (w + 1) * 128]), axis=0)
            most = jnp.maximum(most, jnp.maximum(top[:8], top[8:]))
        self.scs[at] = most * (1.0 / 32000.0)
        src[...] = jnp.round(value * self.tile(32000.0 / most, lanes)).astype(jnp.int32).astype(jnp.int16)
        made = (
            self.sender.copy(self.scs.at[at], self.scr.at[at], peer),
            self.sender.copy(src, dst, peer),
        )
        return made, dst, at

    def tile(self, scale, lanes):
        both = jnp.concatenate([scale, scale], axis=0)
        return jnp.concatenate([both] * lanes, axis=1)[None]

    def take(self, sent):
        made, dst, at = sent
        made[0].wait_recv()
        made[1].wait_recv()
        value = dst[...].astype(jnp.int32).astype(F32)
        return value * self.tile(self.scr[at], value.shape[-1] // 128)


def reduce_kernel(
    nacc, CF, Mt, tm, ohs, perm, mqb, charges, counts, self_tiles, basis_t, out,
    R, C, V, W, hs, hr, ws, wr, z2s, z2r, z1s, z1r, y2s, y2r, y1s, y1r, scs, scr,
    out1, gtmp, gj, ss, rs,
):
    p = Place()
    x, k = p.x, p.k
    p.greet(False)
    C[0] = nacc[7 * k]
    p.met()
    s = Sender(ss, rs)
    wire = Wire(s, scs, scr)
    near_sib = [
        s.copy(nacc.at[u], R.at[i], p.sib) for i, u in enumerate((6 - 5 * k, 2 + 3 * k, 4 - k))
    ]
    two = {}
    ring = {}

    def first(i):
        two[i] = (
            wire.send(C[i, p.xo, pl.ds(0, 8)], hs.at[2 * i], hr.at[2 * i], p.east),
            wire.send(C[i, p.xo, pl.ds(8, 8)], hs.at[2 * i + 1], hr.at[2 * i + 1], p.west),
        )

    def second(i):
        C[i, p.xp, pl.ds(0, 8)] += wire.take(two[i][0])
        C[i, p.xm, pl.ds(8, 8)] += wire.take(two[i][1])
        ring[i] = (
            wire.send(C[i, p.xp], ws.at[2 * i], wr.at[2 * i], p.east),
            wire.send(C[i, p.xm], ws.at[2 * i + 1], wr.at[2 * i + 1], p.west),
        )

    def third(i):
        V[i] = C[i, x] + wire.take(ring[i][0]) + wire.take(ring[i][1])

    def source_moments(half):
        for h in (2 * half, 2 * half + 1):
            table = Mt[:, :, :, :, h * 256 : (h + 1) * 256].reshape(512, 256)
            gtmp[h * 256 : (h + 1) * 256, :] = lax.dot_general(
                table, ohs[...], TN, preferred_element_type=F32
            ).astype(BF16)

    def reorder():
        for h in range(4):
            block = jnp.concatenate(
                [gtmp[r * 64 + h * 16 : r * 64 + (h + 1) * 16, :] for r in range(16)], axis=0
            )
            gj[h * 256 : (h + 1) * 256, :] = jnp.dot(
                perm[...], block, preferred_element_type=F32
            ).astype(BF16)

    def to_targets(first, last):
        @pl.loop(first, last)
        def _(n):
            total = out1[...]
            for a in range(NJ):
                j = n * NJ + a
                ms = gj[pl.ds(pl.multiple_of(j * 16, 16), 16), :]
                zj = (ms[None] * mqb[...]).reshape(TQ * 16, 512)
                total = total + lax.dot_general(zj, tm[j], NT, preferred_element_type=F32)
            out1[...] = total

    first(0)
    fz2 = (
        wire.send(CF[p.zo, pl.ds(0, 2)], z2s.at[0], z2r.at[0], p.z_plus),
        wire.send(CF[p.zo, pl.ds(2, 2)], z2s.at[1], z2r.at[1], p.z_minus),
    )
    for i, (slot, u) in enumerate(((1, 1 + 5 * k), (3, 5 - 3 * k), (2, 3 + k))):
        near_sib[i].wait_recv()
        C[slot] = nacc[u] + R[i]
        first(slot)
    out1[...] = jnp.zeros_like(out1)
    second(0)
    z_up = CF[p.zp]
    z_down = CF[p.zm]
    fz = (
        wire.send(
            jnp.concatenate([z_up[:2] + wire.take(fz2[0]), z_up[2:]], axis=0),
            z1s.at[0],
            z1r.at[0],
            p.z_plus,
        ),
        wire.send(
            jnp.concatenate([z_down[:2], z_down[2:] + wire.take(fz2[1])], axis=0),
            z1s.at[1],
            z1r.at[1],
            p.z_minus,
        ),
    )
    second(1)
    second(3)
    source_moments(0)
    second(2)
    third(0)
    relay = wire.send(V[0], ws.at[8], wr.at[8], p.far_chip)
    source_moments(1)
    W[...] = CF[p.z] + wire.take(fz[0]) + wire.take(fz[1])
    fy2 = (
        wire.send(W[pl.ds(p.yo, 1), :, pl.ds(0, 512)], y2s.at[0], y2r.at[0], p.y_plus),
        wire.send(W[pl.ds(p.yo, 1), :, pl.ds(512, 512)], y2s.at[1], y2r.at[1], p.y_minus),
    )
    third(1)
    near_last = [wire.send(V[1], ws.at[9], wr.at[9], p.near_relay)]
    reorder()
    third(3)
    V[3] += wire.take(relay)
    near_last.append(wire.send(V[3], ws.at[10], wr.at[10], p.near_away))
    W[pl.ds(p.yp, 1), :, pl.ds(0, 512)] += wire.take(fy2[0])
    W[pl.ds(p.ym, 1), :, pl.ds(512, 512)] += wire.take(fy2[1])
    fy = (
        wire.send(W[pl.ds(p.yp, 1)], y1s.at[0], y1r.at[0], p.y_plus),
        wire.send(W[pl.ds(p.ym, 1)], y1s.at[1], y1r.at[1], p.y_minus),
    )
    to_targets(0, 8)
    third(2)
    to_targets(8, 16)
    lane = lax.broadcasted_iota(jnp.int32, (16, 128), 1)
    for b in range(16):
        part = charges[:, b * 128 : (b + 1) * 128]
        part = jnp.where(lane < counts[b], part.astype(F32), 0.0).astype(BF16)
        out[:, b * 128 : (b + 1) * 128] = lax.dot_general(
            part, self_tiles[b], NT, preferred_element_type=F32
        )
    V[2] += wire.take(near_last[0]) + wire.take(near_last[1])
    flat = (W[pl.ds(p.y, 1)] + wire.take(fy[0]) + wire.take(fy[1]))[0]
    rows = jnp.stack([flat[:, r * 64 : (r + 1) * 64] for r in range(16)], axis=0)
    rows = jnp.swapaxes(rows, 0, 1)
    for b in range(16):
        own1 = out1[b % TQ * 16 : b % TQ * 16 + 16, b // TQ * 64 : b // TQ * 64 + 64]
        fields = (rows[b] + own1).astype(BF16)
        far_part = jnp.dot(fields, basis_t[b], preferred_element_type=F32)
        cols = slice(b * 128, (b + 1) * 128)
        out[:, cols] = jnp.where(lane < counts[b], out[:, cols] + V[2, b] + far_part, 0.0)
    s.drain()


def vmem():
    return pl.BlockSpec(memory_space=pltpu.VMEM)


def body(
    charges, counts, self_tiles, basis, near_first, near_second, near_tiles, far_source, far_target, far_tiles
):
    basis_t = jnp.transpose(basis, (0, 2, 1))
    far_t = jnp.transpose(far_tiles, (1, 2, 0))
    smem = pl.BlockSpec(memory_space=pltpu.SMEM)
    hbm = pl.BlockSpec(memory_space=pltpu.HBM)
    dma = pltpu.SemaphoreType.DMA
    X, CF, Mt, tm, ohs, perm, mqb = pl.pallas_call(
        gather_kernel,
        name="gather",
        out_shape=(
            jax.ShapeDtypeStruct((8, 4, 16, 16, 128), BF16),
            jax.ShapeDtypeStruct((4, 4, 16, 1024), F32),
            jax.ShapeDtypeStruct((4, 4, 2, 16, 1024), BF16),
            jax.ShapeDtypeStruct((64, TG * 64, 512), BF16),
            jax.ShapeDtypeStruct((512, 512), BF16),
            jax.ShapeDtypeStruct((256, 256), BF16),
            jax.ShapeDtypeStruct((TQ, 16, 512), BF16),
        ),
        in_specs=[hbm] * 6,
        out_specs=(vmem(),) * 7,
        scratch_shapes=[
            pltpu.SMEM((16,), jnp.int32),
            pltpu.VMEM((16, 2048), BF16),
            pltpu.VMEM((16, 64, 128), BF16),
            pltpu.VMEM((2, 1, 512), jnp.int32),
            pltpu.VMEM((16, 16, 128), BF16),
            pltpu.VMEM((TQ * 16, TG * 64), BF16),
            pltpu.VMEM((64, 64, 512), BF16),
            pltpu.VMEM((TG, 16, 512), BF16),
            pltpu.VMEM((1024, 512), BF16),
            pltpu.VMEM((1024, 512), BF16),
            pltpu.VMEM((1024, 512), BF16),
            pltpu.VMEM((1024, 512), BF16),
            pltpu.VMEM((4, 4, 2, 16, 1024), F32),
            pltpu.VMEM((4, 4, 16, 1024), F32),
            dma((5,)),
            dma((4,)),
            dma((64,)),
            dma((64,)),
        ],
        compiler_params=pltpu.CompilerParams(
            collective_id=0, has_side_effects=True, vmem_limit_bytes=32 << 20
        ),
    )(*[
        pltpu.with_memory_space_constraint(a, pltpu.HBM)
        for a in (
            charges,
            counts,
            basis_t,
            far_t,
            far_source.reshape(1, 512),
            far_target.reshape(1, 512),
        )
    ])
    nacc = pl.pallas_call(
        local_kernel,
        name="local",
        out_shape=jax.ShapeDtypeStruct((8, 4, 16, 16, 128), F32),
        in_specs=[smem, smem, vmem(), vmem()],
        out_specs=vmem(),
        compiler_params=pltpu.CompilerParams(vmem_limit_bytes=24 << 20),
    )(near_first, near_second, near_tiles, X)
    chunk = (16, 16, 128)
    half = (8, 16, 128)
    i16 = jnp.int16
    return pl.pallas_call(
        reduce_kernel,
        name="reduce",
        out_shape=jax.ShapeDtypeStruct((16, 2048), F32),
        in_specs=[vmem()] * 8 + [smem, vmem(), vmem()],
        out_specs=vmem(),
        scratch_shapes=[
            pltpu.VMEM((3, 4) + chunk, F32),
            pltpu.VMEM((4, 4) + chunk, F32),
            pltpu.VMEM((4,) + chunk, F32),
            pltpu.VMEM((4, 16, 1024), F32),
            pltpu.VMEM((8,) + half, i16),
            pltpu.VMEM((8,) + half, i16),
            pltpu.VMEM((11,) + chunk, i16),
            pltpu.VMEM((11,) + chunk, i16),
            pltpu.VMEM((2, 2, 16, 1024), i16),
            pltpu.VMEM((2, 2, 16, 1024), i16),
            pltpu.VMEM((2, 4, 16, 1024), i16),
            pltpu.VMEM((2, 4, 16, 1024), i16),
            pltpu.VMEM((2, 1, 16, 512), i16),
            pltpu.VMEM((2, 1, 16, 512), i16),
            pltpu.VMEM((2, 1, 16, 1024), i16),
            pltpu.VMEM((2, 1, 16, 1024), i16),
            pltpu.VMEM((27, 8, 128), F32),
            pltpu.VMEM((27, 8, 128), F32),
            pltpu.VMEM((TQ * 16, TG * 64), F32),
            pltpu.VMEM((1024, 512), BF16),
            pltpu.VMEM((1024, 512), BF16),
            dma((57,)),
            dma((57,)),
        ],
        compiler_params=pltpu.CompilerParams(
            collective_id=1, has_side_effects=True, vmem_limit_bytes=28 << 20
        ),
    )(
        nacc, CF, Mt, tm, ohs, perm, mqb, charges, counts, self_tiles, basis_t
    )


def solution(mesh):
    in_specs = (
        P("rhs", "blk"),
        P("blk"),
        P("blk", None, None),
        P("blk", None, None),
        P("blk"),
        P("blk"),
        P(("blk", "rhs"), None, None),
        P("blk"),
        P("blk"),
        P("blk", None, None),
    )
    return jax.shard_map(
        body, mesh=mesh, in_specs=in_specs, out_specs=P("rhs", "blk"), check_vma=False
    )
```

```python
import functools

import jax
import jax.numpy as jnp
from jax import lax
from jax.experimental import pallas as pl
from jax.experimental.pallas import tpu as pltpu
from jax.sharding import PartitionSpec as P

MESH = pl.DeviceIdType.MESH
F32 = jnp.float32
BF16 = jnp.bfloat16
NT = (((1,), (1,)), ((), ()))
TN = (((0,), (0,)), ((), ()))


class Place:
    def __init__(self):
        self.o = lax.axis_index("blk")
        self.x = lax.axis_index("rhs")
        self.k = self.o % 2
        self.c = self.o // 2
        self.y = self.c % 4
        self.z = self.c // 4
        self.xp = (self.x + 1) % 4
        self.xm = (self.x + 3) % 4
        self.xo = (self.x + 2) % 4
        self.yp = (self.y + 1) % 4
        self.ym = (self.y + 3) % 4
        self.yo = (self.y + 2) % 4
        self.zp = (self.z + 1) % 4
        self.zm = (self.z + 3) % 4
        self.zo = (self.z + 2) % 4
        self.sib = self.dev(self.c, 1 - self.k)
        self.east = {"blk": self.o, "rhs": self.xp}
        self.west = {"blk": self.o, "rhs": self.xm}
        self.cp = (self.c + 1) % 16
        self.cm = (self.c + 15) % 16
        self.up = self.dev(self.cp, self.k)
        self.down = self.dev(self.cm, self.k)
        self.up_other = self.dev(self.cp, 1 - self.k)
        self.down_other = self.dev(self.cm, 1 - self.k)
        self.y_plus = self.dev(self.z * 4 + self.yp, self.k)
        self.y_minus = self.dev(self.z * 4 + self.ym, self.k)
        self.z_plus = self.dev(self.zp * 4 + self.y, self.k)
        self.z_minus = self.dev(self.zm * 4 + self.y, self.k)
        self.two_away = self.dev((self.c + 14 + 4 * self.k) % 16, 1 - self.k)
        self.near_relay = self.dev((self.c + 15 + 2 * self.k) % 16, self.k)
        self.near_away = self.dev((self.c + 1 + 14 * self.k) % 16, self.k)
        self.far_chip = self.dev((self.c + 15 + 2 * self.k) % 16, 1 - self.k)

    def dev(self, chip, core):
        return {"blk": chip * 2 + core, "rhs": self.x}

    def plane(self):
        return [((self.z + dz) % 4, (self.y + dy) % 4) for dz, dy in STEPS]

    def greet(self, whole_plane):
        self.barrier = pltpu.get_barrier_semaphore()
        self.peers = [
            self.sib,
            self.east,
            self.west,
            self.up,
            self.down,
            self.up_other,
            self.down_other,
            self.two_away,
        ]
        if whole_plane:
            self.peers += [self.dev(z * 4 + y, self.k) for z, y in self.plane()]
        else:
            self.peers += [self.y_plus, self.y_minus, self.z_plus, self.z_minus]
        for peer in self.peers:
            pl.semaphore_signal(self.barrier, inc=1, device_id=peer, device_id_type=MESH)

    def met(self):
        pl.semaphore_wait(self.barrier, len(self.peers))


class Sender:
    def __init__(self, send_sems, recv_sems):
        self.send_sems, self.recv_sems, self.n, self.out = send_sems, recv_sems, 0, []

    def copy(self, src, dst, peer):
        at = self.n
        self.n += 1
        made = pltpu.make_async_remote_copy(
            src_ref=src,
            dst_ref=dst,
            send_sem=self.send_sems.at[at],
            recv_sem=self.recv_sems.at[at],
            device_id=peer,
            device_id_type=MESH,
        )
        made.start()
        self.out.append(made)
        return made

    def drain(self):
        for made in self.out:
            made.wait_send()


TG = 2
TQ = 16 // TG
NJ = 4
UR = 2
NS = 8


STEPS = [(dz, dy) for dy in (1, 3, 0) for dz in (2, 1, 3, 0) if dz or dy]


def gather_kernel(
    charges, counts, basis_t, far, fs, ft, X, CF, Mt, tm, ohs, perm, mqb,
    nbuf, qbuf, bbuf, ibuf, own, mq, tin, mgb, yhi, ylo, zhi, zlo, S, RF,
    in_sem, tin_sem, ss, rs,
):
    p = Place()
    x, k = p.x, p.k
    p.greet(True)
    small = [
        pltpu.make_async_copy(charges, qbuf, in_sem.at[0]),
        pltpu.make_async_copy(basis_t, bbuf, in_sem.at[1]),
        pltpu.make_async_copy(counts, nbuf, in_sem.at[2]),
        pltpu.make_async_copy(fs, ibuf.at[0], in_sem.at[3]),
        pltpu.make_async_copy(ft, ibuf.at[1], in_sem.at[4]),
    ]
    loads = [
        pltpu.make_async_copy(far.at[pl.ds(i * 16, 16)], tin.at[pl.ds(i * 16, 16)], tin_sem.at[i])
        for i in range(4)
    ]
    for load in small + loads:
        load.start()
    for load in small[:3]:
        load.wait()
    lane = lax.broadcasted_iota(jnp.int32, (16, 128), 1)
    for b in range(16):
        block = qbuf[:, b * 128 : (b + 1) * 128]
        own[b] = jnp.where(lane < nbuf[b], block.astype(F32), 0.0).astype(BF16)
    X[3 + k, x] = own[...]
    p.met()
    s = Sender(ss, rs)
    sib = []
    farsib = []
    me = X.at[3 + k, x]

    def ring_start(u):
        src = X.at[u, x]
        return s.copy(src, X.at[u, x], p.east), s.copy(src, X.at[u, x], p.west)

    def arrived(pair):
        for made in pair:
            made.wait_recv()

    def ring_relay(u, pair):
        arrived(pair)
        made = (
            s.copy(X.at[u, p.xm, pl.ds(0, 8)], X.at[u, p.xm, pl.ds(0, 8)], p.east),
            s.copy(X.at[u, p.xp, pl.ds(8, 8)], X.at[u, p.xp, pl.ds(8, 8)], p.west),
        )
        if u is not edge:
            to_sib(u, p.xm)
            to_sib(u, p.xp)
        return made

    def column_on(y):
        farsib.append(s.copy(Mt.at[:, y, k], Mt.at[:, y, k], p.sib))

    def to_sib(u, at):
        sib.append(s.copy(X.at[u, at], X.at[u, at], p.sib))

    u0, u1, u2, u3 = 7 * k, 1 + k, 3 + k, 5 + k
    edge = u0
    to_up = s.copy(me, X.at[u1, x], p.up)
    to_down = s.copy(me, X.at[u3, x], p.down)
    ring2 = ring_start(u2)

    moments = []
    for b in range(16):
        m = lax.dot_general(own[b], bbuf[b], NT, preferred_element_type=F32).astype(BF16)
        moments.append(m.astype(F32))
    rows = jnp.swapaxes(jnp.stack(moments, axis=0), 0, 1)
    Mt[p.z, p.y, k] = jnp.concatenate([rows[r] for r in range(16)], axis=-1).astype(BF16)
    mine = Mt.at[p.z, p.y, k]
    plane = p.plane()
    far_all = [s.copy(mine, mine, p.dev(z * 4 + y, k)) for z, y in plane]
    to_sib(u2, x)

    for a in range(TQ):
        mq[a * 16 : (a + 1) * 16, :] = jnp.concatenate(
            [moments[g * TQ + a] for g in range(TG)], axis=-1
        ).astype(BF16)
    row = lax.broadcasted_iota(jnp.int32, (256, 256), 0)
    col = lax.broadcasted_iota(jnp.int32, (256, 256), 1)
    swap = ((row >> 4) == (col & 15)) & ((row & 15) == (col >> 4))
    perm[...] = jnp.where(swap, 1.0, 0.0).astype(BF16)
    small[3].wait()
    small[4].wait()
    tl = ibuf[1] - p.o * 16
    tg = tl // TQ
    tq = tl - tg * TQ
    ohs[...] = jnp.where(
        lax.broadcasted_iota(jnp.int32, (512, 512), 0) == ibuf[0], 1.0, 0.0
    ).astype(BF16)
    for g in range(TG):
        mgb[g] = jnp.broadcast_to(jnp.where(tg == g, 1.0, 0.0).astype(BF16), (16, 512))
    for g in range(TQ):
        mqb[g] = jnp.broadcast_to(jnp.where(tq == g, 1.0, 0.0).astype(BF16), (16, 512))

    def relayout(i):
        loads[i].wait()

        @pl.loop(0, 4, unroll=UR)
        def _(n):
            at = pl.ds(pl.multiple_of(n * 16, 16), 16)
            block = tin[i * 16 : (i + 1) * 16, at, :].reshape(256, 512)
            moved = jnp.dot(perm[...], block, preferred_element_type=F32).astype(BF16)
            moved = moved.reshape(16, 16, 512)
            for g in range(TG):
                tm[at, g * 64 + i * 16 : g * 64 + (i + 1) * 16, :] = moved * mgb[g][None]

    def to_sources(first, last):
        @pl.loop(first * 4 // NS, last * 4 // NS)
        def _(n):
            for a in range(NS):
                j = n * NS + a
                yj = jnp.dot(mq[...], tm[j], preferred_element_type=F32)
                y = jnp.where(tq == 0, yj[0:16], 0.0)
                for g in range(1, TQ):
                    y = jnp.where(tq == g, yj[g * 16 : (g + 1) * 16], y)
                hi = y.astype(BF16)
                at = pl.ds(pl.multiple_of(j * 16, 16), 16)
                yhi[at, :] = hi
                ylo[at, :] = (y - hi.astype(F32)).astype(BF16)

    relayout(0)
    relayout(1)
    arrived((to_up, to_down))
    two = s.copy(X.at[5 - 3 * k, x], X.at[7 - 7 * k, x], p.far_chip)
    ring1 = ring_start(u1)
    ring3 = ring_start(u3)
    to_sib(u1, x)
    to_sib(u3, x)
    relayout(2)
    relay2 = ring_relay(u2, ring2)
    relayout(3)
    to_sources(0, 2)
    two.wait_recv()
    ring0 = ring_start(u0)
    to_sources(2, 4)
    relay1 = ring_relay(u1, ring1)
    to_sources(4, 6)
    relay3 = ring_relay(u3, ring3)
    arrived(far_all[:8])
    column_on(p.ym)
    column_on(p.yp)
    east, west = Mt.at[:, p.ym, k, :, pl.ds(0, 512)], Mt.at[:, p.yp, k, :, pl.ds(512, 512)]
    far_y2 = s.copy(east, east, p.y_plus), s.copy(west, west, p.y_minus)
    to_sources(6, 10)
    to_sources(10, 14)
    arrived(relay2)
    to_sib(u2, p.xo)
    relay0 = ring_relay(u0, ring0)
    to_sources(14, 16)
    arrived(far_all[8:])
    column_on(p.y)
    arrived(far_y2)
    column_on(p.yo)
    for h in range(4):
        for src, dst in ((yhi, zhi), (ylo, zlo)):
            moved = jnp.dot(
                perm[...], src[h * 256 : (h + 1) * 256, :], preferred_element_type=F32
            ).astype(BF16)
            for r in range(16):
                dst[r * 64 + h * 16 : r * 64 + (h + 1) * 16, :] = moved[r * 16 : (r + 1) * 16]
    arrived(relay1)
    to_sib(u1, p.xo)
    for h in range(4):
        at = slice(h * 256, (h + 1) * 256)
        part = lax.dot_general(
            ohs[...], zhi[at, :], NT, preferred_element_type=F32
        ) + lax.dot_general(ohs[...], zlo[at, :], NT, preferred_element_type=F32)
        S[:, :, :, :, at] = part.reshape(4, 4, 2, 16, 256)
    sums = s.copy(S.at[:, :, 1 - k], RF, p.sib)
    arrived(relay3)
    to_sib(u3, p.xo)
    arrived(farsib)

    sums.wait_recv()
    CF[...] = S[:, :, k] + RF[...]
    arrived(relay0)
    arrived(sib)
    s.drain()


def local_kernel(nf, ns, tiles, X, nacc):
    o = lax.axis_index("blk")
    k = o % 2
    base = lax.axis_index("rhs") * 128
    nacc[...] = jnp.zeros_like(nacc)

    none = jnp.zeros((64, 128), BF16)
    ua = 3 + k

    def ends(n):
        d = (ns[base + n] - o * 16 + 560) & 511
        return nf[base + n] - o * 16, (d >> 4) + k, d & 15

    @pl.loop(0, 64, unroll=16)
    def _(m):
        a0, u0, b0 = ends(2 * m)
        a1, u1, b1 = ends(2 * m + 1)
        both = jnp.concatenate([tiles[2 * m], tiles[2 * m + 1]], axis=1)
        xb0 = X[u0, :, b0].reshape(64, 128)
        xb1 = X[u1, :, b1].reshape(64, 128)
        xa0 = X[ua, :, a0].reshape(64, 128)
        xa1 = X[ua, :, a1].reshape(64, 128)
        apart = jnp.concatenate(
            [jnp.concatenate([xb0, none], axis=1), jnp.concatenate([none, xb1], axis=1)], axis=0
        )
        to_first = lax.dot_general(apart, both, NT, preferred_element_type=F32)
        to_second = jnp.dot(
            jnp.concatenate([xa0, xa1], axis=0), both, preferred_element_type=F32
        )
        nacc[ua, :, a0] += to_first[:64].reshape(4, 16, 128)
        nacc[u0, :, b0] += to_second[:64, :128].reshape(4, 16, 128)
        nacc[ua, :, a1] += to_first[64:].reshape(4, 16, 128)
        nacc[u1, :, b1] += to_second[64:, 128:].reshape(4, 16, 128)


class Wire:
    def __init__(self, sender, scs, scr):
        self.sender, self.scs, self.scr, self.n = sender, scs, scr, 0

    def send(self, value, src, dst, peer):
        at = self.n
        self.n += 1
        lanes = value.shape[-1] // 128
        most = jnp.full((8, 128), 1e-30, F32)
        for w in range(lanes):
            top = jnp.max(jnp.abs(value[:, :, w * 128 : (w + 1) * 128]), axis=0)
            most = jnp.maximum(most, jnp.maximum(top[:8], top[8:]))
        self.scs[at] = most * (1.0 / 32000.0)
        src[...] = jnp.round(value * self.tile(32000.0 / most, lanes)).astype(jnp.int32).astype(jnp.int16)
        made = (
            self.sender.copy(self.scs.at[at], self.scr.at[at], peer),
            self.sender.copy(src, dst, peer),
        )
        return made, dst, at

    def tile(self, scale, lanes):
        both = jnp.concatenate([scale, scale], axis=0)
        return jnp.concatenate([both] * lanes, axis=1)[None]

    def take(self, sent):
        made, dst, at = sent
        made[0].wait_recv()
        made[1].wait_recv()
        value = dst[...].astype(jnp.int32).astype(F32)
        return value * self.tile(self.scr[at], value.shape[-1] // 128)


def reduce_kernel(
    nacc, CF, Mt, tm, ohs, perm, mqb, charges, counts, self_tiles, basis_t, out,
    R, C, V, W, hs, hr, ws, wr, z2s, z2r, z1s, z1r, y2s, y2r, y1s, y1r, scs, scr,
    out1, gtmp, gj, ss, rs,
):
    p = Place()
    x, k = p.x, p.k
    p.greet(False)
    C[0] = nacc[7 * k]
    p.met()
    s = Sender(ss, rs)
    wire = Wire(s, scs, scr)
    near_sib = [
        s.copy(nacc.at[u], R.at[i], p.sib) for i, u in enumerate((6 - 5 * k, 2 + 3 * k, 4 - k))
    ]
    two = {}
    ring = {}

    def first(i):
        two[i] = (
            wire.send(C[i, p.xo, pl.ds(0, 8)], hs.at[2 * i], hr.at[2 * i], p.east),
            wire.send(C[i, p.xo, pl.ds(8, 8)], hs.at[2 * i + 1], hr.at[2 * i + 1], p.west),
        )

    def second(i):
        C[i, p.xp, pl.ds(0, 8)] += wire.take(two[i][0])
        C[i, p.xm, pl.ds(8, 8)] += wire.take(two[i][1])
        ring[i] = (
            wire.send(C[i, p.xp], ws.at[2 * i], wr.at[2 * i], p.east),
            wire.send(C[i, p.xm], ws.at[2 * i + 1], wr.at[2 * i + 1], p.west),
        )

    def third(i):
        V[i] = C[i, x] + wire.take(ring[i][0]) + wire.take(ring[i][1])

    def source_moments(half):
        for h in (2 * half, 2 * half + 1):
            table = Mt[:, :, :, :, h * 256 : (h + 1) * 256].reshape(512, 256)
            gtmp[h * 256 : (h + 1) * 256, :] = lax.dot_general(
                table, ohs[...], TN, preferred_element_type=F32
            ).astype(BF16)

    def reorder():
        for h in range(4):
            block = jnp.concatenate(
                [gtmp[r * 64 + h * 16 : r * 64 + (h + 1) * 16, :] for r in range(16)], axis=0
            )
            gj[h * 256 : (h + 1) * 256, :] = jnp.dot(
                perm[...], block, preferred_element_type=F32
            ).astype(BF16)

    def to_targets(first, last):
        @pl.loop(first, last)
        def _(n):
            total = out1[...]
            for a in range(NJ):
                j = n * NJ + a
                ms = gj[pl.ds(pl.multiple_of(j * 16, 16), 16), :]
                zj = (ms[None] * mqb[...]).reshape(TQ * 16, 512)
                total = total + lax.dot_general(zj, tm[j], NT, preferred_element_type=F32)
            out1[...] = total

    first(0)
    fz2 = (
        wire.send(CF[p.zo, pl.ds(0, 2)], z2s.at[0], z2r.at[0], p.z_plus),
        wire.send(CF[p.zo, pl.ds(2, 2)], z2s.at[1], z2r.at[1], p.z_minus),
    )
    for i, (slot, u) in enumerate(((1, 1 + 5 * k), (3, 5 - 3 * k), (2, 3 + k))):
        near_sib[i].wait_recv()
        C[slot] = nacc[u] + R[i]
        first(slot)
    out1[...] = jnp.zeros_like(out1)
    lane = lax.broadcasted_iota(jnp.int32, (16, 128), 1)
    for b in range(16):
        part = charges[:, b * 128 : (b + 1) * 128]
        part = jnp.where(lane < counts[b], part.astype(F32), 0.0).astype(BF16)
        out[:, b * 128 : (b + 1) * 128] = lax.dot_general(
            part, self_tiles[b], NT, preferred_element_type=F32
        )
    second(0)
    z_up = CF[p.zp]
    z_down = CF[p.zm]
    fz = (
        wire.send(
            jnp.concatenate([z_up[:2] + wire.take(fz2[0]), z_up[2:]], axis=0),
            z1s.at[0],
            z1r.at[0],
            p.z_plus,
        ),
        wire.send(
            jnp.concatenate([z_down[:2], z_down[2:] + wire.take(fz2[1])], axis=0),
            z1s.at[1],
            z1r.at[1],
            p.z_minus,
        ),
    )
    second(1)
    source_moments(0)
    second(3)
    second(2)
    source_moments(1)
    third(0)
    relay = wire.send(V[0], ws.at[8], wr.at[8], p.two_away)
    reorder()
    third(1)
    near_last = [wire.send(V[1], ws.at[9], wr.at[9], p.near_relay)]
    W[...] = CF[p.z] + wire.take(fz[0]) + wire.take(fz[1])
    fy2 = (
        wire.send(W[pl.ds(p.yo, 1), :, pl.ds(0, 512)], y2s.at[0], y2r.at[0], p.y_plus),
        wire.send(W[pl.ds(p.yo, 1), :, pl.ds(512, 512)], y2s.at[1], y2r.at[1], p.y_minus),
    )
    third(3)
    near_last.append(wire.send(V[3], ws.at[10], wr.at[10], p.near_away))
    to_targets(0, 6)
    W[pl.ds(p.yp, 1), :, pl.ds(0, 512)] += wire.take(fy2[0])
    W[pl.ds(p.ym, 1), :, pl.ds(512, 512)] += wire.take(fy2[1])
    fy = (
        wire.send(W[pl.ds(p.yp, 1)], y1s.at[0], y1r.at[0], p.y_plus),
        wire.send(W[pl.ds(p.ym, 1)], y1s.at[1], y1r.at[1], p.y_minus),
    )
    third(2)
    to_targets(6, 16)
    V[2] += wire.take(relay) + wire.take(near_last[0]) + wire.take(near_last[1])
    flat = (W[pl.ds(p.y, 1)] + wire.take(fy[0]) + wire.take(fy[1]))[0]
    rows = jnp.stack([flat[:, r * 64 : (r + 1) * 64] for r in range(16)], axis=0)
    rows = jnp.swapaxes(rows, 0, 1)
    for b in range(16):
        own1 = out1[b % TQ * 16 : b % TQ * 16 + 16, b // TQ * 64 : b // TQ * 64 + 64]
        fields = (rows[b] + own1).astype(BF16)
        far_part = jnp.dot(fields, basis_t[b], preferred_element_type=F32)
        cols = slice(b * 128, (b + 1) * 128)
        out[:, cols] = jnp.where(lane < counts[b], out[:, cols] + V[2, b] + far_part, 0.0)
    s.drain()


def vmem():
    return pl.BlockSpec(memory_space=pltpu.VMEM)


def body(
    charges, counts, self_tiles, basis, near_first, near_second, near_tiles, far_source, far_target, far_tiles
):
    basis_t = jnp.transpose(basis, (0, 2, 1))
    far_t = jnp.transpose(far_tiles, (1, 2, 0))
    smem = pl.BlockSpec(memory_space=pltpu.SMEM)
    hbm = pl.BlockSpec(memory_space=pltpu.HBM)
    dma = pltpu.SemaphoreType.DMA
    X, CF, Mt, tm, ohs, perm, mqb = pl.pallas_call(
        gather_kernel,
        name="gather",
        out_shape=(
            jax.ShapeDtypeStruct((8, 4, 16, 16, 128), BF16),
            jax.ShapeDtypeStruct((4, 4, 16, 1024), F32),
            jax.ShapeDtypeStruct((4, 4, 2, 16, 1024), BF16),
            jax.ShapeDtypeStruct((64, TG * 64, 512), BF16),
            jax.ShapeDtypeStruct((512, 512), BF16),
            jax.ShapeDtypeStruct((256, 256), BF16),
            jax.ShapeDtypeStruct((TQ, 16, 512), BF16),
        ),
        in_specs=[hbm] * 6,
        out_specs=(vmem(),) * 7,
        scratch_shapes=[
            pltpu.SMEM((16,), jnp.int32),
            pltpu.VMEM((16, 2048), BF16),
            pltpu.VMEM((16, 64, 128), BF16),
            pltpu.VMEM((2, 1, 512), jnp.int32),
            pltpu.VMEM((16, 16, 128), BF16),
            pltpu.VMEM((TQ * 16, TG * 64), BF16),
            pltpu.VMEM((64, 64, 512), BF16),
            pltpu.VMEM((TG, 16, 512), BF16),
            pltpu.VMEM((1024, 512), BF16),
            pltpu.VMEM((1024, 512), BF16),
            pltpu.VMEM((1024, 512), BF16),
            pltpu.VMEM((1024, 512), BF16),
            pltpu.VMEM((4, 4, 2, 16, 1024), F32),
            pltpu.VMEM((4, 4, 16, 1024), F32),
            dma((5,)),
            dma((4,)),
            dma((64,)),
            dma((64,)),
        ],
        compiler_params=pltpu.CompilerParams(
            collective_id=0, has_side_effects=True, vmem_limit_bytes=32 << 20
        ),
    )(*[
        pltpu.with_memory_space_constraint(a, pltpu.HBM)
        for a in (
            charges,
            counts,
            basis_t,
            far_t,
            far_source.reshape(1, 512),
            far_target.reshape(1, 512),
        )
    ])
    nacc = pl.pallas_call(
        local_kernel,
        name="local",
        out_shape=jax.ShapeDtypeStruct((8, 4, 16, 16, 128), F32),
        in_specs=[smem, smem, vmem(), vmem()],
        out_specs=vmem(),
        compiler_params=pltpu.CompilerParams(vmem_limit_bytes=24 << 20),
    )(near_first, near_second, near_tiles, X)
    chunk = (16, 16, 128)
    half = (8, 16, 128)
    i16 = jnp.int16
    return pl.pallas_call(
        reduce_kernel,
        name="reduce",
        out_shape=jax.ShapeDtypeStruct((16, 2048), F32),
        in_specs=[vmem()] * 8 + [smem, vmem(), vmem()],
        out_specs=vmem(),
        scratch_shapes=[
            pltpu.VMEM((3, 4) + chunk, F32),
            pltpu.VMEM((4, 4) + chunk, F32),
            pltpu.VMEM((4,) + chunk, F32),
            pltpu.VMEM((4, 16, 1024), F32),
            pltpu.VMEM((8,) + half, i16),
            pltpu.VMEM((8,) + half, i16),
            pltpu.VMEM((11,) + chunk, i16),
            pltpu.VMEM((11,) + chunk, i16),
            pltpu.VMEM((2, 2, 16, 1024), i16),
            pltpu.VMEM((2, 2, 16, 1024), i16),
            pltpu.VMEM((2, 4, 16, 1024), i16),
            pltpu.VMEM((2, 4, 16, 1024), i16),
            pltpu.VMEM((2, 1, 16, 512), i16),
            pltpu.VMEM((2, 1, 16, 512), i16),
            pltpu.VMEM((2, 1, 16, 1024), i16),
            pltpu.VMEM((2, 1, 16, 1024), i16),
            pltpu.VMEM((27, 8, 128), F32),
            pltpu.VMEM((27, 8, 128), F32),
            pltpu.VMEM((TQ * 16, TG * 64), F32),
            pltpu.VMEM((1024, 512), BF16),
            pltpu.VMEM((1024, 512), BF16),
            dma((57,)),
            dma((57,)),
        ],
        compiler_params=pltpu.CompilerParams(
            collective_id=1, has_side_effects=True, vmem_limit_bytes=28 << 20
        ),
    )(
        nacc, CF, Mt, tm, ohs, perm, mqb, charges, counts, self_tiles, basis_t
    )


def solution(mesh):
    in_specs = (
        P("rhs", "blk"),
        P("blk"),
        P("blk", None, None),
        P("blk", None, None),
        P("blk"),
        P("blk"),
        P(("blk", "rhs"), None, None),
        P("blk"),
        P("blk"),
        P("blk", None, None),
    )
    return jax.shard_map(
        body, mesh=mesh, in_specs=in_specs, out_specs=P("rhs", "blk"), check_vma=False
    )
```

```python
import functools

import jax
import jax.numpy as jnp
from jax import lax
from jax.experimental import pallas as pl
from jax.experimental.pallas import tpu as pltpu
from jax.sharding import PartitionSpec as P

MESH = pl.DeviceIdType.MESH
F32 = jnp.float32
BF16 = jnp.bfloat16
NT = (((1,), (1,)), ((), ()))
TN = (((0,), (0,)), ((), ()))


class Place:
    def __init__(self):
        self.o = lax.axis_index("blk")
        self.x = lax.axis_index("rhs")
        self.k = self.o % 2
        self.c = self.o // 2
        self.y = self.c % 4
        self.z = self.c // 4
        self.xp = (self.x + 1) % 4
        self.xm = (self.x + 3) % 4
        self.xo = (self.x + 2) % 4
        self.yp = (self.y + 1) % 4
        self.ym = (self.y + 3) % 4
        self.yo = (self.y + 2) % 4
        self.zp = (self.z + 1) % 4
        self.zm = (self.z + 3) % 4
        self.zo = (self.z + 2) % 4
        self.sib = self.dev(self.c, 1 - self.k)
        self.east = {"blk": self.o, "rhs": self.xp}
        self.west = {"blk": self.o, "rhs": self.xm}
        self.cp = (self.c + 1) % 16
        self.cm = (self.c + 15) % 16
        self.up = self.dev(self.cp, self.k)
        self.down = self.dev(self.cm, self.k)
        self.up_other = self.dev(self.cp, 1 - self.k)
        self.down_other = self.dev(self.cm, 1 - self.k)
        self.y_plus = self.dev(self.z * 4 + self.yp, self.k)
        self.y_minus = self.dev(self.z * 4 + self.ym, self.k)
        self.y_across = self.dev(self.z * 4 + self.yo, self.k)
        self.z_plus = self.dev(self.zp * 4 + self.y, self.k)
        self.z_minus = self.dev(self.zm * 4 + self.y, self.k)
        self.two_away = self.dev((self.c + 14 + 4 * self.k) % 16, 1 - self.k)
        self.near_relay = self.dev((self.c + 15 + 2 * self.k) % 16, self.k)
        self.near_away = self.dev((self.c + 1 + 14 * self.k) % 16, self.k)
        self.far_chip = self.dev((self.c + 15 + 2 * self.k) % 16, 1 - self.k)

    def dev(self, chip, core):
        return {"blk": chip * 2 + core, "rhs": self.x}

    def plane(self):
        return [((self.z + dz) % 4, (self.y + dy) % 4) for dz, dy in STEPS]

    def greet(self, whole_plane):
        self.barrier = pltpu.get_barrier_semaphore()
        self.peers = [
            self.sib,
            self.east,
            self.west,
            self.up,
            self.down,
            self.up_other,
            self.down_other,
            self.two_away,
        ]
        if whole_plane:
            self.peers += [self.dev(z * 4 + y, self.k) for z, y in self.plane()]
        else:
            self.peers += [self.y_plus, self.y_minus, self.y_across, self.z_plus, self.z_minus]
        for peer in self.peers:
            pl.semaphore_signal(self.barrier, inc=1, device_id=peer, device_id_type=MESH)

    def met(self):
        pl.semaphore_wait(self.barrier, len(self.peers))


class Sender:
    def __init__(self, send_sems, recv_sems):
        self.send_sems, self.recv_sems, self.n, self.out = send_sems, recv_sems, 0, []

    def copy(self, src, dst, peer):
        at = self.n
        self.n += 1
        made = pltpu.make_async_remote_copy(
            src_ref=src,
            dst_ref=dst,
            send_sem=self.send_sems.at[at],
            recv_sem=self.recv_sems.at[at],
            device_id=peer,
            device_id_type=MESH,
        )
        made.start()
        self.out.append(made)
        return made

    def drain(self):
        for made in self.out:
            made.wait_send()


TG = 2
TQ = 16 // TG
NJ = 4
UR = 2
NS = 8


STEPS = [(dz, dy) for dy in (1, 3, 0) for dz in (2, 1, 3, 0) if dz or dy]


def gather_kernel(
    charges, counts, basis_t, far, fs, ft, X, CF, Mt, tm, ohs, perm, mqb,
    nbuf, qbuf, bbuf, ibuf, own, mq, tin, mgb, yhi, ylo, zhi, zlo, S, RF,
    in_sem, tin_sem, ss, rs,
):
    p = Place()
    x, k = p.x, p.k
    p.greet(True)
    small = [
        pltpu.make_async_copy(charges, qbuf, in_sem.at[0]),
        pltpu.make_async_copy(basis_t, bbuf, in_sem.at[1]),
        pltpu.make_async_copy(counts, nbuf, in_sem.at[2]),
        pltpu.make_async_copy(fs, ibuf.at[0], in_sem.at[3]),
        pltpu.make_async_copy(ft, ibuf.at[1], in_sem.at[4]),
    ]
    loads = [
        pltpu.make_async_copy(far.at[pl.ds(i * 16, 16)], tin.at[pl.ds(i * 16, 16)], tin_sem.at[i])
        for i in range(4)
    ]
    for load in small + loads:
        load.start()
    for load in small[:3]:
        load.wait()
    lane = lax.broadcasted_iota(jnp.int32, (16, 128), 1)
    for b in range(16):
        block = qbuf[:, b * 128 : (b + 1) * 128]
        own[b] = jnp.where(lane < nbuf[b], block.astype(F32), 0.0).astype(BF16)
    X[3 + k, x] = own[...]
    p.met()
    s = Sender(ss, rs)
    sib = []
    farsib = []
    me = X.at[3 + k, x]

    def ring_start(u):
        src = X.at[u, x]
        return s.copy(src, X.at[u, x], p.east), s.copy(src, X.at[u, x], p.west)

    def arrived(pair):
        for made in pair:
            made.wait_recv()

    def ring_relay(u, pair):
        arrived(pair)
        made = (
            s.copy(X.at[u, p.xm, pl.ds(0, 8)], X.at[u, p.xm, pl.ds(0, 8)], p.east),
            s.copy(X.at[u, p.xp, pl.ds(8, 8)], X.at[u, p.xp, pl.ds(8, 8)], p.west),
        )
        if u is not edge:
            to_sib(u, p.xm)
            to_sib(u, p.xp)
        return made

    def column_on(y):
        farsib.append(s.copy(Mt.at[:, y, k], Mt.at[:, y, k], p.sib))

    def to_sib(u, at):
        sib.append(s.copy(X.at[u, at], X.at[u, at], p.sib))

    u0, u1, u2, u3 = 7 * k, 1 + k, 3 + k, 5 + k
    edge = u0
    to_up = s.copy(me, X.at[u1, x], p.up)
    to_down = s.copy(me, X.at[u3, x], p.down)
    ring2 = ring_start(u2)

    moments = []
    for b in range(16):
        m = lax.dot_general(own[b], bbuf[b], NT, preferred_element_type=F32).astype(BF16)
        moments.append(m.astype(F32))
    rows = jnp.swapaxes(jnp.stack(moments, axis=0), 0, 1)
    Mt[p.z, p.y, k] = jnp.concatenate([rows[r] for r in range(16)], axis=-1).astype(BF16)
    mine = Mt.at[p.z, p.y, k]
    plane = p.plane()
    far_all = [s.copy(mine, mine, p.dev(z * 4 + y, k)) for z, y in plane]
    to_sib(u2, x)

    for a in range(TQ):
        mq[a * 16 : (a + 1) * 16, :] = jnp.concatenate(
            [moments[g * TQ + a] for g in range(TG)], axis=-1
        ).astype(BF16)
    row = lax.broadcasted_iota(jnp.int32, (256, 256), 0)
    col = lax.broadcasted_iota(jnp.int32, (256, 256), 1)
    swap = ((row >> 4) == (col & 15)) & ((row & 15) == (col >> 4))
    perm[...] = jnp.where(swap, 1.0, 0.0).astype(BF16)
    small[3].wait()
    small[4].wait()
    tl = ibuf[1] - p.o * 16
    tg = tl // TQ
    tq = tl - tg * TQ
    ohs[...] = jnp.where(
        lax.broadcasted_iota(jnp.int32, (512, 512), 0) == ibuf[0], 1.0, 0.0
    ).astype(BF16)
    for g in range(TG):
        mgb[g] = jnp.broadcast_to(jnp.where(tg == g, 1.0, 0.0).astype(BF16), (16, 512))
    for g in range(TQ):
        mqb[g] = jnp.broadcast_to(jnp.where(tq == g, 1.0, 0.0).astype(BF16), (16, 512))

    def relayout(i):
        loads[i].wait()

        @pl.loop(0, 4, unroll=UR)
        def _(n):
            at = pl.ds(pl.multiple_of(n * 16, 16), 16)
            block = tin[i * 16 : (i + 1) * 16, at, :].reshape(256, 512)
            moved = jnp.dot(perm[...], block, preferred_element_type=F32).astype(BF16)
            moved = moved.reshape(16, 16, 512)
            for g in range(TG):
                tm[at, g * 64 + i * 16 : g * 64 + (i + 1) * 16, :] = moved * mgb[g][None]

    def to_sources(first, last):
        @pl.loop(first * 4 // NS, last * 4 // NS)
        def _(n):
            for a in range(NS):
                j = n * NS + a
                yj = jnp.dot(mq[...], tm[j], preferred_element_type=F32)
                y = jnp.where(tq == 0, yj[0:16], 0.0)
                for g in range(1, TQ):
                    y = jnp.where(tq == g, yj[g * 16 : (g + 1) * 16], y)
                hi = y.astype(BF16)
                at = pl.ds(pl.multiple_of(j * 16, 16), 16)
                yhi[at, :] = hi
                ylo[at, :] = (y - hi.astype(F32)).astype(BF16)

    relayout(0)
    arrived((to_up, to_down))
    two = s.copy(X.at[5 - 3 * k, x], X.at[7 - 7 * k, x], p.far_chip)
    ring1 = ring_start(u1)
    ring3 = ring_start(u3)
    to_sib(u1, x)
    to_sib(u3, x)
    relayout(1)
    relayout(2)
    relay2 = ring_relay(u2, ring2)
    relayout(3)
    to_sources(0, 2)
    two.wait_recv()
    ring0 = ring_start(u0)
    to_sources(2, 4)
    relay1 = ring_relay(u1, ring1)
    to_sources(4, 6)
    relay3 = ring_relay(u3, ring3)
    arrived(far_all[:8])
    column_on(p.ym)
    column_on(p.yp)
    east, west = Mt.at[:, p.ym, k, :, pl.ds(0, 512)], Mt.at[:, p.yp, k, :, pl.ds(512, 512)]
    far_y2 = s.copy(east, east, p.y_plus), s.copy(west, west, p.y_minus)
    to_sources(6, 10)
    to_sources(10, 14)
    arrived(relay2)
    to_sib(u2, p.xo)
    relay0 = ring_relay(u0, ring0)
    to_sources(14, 16)
    for h in range(4):
        for src, dst in ((yhi, zhi), (ylo, zlo)):
            moved = jnp.dot(
                perm[...], src[h * 256 : (h + 1) * 256, :], preferred_element_type=F32
            ).astype(BF16)
            for r in range(16):
                dst[r * 64 + h * 16 : r * 64 + (h + 1) * 16, :] = moved[r * 16 : (r + 1) * 16]
    arrived(relay1)
    to_sib(u1, p.xo)
    sums = []
    for h in range(4):
        at = slice(h * 256, (h + 1) * 256)
        part = lax.dot_general(
            ohs[...], zhi[at, :], NT, preferred_element_type=F32
        ) + lax.dot_general(ohs[...], zlo[at, :], NT, preferred_element_type=F32)
        S[:, :, :, :, at] = part.reshape(4, 4, 2, 16, 256)
        if h == 1:
            arrived(far_all[8:])
            column_on(p.y)
            arrived(far_y2)
            column_on(p.yo)
        lanes = pl.ds(h * 256, 256)
        sums.append(s.copy(S.at[:, :, 1 - k, :, lanes], RF.at[:, :, :, lanes], p.sib))
    arrived(relay3)
    to_sib(u3, p.xo)
    arrived(farsib)

    for h in range(4):
        at = slice(h * 256, (h + 1) * 256)
        sums[h].wait_recv()
        CF[:, :, :, at] = S[:, :, k, :, at] + RF[:, :, :, at]
    arrived(relay0)
    arrived(sib)
    s.drain()


def local_kernel(nf, ns, tiles, X, nacc):
    o = lax.axis_index("blk")
    k = o % 2
    base = lax.axis_index("rhs") * 128
    nacc[...] = jnp.zeros_like(nacc)

    none = jnp.zeros((64, 128), BF16)
    ua = 3 + k

    def ends(n):
        d = (ns[base + n] - o * 16 + 560) & 511
        return nf[base + n] - o * 16, (d >> 4) + k, d & 15

    @pl.loop(0, 64, unroll=16)
    def _(m):
        a0, u0, b0 = ends(2 * m)
        a1, u1, b1 = ends(2 * m + 1)
        both = jnp.concatenate([tiles[2 * m], tiles[2 * m + 1]], axis=1)
        xb0 = X[u0, :, b0].reshape(64, 128)
        xb1 = X[u1, :, b1].reshape(64, 128)
        xa0 = X[ua, :, a0].reshape(64, 128)
        xa1 = X[ua, :, a1].reshape(64, 128)
        apart = jnp.concatenate(
            [jnp.concatenate([xb0, none], axis=1), jnp.concatenate([none, xb1], axis=1)], axis=0
        )
        to_first = lax.dot_general(apart, both, NT, preferred_element_type=F32)
        to_second = jnp.dot(
            jnp.concatenate([xa0, xa1], axis=0), both, preferred_element_type=F32
        )
        nacc[ua, :, a0] += to_first[:64].reshape(4, 16, 128)
        nacc[u0, :, b0] += to_second[:64, :128].reshape(4, 16, 128)
        nacc[ua, :, a1] += to_first[64:].reshape(4, 16, 128)
        nacc[u1, :, b1] += to_second[64:, 128:].reshape(4, 16, 128)


class Wire:
    def __init__(self, sender, scs, scr):
        self.sender, self.scs, self.scr, self.n = sender, scs, scr, 0

    def send(self, value, src, dst, peer):
        at = self.n
        self.n += 1
        lanes = value.shape[-1] // 128
        most = jnp.full((8, 128), 1e-30, F32)
        for w in range(lanes):
            top = jnp.max(jnp.abs(value[:, :, w * 128 : (w + 1) * 128]), axis=0)
            most = jnp.maximum(most, jnp.maximum(top[:8], top[8:]))
        self.scs[at] = most * (1.0 / 32000.0)
        src[...] = jnp.round(value * self.tile(32000.0 / most, lanes)).astype(jnp.int32).astype(jnp.int16)
        made = (
            self.sender.copy(self.scs.at[at], self.scr.at[at], peer),
            self.sender.copy(src, dst, peer),
        )
        return made, dst, at

    def tile(self, scale, lanes):
        both = jnp.concatenate([scale, scale], axis=0)
        return jnp.concatenate([both] * lanes, axis=1)[None]

    def take(self, sent):
        made, dst, at = sent
        made[0].wait_recv()
        made[1].wait_recv()
        value = dst[...].astype(jnp.int32).astype(F32)
        return value * self.tile(self.scr[at], value.shape[-1] // 128)


def reduce_kernel(
    nacc, CF, Mt, tm, ohs, perm, mqb, charges, counts, self_tiles, basis_t, out,
    R, C, V, W, hs, hr, ws, wr, z2s, z2r, z1s, z1r, y1s, y1r, scs, scr,
    out1, gtmp, gj, ss, rs,
):
    p = Place()
    x, k = p.x, p.k
    p.greet(False)
    C[0] = nacc[7 * k]
    p.met()
    s = Sender(ss, rs)
    wire = Wire(s, scs, scr)
    near_sib = [
        s.copy(nacc.at[u], R.at[i], p.sib) for i, u in enumerate((6 - 5 * k, 2 + 3 * k, 4 - k))
    ]
    two = {}
    ring = {}

    def first(i):
        two[i] = (
            wire.send(C[i, p.xo, pl.ds(0, 8)], hs.at[2 * i], hr.at[2 * i], p.east),
            wire.send(C[i, p.xo, pl.ds(8, 8)], hs.at[2 * i + 1], hr.at[2 * i + 1], p.west),
        )

    def second(i):
        C[i, p.xp, pl.ds(0, 8)] += wire.take(two[i][0])
        C[i, p.xm, pl.ds(8, 8)] += wire.take(two[i][1])
        ring[i] = (
            wire.send(C[i, p.xp], ws.at[2 * i], wr.at[2 * i], p.east),
            wire.send(C[i, p.xm], ws.at[2 * i + 1], wr.at[2 * i + 1], p.west),
        )

    def third(i):
        V[i] = C[i, x] + wire.take(ring[i][0]) + wire.take(ring[i][1])

    def source_moments(half):
        for h in (2 * half, 2 * half + 1):
            table = Mt[:, :, :, :, h * 256 : (h + 1) * 256].reshape(512, 256)
            gtmp[h * 256 : (h + 1) * 256, :] = lax.dot_general(
                table, ohs[...], TN, preferred_element_type=F32
            ).astype(BF16)

    def reorder():
        for h in range(4):
            block = jnp.concatenate(
                [gtmp[r * 64 + h * 16 : r * 64 + (h + 1) * 16, :] for r in range(16)], axis=0
            )
            gj[h * 256 : (h + 1) * 256, :] = jnp.dot(
                perm[...], block, preferred_element_type=F32
            ).astype(BF16)

    def to_targets(first, last):
        @pl.loop(first, last)
        def _(n):
            total = out1[...]
            for a in range(NJ):
                j = n * NJ + a
                ms = gj[pl.ds(pl.multiple_of(j * 16, 16), 16), :]
                zj = (ms[None] * mqb[...]).reshape(TQ * 16, 512)
                total = total + lax.dot_general(zj, tm[j], NT, preferred_element_type=F32)
            out1[...] = total

    first(0)
    fz2 = (
        wire.send(CF[p.zo, pl.ds(0, 2)], z2s.at[0], z2r.at[0], p.z_plus),
        wire.send(CF[p.zo, pl.ds(2, 2)], z2s.at[1], z2r.at[1], p.z_minus),
    )
    for i, (slot, u) in enumerate(((1, 1 + 5 * k), (3, 5 - 3 * k), (2, 3 + k))):
        near_sib[i].wait_recv()
        C[slot] = nacc[u] + R[i]
        first(slot)
    out1[...] = jnp.zeros_like(out1)
    lane = lax.broadcasted_iota(jnp.int32, (16, 128), 1)
    for b in range(16):
        part = charges[:, b * 128 : (b + 1) * 128]
        part = jnp.where(lane < counts[b], part.astype(F32), 0.0).astype(BF16)
        out[:, b * 128 : (b + 1) * 128] = lax.dot_general(
            part, self_tiles[b], NT, preferred_element_type=F32
        )
    second(0)
    z_up = CF[p.zp]
    z_down = CF[p.zm]
    fz = (
        wire.send(
            jnp.concatenate([z_up[:2] + wire.take(fz2[0]), z_up[2:]], axis=0),
            z1s.at[0],
            z1r.at[0],
            p.z_plus,
        ),
        wire.send(
            jnp.concatenate([z_down[:2], z_down[2:] + wire.take(fz2[1])], axis=0),
            z1s.at[1],
            z1r.at[1],
            p.z_minus,
        ),
    )
    second(1)
    source_moments(0)
    second(3)
    second(2)
    source_moments(1)
    third(0)
    relay = wire.send(V[0], ws.at[8], wr.at[8], p.two_away)
    reorder()
    third(1)
    near_last = [wire.send(V[1], ws.at[9], wr.at[9], p.near_relay)]
    W[...] = CF[p.z] + wire.take(fz[0]) + wire.take(fz[1])
    fy = [
        wire.send(W[pl.ds(y, 1)], y1s.at[i], y1r.at[i], peer)
        for i, (y, peer) in enumerate(
            ((p.yo, p.y_across), (p.yp, p.y_plus), (p.ym, p.y_minus))
        )
    ]
    third(3)
    near_last.append(wire.send(V[3], ws.at[10], wr.at[10], p.near_away))
    to_targets(0, 6)
    third(2)
    to_targets(6, 16)
    V[2] += wire.take(relay) + wire.take(near_last[0]) + wire.take(near_last[1])
    flat = (W[pl.ds(p.y, 1)] + wire.take(fy[0]) + wire.take(fy[1]) + wire.take(fy[2]))[0]
    rows = jnp.stack([flat[:, r * 64 : (r + 1) * 64] for r in range(16)], axis=0)
    rows = jnp.swapaxes(rows, 0, 1)
    for b in range(16):
        own1 = out1[b % TQ * 16 : b % TQ * 16 + 16, b // TQ * 64 : b // TQ * 64 + 64]
        fields = (rows[b] + own1).astype(BF16)
        far_part = jnp.dot(fields, basis_t[b], preferred_element_type=F32)
        cols = slice(b * 128, (b + 1) * 128)
        out[:, cols] = jnp.where(lane < counts[b], out[:, cols] + V[2, b] + far_part, 0.0)
    s.drain()


def vmem():
    return pl.BlockSpec(memory_space=pltpu.VMEM)


def body(
    charges, counts, self_tiles, basis, near_first, near_second, near_tiles, far_source, far_target, far_tiles
):
    basis_t = jnp.transpose(basis, (0, 2, 1))
    far_t = jnp.transpose(far_tiles, (1, 2, 0))
    smem = pl.BlockSpec(memory_space=pltpu.SMEM)
    hbm = pl.BlockSpec(memory_space=pltpu.HBM)
    dma = pltpu.SemaphoreType.DMA
    X, CF, Mt, tm, ohs, perm, mqb = pl.pallas_call(
        gather_kernel,
        name="gather",
        out_shape=(
            jax.ShapeDtypeStruct((8, 4, 16, 16, 128), BF16),
            jax.ShapeDtypeStruct((4, 4, 16, 1024), F32),
            jax.ShapeDtypeStruct((4, 4, 2, 16, 1024), BF16),
            jax.ShapeDtypeStruct((64, TG * 64, 512), BF16),
            jax.ShapeDtypeStruct((512, 512), BF16),
            jax.ShapeDtypeStruct((256, 256), BF16),
            jax.ShapeDtypeStruct((TQ, 16, 512), BF16),
        ),
        in_specs=[hbm] * 6,
        out_specs=(vmem(),) * 7,
        scratch_shapes=[
            pltpu.SMEM((16,), jnp.int32),
            pltpu.VMEM((16, 2048), BF16),
            pltpu.VMEM((16, 64, 128), BF16),
            pltpu.VMEM((2, 1, 512), jnp.int32),
            pltpu.VMEM((16, 16, 128), BF16),
            pltpu.VMEM((TQ * 16, TG * 64), BF16),
            pltpu.VMEM((64, 64, 512), BF16),
            pltpu.VMEM((TG, 16, 512), BF16),
            pltpu.VMEM((1024, 512), BF16),
            pltpu.VMEM((1024, 512), BF16),
            pltpu.VMEM((1024, 512), BF16),
            pltpu.VMEM((1024, 512), BF16),
            pltpu.VMEM((4, 4, 2, 16, 1024), F32),
            pltpu.VMEM((4, 4, 16, 1024), F32),
            dma((5,)),
            dma((4,)),
            dma((64,)),
            dma((64,)),
        ],
        compiler_params=pltpu.CompilerParams(
            collective_id=0, has_side_effects=True, vmem_limit_bytes=32 << 20
        ),
    )(*[
        pltpu.with_memory_space_constraint(a, pltpu.HBM)
        for a in (
            charges,
            counts,
            basis_t,
            far_t,
            far_source.reshape(1, 512),
            far_target.reshape(1, 512),
        )
    ])
    nacc = pl.pallas_call(
        local_kernel,
        name="local",
        out_shape=jax.ShapeDtypeStruct((8, 4, 16, 16, 128), F32),
        in_specs=[smem, smem, vmem(), vmem()],
        out_specs=vmem(),
        compiler_params=pltpu.CompilerParams(vmem_limit_bytes=24 << 20),
    )(near_first, near_second, near_tiles, X)
    chunk = (16, 16, 128)
    half = (8, 16, 128)
    i16 = jnp.int16
    return pl.pallas_call(
        reduce_kernel,
        name="reduce",
        out_shape=jax.ShapeDtypeStruct((16, 2048), F32),
        in_specs=[vmem()] * 8 + [smem, vmem(), vmem()],
        out_specs=vmem(),
        scratch_shapes=[
            pltpu.VMEM((3, 4) + chunk, F32),
            pltpu.VMEM((4, 4) + chunk, F32),
            pltpu.VMEM((4,) + chunk, F32),
            pltpu.VMEM((4, 16, 1024), F32),
            pltpu.VMEM((8,) + half, i16),
            pltpu.VMEM((8,) + half, i16),
            pltpu.VMEM((11,) + chunk, i16),
            pltpu.VMEM((11,) + chunk, i16),
            pltpu.VMEM((2, 2, 16, 1024), i16),
            pltpu.VMEM((2, 2, 16, 1024), i16),
            pltpu.VMEM((2, 4, 16, 1024), i16),
            pltpu.VMEM((2, 4, 16, 1024), i16),
            pltpu.VMEM((3, 1, 16, 1024), i16),
            pltpu.VMEM((3, 1, 16, 1024), i16),
            pltpu.VMEM((27, 8, 128), F32),
            pltpu.VMEM((27, 8, 128), F32),
            pltpu.VMEM((TQ * 16, TG * 64), F32),
            pltpu.VMEM((1024, 512), BF16),
            pltpu.VMEM((1024, 512), BF16),
            dma((57,)),
            dma((57,)),
        ],
        compiler_params=pltpu.CompilerParams(
            collective_id=1, has_side_effects=True, vmem_limit_bytes=28 << 20
        ),
    )(
        nacc, CF, Mt, tm, ohs, perm, mqb, charges, counts, self_tiles, basis_t
    )


def solution(mesh):
    in_specs = (
        P("rhs", "blk"),
        P("blk"),
        P("blk", None, None),
        P("blk", None, None),
        P("blk"),
        P("blk"),
        P(("blk", "rhs"), None, None),
        P("blk"),
        P("blk"),
        P("blk", None, None),
    )
    return jax.shard_map(
        body, mesh=mesh, in_specs=in_specs, out_specs=P("rhs", "blk"), check_vma=False
    )
```

```python
import functools

import jax
import jax.numpy as jnp
from jax import lax
from jax.experimental import pallas as pl
from jax.experimental.pallas import tpu as pltpu
from jax.sharding import PartitionSpec as P

MESH = pl.DeviceIdType.MESH
F32 = jnp.float32
BF16 = jnp.bfloat16
NT = (((1,), (1,)), ((), ()))
TN = (((0,), (0,)), ((), ()))


class Place:
    def __init__(self):
        self.o = lax.axis_index("blk")
        self.x = lax.axis_index("rhs")
        self.k = self.o % 2
        self.c = self.o // 2
        self.y = self.c % 4
        self.z = self.c // 4
        self.xp = (self.x + 1) % 4
        self.xm = (self.x + 3) % 4
        self.xo = (self.x + 2) % 4
        self.yp = (self.y + 1) % 4
        self.ym = (self.y + 3) % 4
        self.yo = (self.y + 2) % 4
        self.zp = (self.z + 1) % 4
        self.zm = (self.z + 3) % 4
        self.zo = (self.z + 2) % 4
        self.sib = self.dev(self.c, 1 - self.k)
        self.east = {"blk": self.o, "rhs": self.xp}
        self.west = {"blk": self.o, "rhs": self.xm}
        self.cp = (self.c + 1) % 16
        self.cm = (self.c + 15) % 16
        self.up = self.dev(self.cp, self.k)
        self.down = self.dev(self.cm, self.k)
        self.up_other = self.dev(self.cp, 1 - self.k)
        self.down_other = self.dev(self.cm, 1 - self.k)
        self.y_plus = self.dev(self.z * 4 + self.yp, self.k)
        self.y_minus = self.dev(self.z * 4 + self.ym, self.k)
        self.y_across = self.dev(self.z * 4 + self.yo, self.k)
        self.z_plus = self.dev(self.zp * 4 + self.y, self.k)
        self.z_minus = self.dev(self.zm * 4 + self.y, self.k)
        self.two_away = self.dev((self.c + 14 + 4 * self.k) % 16, 1 - self.k)
        self.near_relay = self.dev((self.c + 15 + 2 * self.k) % 16, self.k)
        self.near_away = self.dev((self.c + 1 + 14 * self.k) % 16, self.k)
        self.far_chip = self.dev((self.c + 15 + 2 * self.k) % 16, 1 - self.k)

    def dev(self, chip, core):
        return {"blk": chip * 2 + core, "rhs": self.x}

    def plane(self):
        return [((self.z + dz) % 4, (self.y + dy) % 4) for dz, dy in STEPS]

    def greet(self, whole_plane):
        self.barrier = pltpu.get_barrier_semaphore()
        self.peers = [
            self.sib,
            self.east,
            self.west,
            self.up,
            self.down,
            self.up_other,
            self.down_other,
            self.two_away,
        ]
        if whole_plane:
            self.peers += [self.dev(z * 4 + y, self.k) for z, y in self.plane()]
        else:
            self.peers += [self.y_plus, self.y_minus, self.y_across, self.z_plus, self.z_minus]
        for peer in self.peers:
            pl.semaphore_signal(self.barrier, inc=1, device_id=peer, device_id_type=MESH)

    def met(self):
        pl.semaphore_wait(self.barrier, len(self.peers))


class Sender:
    def __init__(self, send_sems, recv_sems):
        self.send_sems, self.recv_sems, self.n, self.out = send_sems, recv_sems, 0, []

    def copy(self, src, dst, peer):
        at = self.n
        self.n += 1
        made = pltpu.make_async_remote_copy(
            src_ref=src,
            dst_ref=dst,
            send_sem=self.send_sems.at[at],
            recv_sem=self.recv_sems.at[at],
            device_id=peer,
            device_id_type=MESH,
        )
        made.start()
        self.out.append(made)
        return made

    def drain(self):
        for made in self.out:
            made.wait_send()


TG = 2
TQ = 16 // TG
NJ = 8
UR = 2
NS = 8


STEPS = [(dz, dy) for dy in (1, 3, 0) for dz in (2, 1, 3, 0) if dz or dy]


def gather_kernel(
    charges, counts, basis_t, far, fs, ft, X, CF, Mt, tm, ohs, perm, mqb,
    nbuf, qbuf, bbuf, ibuf, own, mq, tin, mgb, yhi, ylo, zhi, zlo, S, RF,
    in_sem, tin_sem, ss, rs,
):
    p = Place()
    x, k = p.x, p.k
    p.greet(True)
    small = [
        pltpu.make_async_copy(charges, qbuf, in_sem.at[0]),
        pltpu.make_async_copy(basis_t, bbuf, in_sem.at[1]),
        pltpu.make_async_copy(counts, nbuf, in_sem.at[2]),
        pltpu.make_async_copy(fs, ibuf.at[0], in_sem.at[3]),
        pltpu.make_async_copy(ft, ibuf.at[1], in_sem.at[4]),
    ]
    loads = [
        pltpu.make_async_copy(far.at[pl.ds(i * 16, 16)], tin.at[pl.ds(i * 16, 16)], tin_sem.at[i])
        for i in range(4)
    ]
    for load in small + loads:
        load.start()
    for load in small[:3]:
        load.wait()
    lane = lax.broadcasted_iota(jnp.int32, (16, 128), 1)
    for b in range(16):
        block = qbuf[:, b * 128 : (b + 1) * 128]
        own[b] = jnp.where(lane < nbuf[b], block.astype(F32), 0.0).astype(BF16)
    X[3 + k, x] = own[...]
    p.met()
    s = Sender(ss, rs)
    sib = []
    farsib = []
    me = X.at[3 + k, x]

    def ring_start(u):
        src = X.at[u, x]
        return s.copy(src, X.at[u, x], p.east), s.copy(src, X.at[u, x], p.west)

    def arrived(pair):
        for made in pair:
            made.wait_recv()

    def ring_relay(u, pair):
        arrived(pair)
        made = (
            s.copy(X.at[u, p.xm, pl.ds(0, 8)], X.at[u, p.xm, pl.ds(0, 8)], p.east),
            s.copy(X.at[u, p.xp, pl.ds(8, 8)], X.at[u, p.xp, pl.ds(8, 8)], p.west),
        )
        if u is not edge:
            to_sib(u, p.xm)
            to_sib(u, p.xp)
        return made

    def column_on(y):
        farsib.append(s.copy(Mt.at[:, y, k], Mt.at[:, y, k], p.sib))

    def to_sib(u, at):
        sib.append(s.copy(X.at[u, at], X.at[u, at], p.sib))

    u0, u1, u2, u3 = 7 * k, 1 + k, 3 + k, 5 + k
    edge = u0
    to_up = s.copy(me, X.at[u1, x], p.up)
    to_down = s.copy(me, X.at[u3, x], p.down)
    ring2 = ring_start(u2)

    moments = []
    for b in range(16):
        m = lax.dot_general(own[b], bbuf[b], NT, preferred_element_type=F32).astype(BF16)
        moments.append(m.astype(F32))
    rows = jnp.swapaxes(jnp.stack(moments, axis=0), 0, 1)
    Mt[p.z, p.y, k] = jnp.concatenate([rows[r] for r in range(16)], axis=-1).astype(BF16)
    mine = Mt.at[p.z, p.y, k]
    plane = p.plane()
    far_all = [s.copy(mine, mine, p.dev(z * 4 + y, k)) for z, y in plane]
    to_sib(u2, x)

    for a in range(TQ):
        mq[a * 16 : (a + 1) * 16, :] = jnp.concatenate(
            [moments[g * TQ + a] for g in range(TG)], axis=-1
        ).astype(BF16)
    row = lax.broadcasted_iota(jnp.int32, (256, 256), 0)
    col = lax.broadcasted_iota(jnp.int32, (256, 256), 1)
    swap = ((row >> 4) == (col & 15)) & ((row & 15) == (col >> 4))
    perm[...] = jnp.where(swap, 1.0, 0.0).astype(BF16)
    small[3].wait()
    small[4].wait()
    tl = ibuf[1] - p.o * 16
    tg = tl // TQ
    tq = tl - tg * TQ
    ohs[...] = jnp.where(
        lax.broadcasted_iota(jnp.int32, (512, 512), 0) == ibuf[0], 1.0, 0.0
    ).astype(BF16)
    for g in range(TG):
        mgb[g] = jnp.broadcast_to(jnp.where(tg == g, 1.0, 0.0).astype(BF16), (16, 512))
    for g in range(TQ):
        mqb[g] = jnp.broadcast_to(jnp.where(tq == g, 1.0, 0.0).astype(BF16), (16, 512))

    def relayout(i):
        loads[i].wait()

        @pl.loop(0, 4, unroll=UR)
        def _(n):
            at = pl.ds(pl.multiple_of(n * 16, 16), 16)
            block = tin[i * 16 : (i + 1) * 16, at, :].reshape(256, 512)
            moved = jnp.dot(perm[...], block, preferred_element_type=F32).astype(BF16)
            moved = moved.reshape(16, 16, 512)
            for g in range(TG):
                tm[at, g * 64 + i * 16 : g * 64 + (i + 1) * 16, :] = moved * mgb[g][None]

    def to_sources(first, last):
        @pl.loop(first * 4 // NS, last * 4 // NS)
        def _(n):
            for a in range(NS):
                j = n * NS + a
                yj = jnp.dot(mq[...], tm[j], preferred_element_type=F32)
                y = jnp.where(tq == 0, yj[0:16], 0.0)
                for g in range(1, TQ):
                    y = jnp.where(tq == g, yj[g * 16 : (g + 1) * 16], y)
                hi = y.astype(BF16)
                at = pl.ds(pl.multiple_of(j * 16, 16), 16)
                yhi[at, :] = hi
                ylo[at, :] = (y - hi.astype(F32)).astype(BF16)

    relayout(0)
    arrived((to_up, to_down))
    two = s.copy(X.at[5 - 3 * k, x], X.at[7 - 7 * k, x], p.far_chip)
    ring1 = ring_start(u1)
    ring3 = ring_start(u3)
    to_sib(u1, x)
    to_sib(u3, x)
    relayout(1)
    relayout(2)
    relay2 = ring_relay(u2, ring2)
    relayout(3)
    to_sources(0, 2)
    two.wait_recv()
    ring0 = ring_start(u0)
    to_sources(2, 4)
    relay1 = ring_relay(u1, ring1)
    to_sources(4, 6)
    relay3 = ring_relay(u3, ring3)
    arrived(far_all[:8])
    column_on(p.ym)
    column_on(p.yp)
    east, west = Mt.at[:, p.ym, k, :, pl.ds(0, 512)], Mt.at[:, p.yp, k, :, pl.ds(512, 512)]
    far_y2 = s.copy(east, east, p.y_plus), s.copy(west, west, p.y_minus)
    to_sources(6, 10)
    to_sources(10, 14)
    arrived(relay2)
    to_sib(u2, p.xo)
    relay0 = ring_relay(u0, ring0)
    to_sources(14, 16)
    for h in range(4):
        for src, dst in ((yhi, zhi), (ylo, zlo)):
            moved = jnp.dot(
                perm[...], src[h * 256 : (h + 1) * 256, :], preferred_element_type=F32
            ).astype(BF16)
            for r in range(16):
                dst[r * 64 + h * 16 : r * 64 + (h + 1) * 16, :] = moved[r * 16 : (r + 1) * 16]
    arrived(relay1)
    to_sib(u1, p.xo)
    sums = []
    for h in range(4):
        at = slice(h * 256, (h + 1) * 256)
        part = lax.dot_general(
            ohs[...], zhi[at, :], NT, preferred_element_type=F32
        ) + lax.dot_general(ohs[...], zlo[at, :], NT, preferred_element_type=F32)
        S[:, :, :, :, at] = part.reshape(4, 4, 2, 16, 256)
        if h == 1:
            arrived(far_all[8:])
            column_on(p.y)
            arrived(far_y2)
            column_on(p.yo)
        lanes = pl.ds(h * 256, 256)
        sums.append(s.copy(S.at[:, :, 1 - k, :, lanes], RF.at[:, :, :, lanes], p.sib))
    arrived(relay3)
    to_sib(u3, p.xo)
    arrived(farsib)

    for h in range(4):
        at = slice(h * 256, (h + 1) * 256)
        sums[h].wait_recv()
        CF[:, :, :, at] = S[:, :, k, :, at] + RF[:, :, :, at]
    arrived(relay0)
    arrived(sib)
    s.drain()


def local_kernel(nf, ns, tiles, X, nacc):
    o = lax.axis_index("blk")
    k = o % 2
    base = lax.axis_index("rhs") * 128
    nacc[...] = jnp.zeros_like(nacc)

    none = jnp.zeros((64, 128), BF16)
    ua = 3 + k

    def ends(n):
        d = (ns[base + n] - o * 16 + 560) & 511
        return nf[base + n] - o * 16, (d >> 4) + k, d & 15

    @pl.loop(0, 64, unroll=32)
    def _(m):
        a0, u0, b0 = ends(2 * m)
        a1, u1, b1 = ends(2 * m + 1)
        both = jnp.concatenate([tiles[2 * m], tiles[2 * m + 1]], axis=1)
        xb0 = X[u0, :, b0].reshape(64, 128)
        xb1 = X[u1, :, b1].reshape(64, 128)
        xa0 = X[ua, :, a0].reshape(64, 128)
        xa1 = X[ua, :, a1].reshape(64, 128)
        apart = jnp.concatenate(
            [jnp.concatenate([xb0, none], axis=1), jnp.concatenate([none, xb1], axis=1)], axis=0
        )
        to_first = lax.dot_general(apart, both, NT, preferred_element_type=F32)
        to_second = jnp.dot(
            jnp.concatenate([xa0, xa1], axis=0), both, preferred_element_type=F32
        )
        nacc[ua, :, a0] += to_first[:64].reshape(4, 16, 128)
        nacc[u0, :, b0] += to_second[:64, :128].reshape(4, 16, 128)
        nacc[ua, :, a1] += to_first[64:].reshape(4, 16, 128)
        nacc[u1, :, b1] += to_second[64:, 128:].reshape(4, 16, 128)


class Wire:
    def __init__(self, sender, scs, scr):
        self.sender, self.scs, self.scr, self.n = sender, scs, scr, 0

    def send(self, value, src, dst, peer):
        at = self.n
        self.n += 1
        lanes = value.shape[-1] // 128
        most = jnp.full((8, 128), 1e-30, F32)
        for w in range(lanes):
            top = jnp.max(jnp.abs(value[:, :, w * 128 : (w + 1) * 128]), axis=0)
            most = jnp.maximum(most, jnp.maximum(top[:8], top[8:]))
        self.scs[at] = most * (1.0 / 32000.0)
        src[...] = jnp.round(value * self.tile(32000.0 / most, lanes)).astype(jnp.int32).astype(jnp.int16)
        made = (
            self.sender.copy(self.scs.at[at], self.scr.at[at], peer),
            self.sender.copy(src, dst, peer),
        )
        return made, dst, at

    def tile(self, scale, lanes):
        both = jnp.concatenate([scale, scale], axis=0)
        return jnp.concatenate([both] * lanes, axis=1)[None]

    def take(self, sent):
        made, dst, at = sent
        made[0].wait_recv()
        made[1].wait_recv()
        value = dst[...].astype(jnp.int32).astype(F32)
        return value * self.tile(self.scr[at], value.shape[-1] // 128)


def reduce_kernel(
    nacc, CF, Mt, tm, ohs, perm, mqb, charges, counts, self_tiles, basis_t, out,
    R, C, V, W, hs, hr, ws, wr, z2s, z2r, z1s, z1r, y1s, y1r, scs, scr,
    out1, gtmp, gj, ss, rs,
):
    p = Place()
    x, k = p.x, p.k
    p.greet(False)
    C[0] = nacc[7 * k]
    p.met()
    s = Sender(ss, rs)
    wire = Wire(s, scs, scr)
    near_sib = [
        s.copy(nacc.at[u], R.at[i], p.sib) for i, u in enumerate((6 - 5 * k, 2 + 3 * k, 4 - k))
    ]
    two = {}
    ring = {}

    def first(i):
        two[i] = (
            wire.send(C[i, p.xo, pl.ds(0, 8)], hs.at[2 * i], hr.at[2 * i], p.east),
            wire.send(C[i, p.xo, pl.ds(8, 8)], hs.at[2 * i + 1], hr.at[2 * i + 1], p.west),
        )

    def second(i):
        C[i, p.xp, pl.ds(0, 8)] += wire.take(two[i][0])
        C[i, p.xm, pl.ds(8, 8)] += wire.take(two[i][1])
        ring[i] = (
            wire.send(C[i, p.xp], ws.at[2 * i], wr.at[2 * i], p.east),
            wire.send(C[i, p.xm], ws.at[2 * i + 1], wr.at[2 * i + 1], p.west),
        )

    def third(i):
        V[i] = C[i, x] + wire.take(ring[i][0]) + wire.take(ring[i][1])

    def source_moments(half):
        for h in (2 * half, 2 * half + 1):
            table = Mt[:, :, :, :, h * 256 : (h + 1) * 256].reshape(512, 256)
            gtmp[h * 256 : (h + 1) * 256, :] = lax.dot_general(
                table, ohs[...], TN, preferred_element_type=F32
            ).astype(BF16)

    def reorder():
        for h in range(4):
            block = jnp.concatenate(
                [gtmp[r * 64 + h * 16 : r * 64 + (h + 1) * 16, :] for r in range(16)], axis=0
            )
            gj[h * 256 : (h + 1) * 256, :] = jnp.dot(
                perm[...], block, preferred_element_type=F32
            ).astype(BF16)

    def to_targets(first, last):
        @pl.loop(first, last)
        def _(n):
            total = out1[...]
            for a in range(NJ):
                j = n * NJ + a
                ms = gj[pl.ds(pl.multiple_of(j * 16, 16), 16), :]
                zj = (ms[None] * mqb[...]).reshape(TQ * 16, 512)
                total = total + lax.dot_general(zj, tm[j], NT, preferred_element_type=F32)
            out1[...] = total

    first(0)
    fz2 = (
        wire.send(CF[p.zo, pl.ds(0, 2)], z2s.at[0], z2r.at[0], p.z_plus),
        wire.send(CF[p.zo, pl.ds(2, 2)], z2s.at[1], z2r.at[1], p.z_minus),
    )
    for i, (slot, u) in enumerate(((1, 1 + 5 * k), (3, 5 - 3 * k), (2, 3 + k))):
        near_sib[i].wait_recv()
        C[slot] = nacc[u] + R[i]
        first(slot)
    out1[...] = jnp.zeros_like(out1)
    lane = lax.broadcasted_iota(jnp.int32, (16, 128), 1)
    for b in range(16):
        part = charges[:, b * 128 : (b + 1) * 128]
        part = jnp.where(lane < counts[b], part.astype(F32), 0.0).astype(BF16)
        out[:, b * 128 : (b + 1) * 128] = lax.dot_general(
            part, self_tiles[b], NT, preferred_element_type=F32
        )
    second(0)
    z_up = CF[p.zp]
    z_down = CF[p.zm]
    fz = (
        wire.send(
            jnp.concatenate([z_up[:2] + wire.take(fz2[0]), z_up[2:]], axis=0),
            z1s.at[0],
            z1r.at[0],
            p.z_plus,
        ),
        wire.send(
            jnp.concatenate([z_down[:2], z_down[2:] + wire.take(fz2[1])], axis=0),
            z1s.at[1],
            z1r.at[1],
            p.z_minus,
        ),
    )
    second(1)
    source_moments(0)
    second(3)
    second(2)
    source_moments(1)
    third(0)
    relay = wire.send(V[0], ws.at[8], wr.at[8], p.two_away)
    reorder()
    third(1)
    near_last = [wire.send(V[1], ws.at[9], wr.at[9], p.near_relay)]
    W[...] = CF[p.z] + wire.take(fz[0]) + wire.take(fz[1])
    fy = [
        wire.send(W[pl.ds(y, 1)], y1s.at[i], y1r.at[i], peer)
        for i, (y, peer) in enumerate(
            ((p.yo, p.y_across), (p.yp, p.y_plus), (p.ym, p.y_minus))
        )
    ]
    third(3)
    near_last.append(wire.send(V[3], ws.at[10], wr.at[10], p.near_away))
    to_targets(0, 3)
    third(2)
    to_targets(3, 8)
    V[2] += wire.take(relay) + wire.take(near_last[0]) + wire.take(near_last[1])
    flat = (W[pl.ds(p.y, 1)] + wire.take(fy[0]) + wire.take(fy[1]) + wire.take(fy[2]))[0]
    rows = jnp.stack([flat[:, r * 64 : (r + 1) * 64] for r in range(16)], axis=0)
    rows = jnp.swapaxes(rows, 0, 1)
    for b in range(16):
        own1 = out1[b % TQ * 16 : b % TQ * 16 + 16, b // TQ * 64 : b // TQ * 64 + 64]
        fields = (rows[b] + own1).astype(BF16)
        far_part = jnp.dot(fields, basis_t[b], preferred_element_type=F32)
        cols = slice(b * 128, (b + 1) * 128)
        out[:, cols] = jnp.where(lane < counts[b], out[:, cols] + V[2, b] + far_part, 0.0)
    s.drain()


def vmem():
    return pl.BlockSpec(memory_space=pltpu.VMEM)


def body(
    charges, counts, self_tiles, basis, near_first, near_second, near_tiles, far_source, far_target, far_tiles
):
    basis_t = jnp.transpose(basis, (0, 2, 1))
    far_t = jnp.transpose(far_tiles, (1, 2, 0))
    smem = pl.BlockSpec(memory_space=pltpu.SMEM)
    hbm = pl.BlockSpec(memory_space=pltpu.HBM)
    dma = pltpu.SemaphoreType.DMA
    X, CF, Mt, tm, ohs, perm, mqb = pl.pallas_call(
        gather_kernel,
        name="gather",
        out_shape=(
            jax.ShapeDtypeStruct((8, 4, 16, 16, 128), BF16),
            jax.ShapeDtypeStruct((4, 4, 16, 1024), F32),
            jax.ShapeDtypeStruct((4, 4, 2, 16, 1024), BF16),
            jax.ShapeDtypeStruct((64, TG * 64, 512), BF16),
            jax.ShapeDtypeStruct((512, 512), BF16),
            jax.ShapeDtypeStruct((256, 256), BF16),
            jax.ShapeDtypeStruct((TQ, 16, 512), BF16),
        ),
        in_specs=[hbm] * 6,
        out_specs=(vmem(),) * 7,
        scratch_shapes=[
            pltpu.SMEM((16,), jnp.int32),
            pltpu.VMEM((16, 2048), BF16),
            pltpu.VMEM((16, 64, 128), BF16),
            pltpu.VMEM((2, 1, 512), jnp.int32),
            pltpu.VMEM((16, 16, 128), BF16),
            pltpu.VMEM((TQ * 16, TG * 64), BF16),
            pltpu.VMEM((64, 64, 512), BF16),
            pltpu.VMEM((TG, 16, 512), BF16),
            pltpu.VMEM((1024, 512), BF16),
            pltpu.VMEM((1024, 512), BF16),
            pltpu.VMEM((1024, 512), BF16),
            pltpu.VMEM((1024, 512), BF16),
            pltpu.VMEM((4, 4, 2, 16, 1024), F32),
            pltpu.VMEM((4, 4, 16, 1024), F32),
            dma((5,)),
            dma((4,)),
            dma((64,)),
            dma((64,)),
        ],
        compiler_params=pltpu.CompilerParams(
            collective_id=0, has_side_effects=True, vmem_limit_bytes=32 << 20
        ),
    )(*[
        pltpu.with_memory_space_constraint(a, pltpu.HBM)
        for a in (
            charges,
            counts,
            basis_t,
            far_t,
            far_source.reshape(1, 512),
            far_target.reshape(1, 512),
        )
    ])
    nacc = pl.pallas_call(
        local_kernel,
        name="local",
        out_shape=jax.ShapeDtypeStruct((8, 4, 16, 16, 128), F32),
        in_specs=[smem, smem, vmem(), vmem()],
        out_specs=vmem(),
        compiler_params=pltpu.CompilerParams(vmem_limit_bytes=24 << 20),
    )(near_first, near_second, near_tiles, X)
    chunk = (16, 16, 128)
    half = (8, 16, 128)
    i16 = jnp.int16
    return pl.pallas_call(
        reduce_kernel,
        name="reduce",
        out_shape=jax.ShapeDtypeStruct((16, 2048), F32),
        in_specs=[vmem()] * 8 + [smem, vmem(), vmem()],
        out_specs=vmem(),
        scratch_shapes=[
            pltpu.VMEM((3, 4) + chunk, F32),
            pltpu.VMEM((4, 4) + chunk, F32),
            pltpu.VMEM((4,) + chunk, F32),
            pltpu.VMEM((4, 16, 1024), F32),
            pltpu.VMEM((8,) + half, i16),
            pltpu.VMEM((8,) + half, i16),
            pltpu.VMEM((11,) + chunk, i16),
            pltpu.VMEM((11,) + chunk, i16),
            pltpu.VMEM((2, 2, 16, 1024), i16),
            pltpu.VMEM((2, 2, 16, 1024), i16),
            pltpu.VMEM((2, 4, 16, 1024), i16),
            pltpu.VMEM((2, 4, 16, 1024), i16),
            pltpu.VMEM((3, 1, 16, 1024), i16),
            pltpu.VMEM((3, 1, 16, 1024), i16),
            pltpu.VMEM((27, 8, 128), F32),
            pltpu.VMEM((27, 8, 128), F32),
            pltpu.VMEM((TQ * 16, TG * 64), F32),
            pltpu.VMEM((1024, 512), BF16),
            pltpu.VMEM((1024, 512), BF16),
            dma((57,)),
            dma((57,)),
        ],
        compiler_params=pltpu.CompilerParams(
            collective_id=1, has_side_effects=True, vmem_limit_bytes=28 << 20
        ),
    )(
        nacc, CF, Mt, tm, ohs, perm, mqb, charges, counts, self_tiles, basis_t
    )


def solution(mesh):
    in_specs = (
        P("rhs", "blk"),
        P("blk"),
        P("blk", None, None),
        P("blk", None, None),
        P("blk"),
        P("blk"),
        P(("blk", "rhs"), None, None),
        P("blk"),
        P("blk"),
        P("blk", None, None),
    )
    return jax.shard_map(
        body, mesh=mesh, in_specs=in_specs, out_specs=P("rhs", "blk"), check_vma=False
    )
```
